32 devices in a mesh: ctx: 8 (over y, x, core), fsdp: 4 (over z).
Axes of the slice: x: 2, y: 2, z: 4, core: 2. Of those that a mesh axis runs over, the one named last changes fastest.
Arguments:
- hidden: bfloat16 [3, 8, 2, 256, 1024], P(None, 'fsdp', None, 'ctx'), may hold values from -6 to 6
- encoder_out: bfloat16 [8, 512, 1024], P('fsdp', 'ctx'), may hold values from -6 to 6
- out_grad: bfloat16 [3, 8, 2, 256, 1024], P(None, 'fsdp', None, 'ctx'), may hold values from -6 to 6
- slot_len: int32 [8], P('fsdp'), may hold values from 128 to 512, as said below
- enc_len: int32 [8], P('fsdp'), may hold values from 128 to 512, as said below
- rel_bucket: int32 [512], replicated, may hold values from 0 to 31, as said below
- query_weight: bfloat16 [1024, 1024], P('fsdp'), may hold values from -0.1875 to 0.1875
- key_weight: bfloat16 [1024, 1024], P('fsdp'), may hold values from -0.1875 to 0.1875
- value_weight: bfloat16 [1024, 1024], P('fsdp'), may hold values from -0.1875 to 0.1875
- relative_weight: bfloat16 [1024, 512], P('fsdp'), may hold values from -0.1875 to 0.1875
- output_weight: bfloat16 [1024, 1024], P('fsdp'), may hold values from -1 to 1
- self_norm_gain: bfloat16 [1024], P('fsdp'), may hold values from 0.5 to 1.5
- self_norm_shift: bfloat16 [1024], P('fsdp'), may hold values from -3 to 3
- cross_query_weight: bfloat16 [1024, 1024], P('fsdp'), may hold values from -0.1875 to 0.1875
- cross_key_weight: bfloat16 [1024, 1024], P('fsdp'), may hold values from -0.1875 to 0.1875
- cross_value_weight: bfloat16 [1024, 1024], P('fsdp'), may hold values from -0.1875 to 0.1875
- cross_output_weight: bfloat16 [1024, 1024], P('fsdp'), may hold values from -1 to 1
- cross_norm_gain: bfloat16 [1024], P('fsdp'), may hold values from 0.5 to 1.5
- cross_norm_shift: bfloat16 [1024], P('fsdp'), may hold values from -3 to 3
- up_weight: bfloat16 [1024, 4096], P('fsdp'), may hold values from -0.1875 to 0.1875
- down_weight: bfloat16 [4096, 1024], P('fsdp'), may hold values from -0.09375 to 0.09375
- feed_norm_gain: bfloat16 [1024], P('fsdp'), may hold values from 0.5 to 1.5
- feed_norm_shift: bfloat16 [1024], P('fsdp'), may hold values from -3 to 3
Outputs:
- layer_out: bfloat16 [3, 8, 2, 256, 1024], P(None, 'fsdp', None, 'ctx')
- hidden_grad: float32 [3, 8, 2, 256, 1024], P(None, 'fsdp', None, 'ctx')
- encoder_grad: float32 [8, 512, 1024], P('fsdp', 'ctx')
- grad_query_weight: float32 [1024, 1024], P('fsdp')
- grad_key_weight: float32 [1024, 1024], P('fsdp')
- grad_value_weight: float32 [1024, 1024], P('fsdp')
- grad_relative_weight: float32 [1024, 512], P('fsdp')
- grad_output_weight: float32 [1024, 1024], P('fsdp')
- grad_self_norm_gain: float32 [1024], P('fsdp')
- grad_self_norm_shift: float32 [1024], P('fsdp')
- grad_cross_query_weight: float32 [1024, 1024], P('fsdp')
- grad_cross_key_weight: float32 [1024, 1024], P('fsdp')
- grad_cross_value_weight: float32 [1024, 1024], P('fsdp')
- grad_cross_output_weight: float32 [1024, 1024], P('fsdp')
- grad_cross_norm_gain: float32 [1024], P('fsdp')
- grad_cross_norm_shift: float32 [1024], P('fsdp')
- grad_up_weight: float32 [1024, 4096], P('fsdp')
- grad_down_weight: float32 [4096, 1024], P('fsdp')
- grad_feed_norm_gain: float32 [1024], P('fsdp')
- grad_feed_norm_shift: float32 [1024], P('fsdp')
The draws below stay inside these ranges and needn't reach their ends.
Inputs may be any that keep to these rules, and one draw needn't show every extreme that they name: `slot_len`: one slot in every draw is 512 long. `enc_len`: one slot in every draw has all 512 encoder rows. `rel_bucket`: entry d is the bucket of distance d: 0 at d = 0, never falling, rising by at most one from a distance to the next, and reaching 31 before d = 256.
All inputs are finite; a program needn't handle non-finite values.
Results may differ from the reference program's by a relative error of at most 0.03.
Values may be sent and summed in bfloat16 or wider, within the bound.
No kernel may reach another device: no remote copies, remote signals or barrier semaphores. Data moves between devices by JAX's collectives and lax.ppermute only.
A program may use at most 256 MiB of HBM per device.

```python
import jax
import jax.numpy as jnp
from jax import lax

D = 1024
HEADS = 16
HEAD_DIM = 64
FF = 4096
BUCKETS = 32
LANES = 3
ENC = 512
SLOT_LEN = 512
HALF = 256
SLOTS = 8


def draw_slot_len(key, part):
    lengths = jax.random.randint(key, (SLOTS,), SLOT_LEN // 4, SLOT_LEN + 1, dtype=jnp.int32)
    longest = jax.random.randint(jax.random.fold_in(key, 7), (), 0, SLOTS, dtype=jnp.int32)
    return jnp.where(jnp.arange(SLOTS, dtype=jnp.int32) == longest, SLOT_LEN, lengths).astype(jnp.int32)


def draw_enc_len(key, part):
    lengths = jax.random.randint(key, (SLOTS,), ENC // 4, ENC + 1, dtype=jnp.int32)
    longest = jax.random.randint(jax.random.fold_in(key, 11), (), 0, SLOTS, dtype=jnp.int32)
    return jnp.where(jnp.arange(SLOTS, dtype=jnp.int32) == longest, ENC, lengths).astype(jnp.int32)


def draw_rel_bucket(key, part):
    widest = max(2, SLOT_LEN // (2 * BUCKETS))
    spacing = jax.random.randint(key, (BUCKETS - 1,), 1, widest + 1, dtype=jnp.int32)
    bounds = jnp.cumsum(spacing).astype(jnp.int32)
    distance = jnp.arange(SLOT_LEN, dtype=jnp.int32)
    return jnp.sum((distance[:, None] >= bounds[None, :]).astype(jnp.int32), axis=1).astype(jnp.int32)


def steps_of(key, extent, cuts, low, largest):
    loudness = 1.0
    for dim, shards_of in cuts:
        heights = jax.random.uniform(jax.random.fold_in(jax.random.fold_in(key, 6), dim), (shards_of,), jnp.float32, low / len(cuts), largest / len(cuts))
        loudness = loudness * jnp.repeat(jnp.exp(heights), extent[dim] // shards_of).reshape((-1,) + (1,) * (len(extent) - 1 - dim))
    return loudness


def gaussian(key, dims, spread, reach, shards=(), kind=jnp.bfloat16):
    values = jax.random.normal(key, dims, jnp.float32) * spread
    if len(shards) > 0:
        values = steps_of(key, dims, shards, -0.22, 0.18) * values
    return jnp.clip(values, min=-reach, max=reach).astype(kind)


def setup_inputs(seed: int = 0) -> dict:
    streams_of = jax.random.split(jax.random.key(seed), 24)
    return {
        "hidden": gaussian(streams_of[0], (LANES, SLOTS, 2, HALF, D), 1.0, 6.0, ((1, 4), (3, 8))),
        "encoder_out": gaussian(streams_of[1], (SLOTS, ENC, D), 1.0, 6.0, ((0, 4), (1, 8))),
        "out_grad": gaussian(streams_of[2], (LANES, SLOTS, 2, HALF, D), 1.0, 6.0, ((1, 4), (3, 8))),
        "slot_len": draw_slot_len(jax.random.fold_in(streams_of[23], 71), 0),
        "enc_len": draw_enc_len(jax.random.fold_in(streams_of[23], 71), 0),
        "rel_bucket": draw_rel_bucket(jax.random.fold_in(streams_of[23], 71), 0),
        "query_weight": gaussian(streams_of[6], (D, D), D ** -0.5, 0.1875, ((0, 4),)),
        "key_weight": gaussian(streams_of[7], (D, D), D ** -0.5, 0.1875, ((0, 4),)),
        "value_weight": gaussian(streams_of[8], (D, D), D ** -0.5, 0.1875, ((0, 4),)),
        "relative_weight": gaussian(streams_of[9], (D, HEADS * BUCKETS), D ** -0.5, 0.1875, ((0, 4),)),
        "output_weight": gaussian(streams_of[10], (D, D), 32 ** -0.5, 1.0, ((0, 4),)),
        "self_norm_gain": jnp.clip(1.0 + 0.1 * jax.random.normal(streams_of[11], (D,), jnp.float32), 0.5, 1.5).astype(jnp.bfloat16),
        "self_norm_shift": gaussian(streams_of[12], (D,), 0.5, 3.0, ((0, 4),)),
        "cross_query_weight": gaussian(streams_of[13], (D, D), D ** -0.5, 0.1875, ((0, 4),)),
        "cross_key_weight": gaussian(streams_of[14], (D, D), D ** -0.5, 0.1875, ((0, 4),)),
        "cross_value_weight": gaussian(streams_of[15], (D, D), D ** -0.5, 0.1875, ((0, 4),)),
        "cross_output_weight": gaussian(streams_of[16], (D, D), 32 ** -0.5, 1.0, ((0, 4),)),
        "cross_norm_gain": jnp.clip(1.0 + 0.1 * jax.random.normal(streams_of[17], (D,), jnp.float32), 0.5, 1.5).astype(jnp.bfloat16),
        "cross_norm_shift": gaussian(streams_of[18], (D,), 0.5, 3.0, ((0, 4),)),
        "up_weight": gaussian(streams_of[19], (D, FF), D ** -0.5, 0.1875, ((0, 4),)),
        "down_weight": gaussian(streams_of[20], (FF, D), FF ** -0.5, 0.09375, ((0, 4),)),
        "feed_norm_gain": jnp.clip(1.0 + 0.1 * jax.random.normal(streams_of[21], (D,), jnp.float32), 0.5, 1.5).astype(jnp.bfloat16),
        "feed_norm_shift": gaussian(streams_of[22], (D,), 0.5, 3.0, ((0, 4),)),
    }


@jax.custom_vjp
def low(v):
    return lax.optimization_barrier(v.astype(jnp.bfloat16)).astype(jnp.float32)

@jax.custom_vjp
def low_back(v):
    return v

def low_keep(v):
    return (low(v), None)

def low_pass(kept, grad):
    return (grad,)

def back_keep(v):
    return (v, None)

def back_low(kept, grad):
    return (low(grad),)
low.defvjp(low_keep, low_pass)
low_back.defvjp(back_keep, back_low)
highest = lax.Precision.HIGHEST
eps_norm = 1e-05
neg_fill = -1e+30

def narrowed(values):
    return low_back(low(values))

def dense(left_side, right_side):
    return jnp.dot(left_side, right_side, precision=highest, preferred_element_type=jnp.float32)

def layer_norm(values, norm_gain, norm_shift):
    row_mean = lax.optimization_barrier(jnp.mean(values, axis=-1, keepdims=True))
    centered = values - row_mean
    variance = lax.optimization_barrier(jnp.mean(centered * centered, axis=-1, keepdims=True))
    return centered * lax.rsqrt(variance + eps_norm) * norm_gain + norm_shift

def soft_mix(scores, own_score):
    row_max = jnp.maximum(lax.optimization_barrier(jnp.max(scores, axis=-1)), own_score)
    exp_terms = jnp.exp(scores - row_max[..., None])
    own_exp = jnp.exp(own_score - row_max)
    row_sum = lax.optimization_barrier(jnp.sum(exp_terms, axis=-1)) + own_exp
    return (low(exp_terms / row_sum[..., None]), low(own_exp / row_sum))

def slot_forward(x_slot, enc_slot, weight_set, length, enc_length, table, positions):
    query_weight, key_weight, value_weight, relative_weight, output_weight, gain_one, shift_one, cquery_weight, ckey_weight, cvalue_weight, coutput_weight, gain_two, shift_two, up_weight, down_weight, gain_three, shift_three = weight_set
    score_scale = HEAD_DIM ** (-0.5)
    query_all = narrowed(dense(x_slot, query_weight)).reshape(LANES, SLOT_LEN, HEADS, HEAD_DIM)
    key_all = narrowed(dense(x_slot, key_weight)).reshape(LANES, SLOT_LEN, HEADS, HEAD_DIM)
    value_all = narrowed(dense(x_slot, value_weight)).reshape(LANES, SLOT_LEN, HEADS, HEAD_DIM)
    embed_all = narrowed(dense(x_slot, relative_weight)).reshape(LANES, SLOT_LEN, HEADS, BUCKETS)
    key_valid = positions < length
    block = min(512, SLOT_LEN)
    block_count = SLOT_LEN // block
    attended_list = []
    for lane in range(LANES):

        def self_block(block_index, lane=lane):
            start = block_index * block
            query_rows = lax.dynamic_slice_in_dim(query_all[lane], start, block, 0)
            embed_rows = lax.dynamic_slice_in_dim(embed_all[lane], start, block, 0)
            key_own = lax.dynamic_slice_in_dim(key_all[lane], start, block, 0)
            value_own = lax.dynamic_slice_in_dim(value_all[lane], start, block, 0)
            pos_rows = lax.dynamic_slice_in_dim(positions, start, block, 0)
            distance = pos_rows[:, None] - positions[None, :]
            bucket = table[jnp.clip(distance, 0, SLOT_LEN - 1)]
            rel_bias = jnp.take_along_axis(embed_rows, jnp.broadcast_to(bucket[:, None, :], (block, HEADS, SLOT_LEN)), axis=2)
            scores = low_back(score_scale * jnp.einsum('the,jhe->thj', query_rows, key_all[0], precision=highest) + rel_bias)
            if lane == 0:
                allowed = (distance >= 0) & key_valid[None, :]
                own_score = jnp.full((block, HEADS), neg_fill, jnp.float32)
            else:
                allowed = (distance > 0) & key_valid[None, :]
                own_score = low_back(score_scale * lax.optimization_barrier(jnp.sum(query_rows * key_own, axis=-1)) + embed_rows[:, :, 0])
            scores = jnp.where(allowed[:, None, :], scores, neg_fill)
            probs, own_prob = soft_mix(scores, own_score)
            mixed = jnp.einsum('thj,jhe->the', probs, value_all[0], precision=highest)
            return mixed + own_prob[..., None] * value_own
        mapped = lax.map(jax.checkpoint(self_block), jnp.arange(block_count, dtype=jnp.int32))
        attended_list.append(mapped.reshape(SLOT_LEN, D))
    attended = narrowed(jnp.stack(attended_list))
    resid_one = x_slot + low_back(dense(attended, output_weight))
    normed_one = layer_norm(resid_one, gain_one, shift_one)
    cross_query = narrowed(dense(low(normed_one), cquery_weight)).reshape(LANES * SLOT_LEN, HEADS, HEAD_DIM)
    enc_key = narrowed(dense(enc_slot, ckey_weight)).reshape(ENC, HEADS, HEAD_DIM)
    enc_value = narrowed(dense(enc_slot, cvalue_weight)).reshape(ENC, HEADS, HEAD_DIM)
    enc_valid = jnp.arange(ENC, dtype=jnp.int32) < enc_length

    def cross_block(block_index):
        start = block_index * block
        query_rows = lax.dynamic_slice_in_dim(cross_query, start, block, 0)
        scores = low_back(score_scale * jnp.einsum('the,jhe->thj', query_rows, enc_key, precision=highest))
        scores = jnp.where(enc_valid[None, None, :], scores, neg_fill)
        row_max = lax.optimization_barrier(jnp.max(scores, axis=-1, keepdims=True))
        exp_terms = jnp.exp(scores - row_max)
        probs = low(exp_terms / lax.optimization_barrier(jnp.sum(exp_terms, axis=-1, keepdims=True)))
        return jnp.einsum('thj,jhe->the', probs, enc_value, precision=highest)
    cross_mapped = lax.map(jax.checkpoint(cross_block), jnp.arange(LANES * block_count, dtype=jnp.int32))
    cross_attended = narrowed(cross_mapped.reshape(LANES, SLOT_LEN, D))
    resid_two = normed_one + low_back(dense(cross_attended, coutput_weight))
    normed_two = layer_norm(resid_two, gain_two, shift_two)
    pre_act = low_back(dense(low(normed_two), up_weight))
    act_low = low(jax.nn.gelu(pre_act, approximate=False))
    resid_three = normed_two + low_back(dense(act_low, down_weight))
    return layer_norm(resid_three, gain_three, shift_three)

def reference(hidden, encoder_out, out_grad, slot_len, enc_len, rel_bucket, query_weight, key_weight, value_weight, relative_weight, output_weight, self_norm_gain, self_norm_shift, cross_query_weight, cross_key_weight, cross_value_weight, cross_output_weight, cross_norm_gain, cross_norm_shift, up_weight, down_weight, feed_norm_gain, feed_norm_shift):
    weights = tuple((item.astype(jnp.float32) for item in (query_weight, key_weight, value_weight, relative_weight, output_weight, self_norm_gain, self_norm_shift, cross_query_weight, cross_key_weight, cross_value_weight, cross_output_weight, cross_norm_gain, cross_norm_shift, up_weight, down_weight, feed_norm_gain, feed_norm_shift)))
    half_index = jnp.arange(HALF, dtype=jnp.int32)
    positions = jnp.concatenate([half_index, SLOT_LEN - 1 - half_index]).astype(jnp.int32)
    slot_hidden = jnp.moveaxis(hidden, 1, 0)
    slot_grad = jnp.moveaxis(out_grad, 1, 0)

    def one_slot(carry, inputs):
        hid_slot, enc_slot, grad_slot, length, enc_length = inputs
        x_slot = hid_slot.astype(jnp.float32).reshape(LANES, SLOT_LEN, D)
        enc_f32 = enc_slot.astype(jnp.float32)
        row_valid = (positions < length).astype(jnp.float32)
        cotangent = grad_slot.astype(jnp.float32).reshape(LANES, SLOT_LEN, D) * row_valid[None, :, None]

        def forward(x_in, enc_in, weight_set):
            return slot_forward(x_in, enc_in, weight_set, length, enc_length, rel_bucket, positions)
        result, pullback = jax.vjp(forward, x_slot, enc_f32, weights)
        back_x, back_enc, back_weights = pullback(cotangent)
        carry = tuple((left_item + right_item for left_item, right_item in zip(carry, back_weights)))
        return (carry, (result.astype(jnp.bfloat16).reshape(LANES, 2, HALF, D), back_x.reshape(LANES, 2, HALF, D), back_enc))
    start_carry = tuple((jnp.zeros_like(item) for item in weights))
    totals, stacked = lax.scan(one_slot, start_carry, (slot_hidden, encoder_out, slot_grad, slot_len, enc_len))
    layer_out = jnp.moveaxis(stacked[0], 0, 1)
    hidden_grad = jnp.moveaxis(stacked[1], 0, 1)
    encoder_grad = stacked[2]
    return (layer_out, hidden_grad, encoder_grad, totals[0], totals[1], totals[2], totals[3], totals[4], totals[5], totals[6], totals[7], totals[8], totals[9], totals[10], totals[11], totals[12], totals[13], totals[14], totals[15], totals[16])
```

```python
import functools

import jax
import jax.numpy as jnp
from jax import lax
from jax.experimental import pallas as pl
from jax.experimental.pallas import tpu as pltpu
from jax.sharding import PartitionSpec as P

HEAD_DIM = 64
BUCKETS = 32
LANE = 128
GROUP = 4
eps_norm = 1e-05
neg_fill = -1e30
bf16 = jnp.bfloat16
f32 = jnp.float32
CORE, XBIT, YBIT = 1, 2, 4
VMEM_LIMIT = 60 * 1024 * 1024


def gelu_exact(values):
    return jax.nn.gelu(values, approximate=False)


def matmul(left_side, right_side):
    return jnp.dot(left_side, right_side, preferred_element_type=f32)


def matmul_back(left_side, right_side):
    return lax.dot_general(left_side, right_side, (((1,), (1,)), ((), ())), preferred_element_type=f32)


def outer_rows(left_side, right_side):
    return lax.dot_general(left_side, right_side, (((0,), (0,)), ((), ())), preferred_element_type=f32)


def norm_forward(values, gain, shift):
    row_mean = jnp.mean(values, axis=-1, keepdims=True)
    centered = values - row_mean
    scale = lax.rsqrt(jnp.mean(centered * centered, axis=-1, keepdims=True) + eps_norm)
    unit = centered * scale
    return unit * gain + shift, unit, scale


def norm_backward(unit, scale, gain, cotangent):
    back_unit = cotangent * gain
    first = jnp.mean(back_unit, axis=-1, keepdims=True)
    second = jnp.mean(back_unit * unit, axis=-1, keepdims=True)
    back = scale * (back_unit - first - unit * second)
    return back, jnp.sum(cotangent * unit, axis=0), jnp.sum(cotangent, axis=0)


def dot_nt(left_side, right_side):
    return lax.dot_general(left_side, right_side, (((1,), (1,)), ((), ())), preferred_element_type=f32)


def dot_nn(left_side, right_side):
    return lax.dot_general(left_side, right_side, (((1,), (0,)), ((), ())), preferred_element_type=f32)


def dot_tn(left_side, right_side):
    return lax.dot_general(left_side, right_side, (((0,), (0,)), ((), ())), preferred_element_type=f32)


def pick_lanes(table, index):
    return jnp.take_along_axis(table, index, axis=1)


def stack_heads(pair, low_half):
    zero = jnp.zeros_like(pair)
    return jnp.concatenate([jnp.where(low_half, pair, zero), jnp.where(low_half, zero, pair)], axis=0)


def rows_of(ref, first, last, cols):
    block = ref[first:last, 0, :, cols]
    return block.reshape(block.shape[0] * block.shape[1], block.shape[2])


def self_forward_kernel(
    length_ref, bounds_ref, posq_ref, posk_ref, q_ref, e_ref, k_ref, v_ref, o_ref, p_ref, own_ref,
    index_ref, mask_ref,
):
    slot = pl.program_id(0)
    lanes, _, rows, _ = q_ref.shape
    pieces = k_ref.shape[0] - (lanes - 1)
    keys = pieces * k_ref.shape[2]

    @pl.when(pl.program_id(1) == 0)
    def _():
        distance = posq_ref[...] - posk_ref[...]
        bucket = jnp.zeros(distance.shape, jnp.int32)
        for level in range(1, BUCKETS):
            bucket = bucket + (distance >= bounds_ref[level]).astype(jnp.int32)
        index_ref[...] = bucket
        valid = posk_ref[...] < length_ref[slot]
        mask_ref[0] = jnp.where(valid & (distance >= 0), 0.0, neg_fill)
        mask_ref[1] = jnp.where(valid & (distance > 0), 0.0, neg_fill)

    low_half = lax.broadcasted_iota(jnp.int32, (1, LANE), 1) < HEAD_DIM
    lane_id = lax.broadcasted_iota(jnp.int32, (1, LANE), 1)
    tables = [e_ref[lane, 0].astype(f32) for lane in range(lanes)]
    own_all = [jnp.zeros((rows, LANE), f32) for _ in range(lanes)]
    for pair in range(GROUP // 2):
        cols = slice(pair * LANE, (pair + 1) * LANE)
        q_pair = rows_of(q_ref, 0, lanes, cols) * jnp.asarray(HEAD_DIM**-0.5, bf16)
        k_main = rows_of(k_ref, 0, pieces, cols)
        v_main = rows_of(v_ref, 0, pieces, cols)
        scores = dot_nt(stack_heads(q_pair, low_half), k_main)
        own_pair = []
        for half in range(2):
            head = pair * 2 + half
            keep = low_half if half == 0 else jnp.logical_not(low_half)
            for lane in range(lanes):
                start = (half * lanes + lane) * rows
                part = scores[start : start + rows]
                bias = jnp.concatenate(
                    [
                        pick_lanes(tables[lane], index_ref[:, c * LANE : (c + 1) * LANE] + head * BUCKETS)
                        for c in range(keys // LANE)
                    ],
                    axis=1,
                )
                part = part + bias + mask_ref[min(lane, 1)]
                top = jnp.max(part, axis=1, keepdims=True)
                if lane > 0:
                    q_row = q_pair[lane * rows : (lane + 1) * rows].astype(f32)
                    k_row = k_ref[pieces + lane - 1, 0, :, cols].astype(f32)
                    own = jnp.sum(jnp.where(keep, q_row * k_row, 0.0), axis=1, keepdims=True)
                    own = own + tables[lane][:, head * BUCKETS : head * BUCKETS + 1]
                    top = jnp.maximum(top, own)
                    own_exp = jnp.exp(own - top)
                terms = jnp.exp(part - top)
                total = jnp.sum(terms, axis=1, keepdims=True)
                if lane > 0:
                    total = total + own_exp
                inverse = 1.0 / total
                p_ref[0, head, lane * rows : (lane + 1) * rows, :] = (terms * inverse).astype(bf16)
                if lane > 0:
                    own_prob = own_exp * inverse
                    own_all[lane] = jnp.where(lane_id == head, own_prob, own_all[lane])
                else:
                    own_prob = jnp.zeros((rows, 1), f32)
                own_pair.append(own_prob)
        p_low = p_ref[0, pair * 2 : pair * 2 + 2].reshape(2 * lanes * rows, keys)
        mixed = dot_nn(p_low, v_main)
        for lane in range(lanes):
            first = lane * rows
            second = (lanes + lane) * rows
            out = jnp.where(low_half, mixed[first : first + rows], mixed[second : second + rows])
            if lane > 0:
                own_prob = jnp.where(low_half, own_pair[lane], own_pair[lanes + lane])
                v_row = v_ref[pieces + lane - 1, 0, :, cols].astype(f32)
                out = out + own_prob.astype(bf16).astype(f32) * v_row
            o_ref[lane, 0, :, cols] = out.astype(bf16)
    for lane in range(lanes):
        own_ref[0, 0, lane * rows : (lane + 1) * rows, :] = own_all[lane]


def self_backward_kernel(
    posq_ref, posk_ref, low_ref, high_ref, p_ref, own_ref, do_ref, q_ref, k_ref, v_ref,
    dq_ref, dk_ref, dv_ref, de_ref, sums_ref,
):
    lanes, _, rows, _ = q_ref.shape
    pieces = k_ref.shape[0] - (lanes - 1)
    piece_rows = k_ref.shape[2]
    keys = pieces * piece_rows
    scale = HEAD_DIM**-0.5

    @pl.when((pl.program_id(0) == 0) & (pl.program_id(1) == 0))
    def _():
        ends = lax.broadcasted_iota(jnp.int32, (keys, keys), 1)
        sums_ref[...] = jnp.where(posk_ref[...] <= ends, 1.0, 0.0).astype(bf16)

    lane_id = lax.broadcasted_iota(jnp.int32, (1, LANE), 1)
    low_half = lane_id < HEAD_DIM
    near = posq_ref[...] - low_ref[...]
    far = posq_ref[...] - high_ref[...]
    back_embed = [jnp.zeros((rows, LANE), f32) for _ in range(lanes)]
    for pair in range(GROUP // 2):
        cols = slice(pair * LANE, (pair + 1) * LANE)
        q_pair = rows_of(q_ref, 0, lanes, cols) * jnp.asarray(scale, bf16)
        do_pair = rows_of(do_ref, 0, lanes, cols)
        k_main = rows_of(k_ref, 0, pieces, cols)
        v_main = rows_of(v_ref, 0, pieces, cols)
        q_stack = stack_heads(q_pair, low_half)
        do_stack = stack_heads(do_pair, low_half)
        back_probs = dot_nt(do_stack, v_main)
        p_low = p_ref[0, pair * 2 : pair * 2 + 2].reshape(2 * lanes * rows, keys)
        probs = p_low.astype(f32)
        weighted = probs * back_probs
        delta = jnp.sum(weighted, axis=1, keepdims=True)
        down_pair = []
        delta_list = []
        for half in range(2):
            head = pair * 2 + half
            keep = low_half if half == 0 else jnp.logical_not(low_half)
            for lane in range(lanes):
                start = (half * lanes + lane) * rows
                part = delta[start : start + rows]
                if lane > 0:
                    do_row = do_pair[lane * rows : (lane + 1) * rows].astype(f32)
                    v_row = v_ref[pieces + lane - 1, 0, :, cols].astype(f32)
                    back_own = jnp.sum(jnp.where(keep, do_row * v_row, 0.0), axis=1, keepdims=True)
                    own_prob = own_ref[0, 0, lane * rows : (lane + 1) * rows, head : head + 1]
                    part = part + own_prob * back_own
                    down_pair.append((own_prob * (back_own - part)).astype(bf16).astype(f32))
                else:
                    down_pair.append(None)
                delta_list.append(part)
        delta = jnp.concatenate(delta_list, axis=0)
        back_scores = (weighted - probs * delta).astype(bf16)
        back_q = dot_nn(back_scores, k_main)
        back_k = dot_tn(q_stack, back_scores)
        back_v = dot_tn(do_stack, p_low)
        dk_ref[:pieces, 0, :, cols] = back_k.T.astype(bf16).reshape(pieces, piece_rows, LANE)
        dv_ref[:pieces, 0, :, cols] = back_v.T.astype(bf16).reshape(pieces, piece_rows, LANE)
        prefix = dot_nn(back_scores, sums_ref[...])
        for lane in range(lanes):
            first = lane * rows
            second = (lanes + lane) * rows
            back = jnp.where(low_half, back_q[first : first + rows], back_q[second : second + rows])
            if lane > 0:
                k_row = k_ref[pieces + lane - 1, 0, :, cols].astype(f32)
                down = jnp.where(low_half, down_pair[lane], down_pair[lanes + lane])
                back = back + down * k_row
                own_low = jnp.where(
                    low_half,
                    own_ref[0, 0, lane * rows : (lane + 1) * rows, pair * 2 : pair * 2 + 1],
                    own_ref[0, 0, lane * rows : (lane + 1) * rows, pair * 2 + 1 : pair * 2 + 2],
                )
                own_low = own_low.astype(bf16).astype(f32)
                dk_ref[pieces + lane - 1, 0, :, cols] = (
                    down * q_pair[first : first + rows].astype(f32)
                ).astype(bf16)
                dv_ref[pieces + lane - 1, 0, :, cols] = (
                    own_low * do_pair[first : first + rows].astype(f32)
                ).astype(bf16)
            dq_ref[lane, 0, :, cols] = (back * scale).astype(bf16)
            for half in range(2):
                head = pair * 2 + half
                start = (half * lanes + lane) * rows
                upper = jnp.zeros((rows, LANE), f32)
                lower = jnp.zeros((rows, LANE), f32)
                for c in range(keys // LANE):
                    table = prefix[start : start + rows, c * LANE : (c + 1) * LANE]
                    spot = near - c * LANE
                    upper = jnp.where((spot >= 0) & (spot < LANE), pick_lanes(table, spot & (LANE - 1)), upper)
                    spot = far - c * LANE
                    lower = jnp.where((spot >= 0) & (spot < LANE), pick_lanes(table, spot & (LANE - 1)), lower)
                change = upper - lower
                if lane > 0:
                    change = change + jnp.where(lane_id == head * BUCKETS, down_pair[half * lanes + lane], 0.0)
                back_embed[lane] = jnp.where(lane_id // BUCKETS == head, change, back_embed[lane])
    for lane in range(lanes):
        de_ref[lane, 0] = back_embed[lane].astype(bf16)


def cross_forward_kernel(length_ref, posk_ref, q_ref, k_ref, v_ref, o_ref, p_ref):
    slot = pl.program_id(0)
    lanes, _, rows, _ = q_ref.shape
    pieces = k_ref.shape[0]
    keys = pieces * k_ref.shape[2]
    low_half = lax.broadcasted_iota(jnp.int32, (1, LANE), 1) < HEAD_DIM
    fill = jnp.where(posk_ref[...] < length_ref[slot], 0.0, neg_fill)
    count = lanes * rows
    for pair in range(GROUP // 2):
        cols = slice(pair * LANE, (pair + 1) * LANE)
        q_pair = rows_of(q_ref, 0, lanes, cols) * jnp.asarray(HEAD_DIM**-0.5, bf16)
        k_main = rows_of(k_ref, 0, pieces, cols)
        v_main = rows_of(v_ref, 0, pieces, cols)
        scores = dot_nt(stack_heads(q_pair, low_half), k_main) + fill
        top = jnp.max(scores, axis=1, keepdims=True)
        terms = jnp.exp(scores - top)
        inverse = 1.0 / jnp.sum(terms, axis=1, keepdims=True)
        p_low = (terms * inverse).astype(bf16)
        p_ref[0, pair * 2 : pair * 2 + 2] = p_low.reshape(2, count, keys)
        mixed = dot_nn(p_low, v_main)
        out = jnp.where(low_half, mixed[:count], mixed[count:]).astype(bf16)
        o_ref[:, 0, :, cols] = out.reshape(lanes, rows, LANE)


def cross_backward_kernel(p_ref, do_ref, q_ref, k_ref, v_ref, dq_ref, dk_ref, dv_ref):
    lanes, _, rows, _ = q_ref.shape
    pieces = k_ref.shape[0]
    piece_rows = k_ref.shape[2]
    keys = pieces * piece_rows
    count = lanes * rows
    scale = HEAD_DIM**-0.5
    low_half = lax.broadcasted_iota(jnp.int32, (1, LANE), 1) < HEAD_DIM
    for pair in range(GROUP // 2):
        cols = slice(pair * LANE, (pair + 1) * LANE)
        q_pair = rows_of(q_ref, 0, lanes, cols) * jnp.asarray(scale, bf16)
        do_pair = rows_of(do_ref, 0, lanes, cols)
        k_main = rows_of(k_ref, 0, pieces, cols)
        v_main = rows_of(v_ref, 0, pieces, cols)
        q_stack = stack_heads(q_pair, low_half)
        do_stack = stack_heads(do_pair, low_half)
        back_probs = dot_nt(do_stack, v_main)
        p_low = p_ref[0, pair * 2 : pair * 2 + 2].reshape(2 * count, keys)
        probs = p_low.astype(f32)
        weighted = probs * back_probs
        delta = jnp.sum(weighted, axis=1, keepdims=True)
        back_scores = (weighted - probs * delta).astype(bf16)
        back_q = dot_nn(back_scores, k_main)
        back_k = dot_tn(q_stack, back_scores)
        back_v = dot_tn(do_stack, p_low)
        dk_ref[:, 0, :, cols] = back_k.T.astype(bf16).reshape(pieces, piece_rows, LANE)
        dv_ref[:, 0, :, cols] = back_v.T.astype(bf16).reshape(pieces, piece_rows, LANE)
        back = jnp.where(low_half, back_q[:count], back_q[count:]) * scale
        dq_ref[:, 0, :, cols] = back.astype(bf16).reshape(lanes, rows, LANE)


def head_block(array, width=GROUP * HEAD_DIM):
    return pl.BlockSpec((array.shape[0], 1, array.shape[2], width), lambda s, g: (0, s, 0, g))


def whole_block(array):
    return pl.BlockSpec(array.shape, lambda s, g: (0,) * array.ndim)


SMEM_SPEC = pl.BlockSpec(memory_space=pltpu.SMEM)


def params():
    return pltpu.CompilerParams(vmem_limit_bytes=VMEM_LIMIT)


def shaped(shape, dtype):
    return jax.ShapeDtypeStruct(shape, dtype)


def attention_cost(matmuls, rows, keys, width, slots, passes):
    return pl.CostEstimate(
        flops=2 * matmuls * slots * rows * keys * width * 2,
        bytes_accessed=4 * slots * rows * keys * (width // HEAD_DIM),
        transcendentals=passes * slots * rows * keys * (width // HEAD_DIM),
    )


def self_forward(length, bounds, posq, posk, q, e, k, v):
    lanes, slots, rows, width = q.shape
    heads = width // HEAD_DIM
    keys = posk.shape[1]
    count = lanes * rows
    groups = heads // GROUP
    return pl.pallas_call(
        self_forward_kernel,
        grid=(slots, groups),
        in_specs=[
            SMEM_SPEC, SMEM_SPEC, whole_block(posq), whole_block(posk),
            head_block(q), head_block(e, GROUP * BUCKETS), head_block(k), head_block(v),
        ],
        out_specs=[
            head_block(q),
            pl.BlockSpec((1, GROUP, count, keys), lambda s, g: (s, g, 0, 0)),
            pl.BlockSpec((1, 1, count, LANE), lambda s, g: (s, g, 0, 0)),
        ],
        out_shape=[
            shaped(q.shape, bf16),
            shaped((slots, heads, count, keys), bf16),
            shaped((slots, groups, count, LANE), f32),
        ],
        scratch_shapes=[pltpu.VMEM((rows, keys), jnp.int32), pltpu.VMEM((2, rows, keys), f32)],
        compiler_params=params(),
        cost_estimate=attention_cost(2, count, keys, width, slots, 1),
        name="self_forward",
    )(length, bounds, posq, posk, q, e, k, v)


def self_backward(posq, posk_col, low, high, p, own, do, q, k, v):
    lanes, slots, rows, width = q.shape
    heads = width // HEAD_DIM
    keys = p.shape[3]
    count = lanes * rows
    return pl.pallas_call(
        self_backward_kernel,
        grid=(slots, heads // GROUP),
        in_specs=[
            whole_block(posq), whole_block(posk_col), whole_block(low), whole_block(high),
            pl.BlockSpec((1, GROUP, count, keys), lambda s, g: (s, g, 0, 0)),
            pl.BlockSpec((1, 1, count, LANE), lambda s, g: (s, g, 0, 0)),
            head_block(do), head_block(q), head_block(k), head_block(v),
        ],
        out_specs=[
            head_block(q), head_block(k), head_block(v),
            pl.BlockSpec((lanes, 1, rows, GROUP * BUCKETS), lambda s, g: (0, s, 0, g)),
        ],
        out_shape=[
            shaped(q.shape, bf16), shaped(k.shape, bf16), shaped(v.shape, bf16),
            shaped((lanes, slots, rows, heads * BUCKETS), bf16),
        ],
        scratch_shapes=[pltpu.VMEM((keys, keys), bf16)],
        compiler_params=params(),
        cost_estimate=attention_cost(6, count, keys, width, slots, 1),
        name="self_backward",
    )(posq, posk_col, low, high, p, own, do, q, k, v)


def cross_forward(length, posk, q, k, v):
    lanes, slots, rows, width = q.shape
    heads = width // HEAD_DIM
    keys = posk.shape[1]
    count = lanes * rows
    return pl.pallas_call(
        cross_forward_kernel,
        grid=(slots, heads // GROUP),
        in_specs=[SMEM_SPEC, whole_block(posk), head_block(q), head_block(k), head_block(v)],
        out_specs=[head_block(q), pl.BlockSpec((1, GROUP, count, keys), lambda s, g: (s, g, 0, 0))],
        out_shape=[shaped(q.shape, bf16), shaped((slots, heads, count, keys), bf16)],
        compiler_params=params(),
        cost_estimate=attention_cost(2, count, keys, width, slots, 1),
        name="cross_forward",
    )(length, posk, q, k, v)


def cross_backward(p, do, q, k, v):
    lanes, slots, rows, width = q.shape
    heads = width // HEAD_DIM
    keys = p.shape[3]
    count = lanes * rows
    return pl.pallas_call(
        cross_backward_kernel,
        grid=(slots, heads // GROUP),
        in_specs=[
            pl.BlockSpec((1, GROUP, count, keys), lambda s, g: (s, g, 0, 0)),
            head_block(do), head_block(q), head_block(k), head_block(v),
        ],
        out_specs=[head_block(q), head_block(k), head_block(v)],
        out_shape=[shaped(q.shape, bf16), shaped(k.shape, bf16), shaped(v.shape, bf16)],
        compiler_params=params(),
        cost_estimate=attention_cost(5, count, keys, width, slots, 0),
        name="cross_backward",
    )(p, do, q, k, v)


def ctx_hop(array, bit):
    size = lax.axis_size("ctx")
    return lax.ppermute(array, "ctx", [(i, i ^ bit) for i in range(size)])


def z_hop(array, step):
    size = lax.axis_size("fsdp")
    return lax.ppermute(array, "fsdp", [(i, (i + step) % size) for i in range(size)])


def ctx_spread(array, axis, cut):
    from_x = ctx_hop(array, XBIT)
    from_y = ctx_hop(array, YBIT)
    size = array.shape[axis]
    corner_one = ctx_hop(lax.slice_in_dim(from_y, 0, cut, axis=axis), XBIT)
    corner_two = ctx_hop(lax.slice_in_dim(from_x, cut, size, axis=axis), YBIT)
    near = [array, from_x, from_y, corner_one, corner_two]
    return near + [ctx_hop(item, CORE) for item in near]


SPREAD_PLAN = tuple(
    (offset + core, part) for core in (0, 1) for offset, part in ((0, 0), (XBIT, 0), (YBIT, 0), (XBIT + YBIT, 1), (XBIT + YBIT, 2))
)


def piece_number(index):
    return (index & 1) * 4 + (index >> 1)


def block_copies(layout):
    copies = []
    row = 0
    for number, (shard_rows, columns) in enumerate(layout):
        piece_rows = shard_rows // 8
        if columns >= 1024:
            for block in range(columns // 1024):
                copies.append((row, piece_rows, 0, 1024, number, 0, block * 1024))
                row += piece_rows
        else:
            parts = 1024 // columns
            rows = piece_rows // parts
            for part in range(parts):
                copies.append((row, rows, part * columns, columns, number, part * rows, 0))
            row += rows
    return tuple(copies), row


def to_buffer(pieces, layout):
    rows = []
    for piece, (shard_rows, columns) in zip(pieces, layout):
        piece_rows = shard_rows // 8
        if columns >= 1024:
            for block in range(columns // 1024):
                rows.append(piece[:, block * 1024 : (block + 1) * 1024])
        else:
            parts = 1024 // columns
            step = piece_rows // parts
            rows.append(jnp.concatenate([piece[i * step : (i + 1) * step] for i in range(parts)], axis=1))
    return jnp.concatenate(rows, axis=0)


def place_copies(copies, cut):
    def chosen(part):
        if part == 0:
            return copies
        if part == 1:
            return tuple(item for item in copies if item[0] < cut)
        return tuple((item[0] - cut,) + item[1:] for item in copies if item[0] >= cut)

    return chosen


def assemble_kernel(layout, copies, cut, steps, place_ref, *refs):
    count = len(layout)
    locals_ = refs[:count]
    arrivals = refs[count : count + len(SPREAD_PLAN)]
    outs = refs[count + len(SPREAD_PLAN) : -1]
    sem = refs[-1]
    chosen = place_copies(copies, cut)
    moves = []
    for number, (shard_rows, _) in enumerate(layout):
        start = pl.multiple_of(place_ref[0] * shard_rows, shard_rows)
        moves.append(pltpu.make_async_copy(locals_[number], outs[number].at[pl.ds(start, shard_rows), :], sem))
    for arrival, (offset, part) in zip(arrivals, SPREAD_PLAN):
        for step in range(1, steps):
            for row, rows, col, cols, number, prow, wcol in chosen(part):
                shard_rows = layout[number][0]
                piece_rows = shard_rows // 8
                start = place_ref[step] * shard_rows + place_ref[steps + offset] * piece_rows + prow
                start = pl.multiple_of(start, 16)
                moves.append(
                    pltpu.make_async_copy(
                        arrival.at[step - 1, pl.ds(row, rows), pl.ds(col, cols)],
                        outs[number].at[pl.ds(start, rows), pl.ds(wcol, cols)],
                        sem,
                    )
                )
    for move in moves:
        move.start()
    for move in moves:
        move.wait()


def gather_group(weights, layout, cut, z_index, c_index):
    steps = lax.axis_size("fsdp")
    copies, _ = block_copies(layout)
    number = piece_number(c_index)
    mine = to_buffer(
        [lax.dynamic_slice_in_dim(w, number * (rows // 8), rows // 8, 0) for w, (rows, _) in zip(weights, layout)],
        layout,
    )
    ring = [mine]
    for _ in range(steps - 1):
        ring.append(z_hop(ring[-1], 1))
    arrivals = ctx_spread(jnp.stack(ring[1:]), 1, cut)
    place = jnp.stack(
        [(z_index - step) % steps for step in range(steps)] + [piece_number(c_index ^ j) for j in range(8)]
    ).astype(jnp.int32)
    vmem = pl.BlockSpec(memory_space=pltpu.VMEM)
    total = sum(rows * columns for rows, columns in layout) * steps * 2
    return pl.pallas_call(
        functools.partial(assemble_kernel, layout, copies, cut, steps),
        in_specs=[SMEM_SPEC] + [vmem] * (len(weights) + len(arrivals)),
        out_specs=[pl.BlockSpec(memory_space=pl.ANY)] * len(weights),
        out_shape=[shaped((rows * steps, columns), bf16) for rows, columns in layout],
        scratch_shapes=[pltpu.SemaphoreType.DMA],
        compiler_params=params(),
        cost_estimate=pl.CostEstimate(flops=0, bytes_accessed=2 * total, transcendentals=0),
        name="assemble",
    )(place, *weights, *arrivals)


def fold_kernel(copies, buffer_rows, extra, quarter, table_ref, *refs):
    count = (len(refs) - 4) // 2
    keeps, arrivals, outs = refs[:count], refs[count : 2 * count], refs[2 * count :]
    step = pl.program_id(0)
    for number, out in enumerate(outs):

        @pl.when(step // quarter == number)
        def _(out=out):
            for row, rows, col, cols, weight, prow, wcol in copies:
                total = keeps[weight][0, prow : prow + rows, wcol : wcol + cols].astype(f32)
                total = total + arrivals[weight][0, prow : prow + rows, wcol : wcol + cols].astype(f32)
                out[0, row : row + rows, col : col + cols] = total.astype(bf16)
            if extra:
                total = keeps[-1][0].astype(f32) + arrivals[-1][0].astype(f32)
                out[0, buffer_rows:, :] = total.astype(bf16)


def fold_cores(keeps, arrivals, copies, buffer_rows, extra_rows, table, steps):
    quarter = steps
    total_steps = 4 * steps

    def by_table(array):
        return pl.BlockSpec((1,) + array.shape[1:], lambda t, tab: (tab[t], 0, 0))

    def by_extra(array):
        return pl.BlockSpec((1,) + array.shape[1:], lambda t, tab: (tab[total_steps + t], 0, 0))

    def specs(arrays):
        out = [by_table(a) for a in arrays]
        if extra_rows:
            out[-1] = by_extra(arrays[-1])
        return out

    rows = buffer_rows + extra_rows

    def out_spec(number):
        return pl.BlockSpec((1, rows, 1024), lambda t, tab: (jnp.clip(t - number * quarter, 0, quarter - 1), 0, 0))

    return pl.pallas_call(
        functools.partial(fold_kernel, copies, buffer_rows, extra_rows > 0, quarter),
        grid_spec=pltpu.PrefetchScalarGridSpec(
            num_scalar_prefetch=1,
            grid=(total_steps,),
            in_specs=specs(keeps) + specs(arrivals),
            out_specs=[out_spec(n) for n in range(4)],
        ),
        out_shape=[shaped((quarter, rows, 1024), bf16)] * 4,
        compiler_params=params(),
        cost_estimate=pl.CostEstimate(flops=0, bytes_accessed=6 * total_steps * rows * 1024, transcendentals=0),
        name="fold_cores",
    )(table, *keeps, *arrivals)


def unpack_kernel(layout, copies, cut, place_ref, *refs):
    arrivals = refs[: len(SPREAD_PLAN)]
    outs = refs[len(SPREAD_PLAN) :]
    chosen = place_copies(copies, cut)
    for arrival, (offset, part) in zip(arrivals, SPREAD_PLAN):
        for row, rows, col, cols, number, prow, wcol in chosen(part):
            piece_rows = layout[number][0] // 8
            start = pl.multiple_of(place_ref[offset] * piece_rows + prow, 8)
            outs[number][pl.ds(start, rows), wcol : wcol + cols] = arrival[row : row + rows, col : col + cols].astype(f32)


def reduce_group(keeps, sends, layout, cut, extra, z_index, c_index):
    steps = lax.axis_size("fsdp")
    half = steps // 2
    copies, buffer_rows = block_copies(layout)
    keeps = [k.reshape(steps * 4, rows // 8, columns) for k, (rows, columns) in zip(keeps, layout)]
    arrivals = [
        ctx_hop(s.reshape(steps * 4, rows // 8, columns), CORE) for s, (rows, columns) in zip(sends, layout)
    ]
    extra_rows = 0
    if extra is not None:
        rows = extra.shape[1]
        extra_rows = rows // steps
        pairs = extra.reshape(4, 2, rows, 1024)
        keeps.append(pairs[:, 0].reshape(4 * steps, extra_rows, 1024))
        arrivals.append(ctx_hop(pairs[:, 1].reshape(4 * steps, extra_rows, 1024), CORE))
    table, extra_table = [], []
    for first_x, on in ((True, 1), (True, 0), (False, 1), (False, 0)):
        for other in range(2):
            for kk in range(half):
                k = kk if first_x else kk + half
                offset = (other * 2 + on) if first_x else (on * 2 + other)
                table.append(((z_index + k) % steps) * 4 + ((c_index >> 1) ^ offset))
                extra_table.append(jnp.int32(offset * steps + k))
    table = jnp.stack(table + extra_table).astype(jnp.int32)
    send_x, keep_x, send_y, keep_y = fold_cores(keeps, arrivals, copies, buffer_rows, extra_rows, table, steps)
    got_x = ctx_hop(send_x, XBIT)
    got_y = ctx_hop(send_y, YBIT)

    def add(a, b):
        return (a.astype(f32) + b.astype(f32)).astype(bf16)

    second_x = ctx_hop(add(keep_x[half:], got_x[half:]), YBIT)
    second_y = ctx_hop(add(keep_y[half:], got_y[half:]), XBIT)
    done = []
    for keep, got, second in ((keep_x, got_x, second_x), (keep_y, got_y, second_y)):
        for kk in range(half):
            done.append(keep[kk].astype(f32) + got[kk].astype(f32) + second[kk].astype(f32))
    total = done[0][:buffer_rows]
    for k in range(1, steps):
        total = total + z_hop(done[k][:buffer_rows].astype(bf16), k).astype(f32)
    arrivals = ctx_spread(total.astype(bf16), 0, cut)
    place = jnp.stack([piece_number(c_index ^ j) for j in range(8)]).astype(jnp.int32)
    vmem = pl.BlockSpec(memory_space=pltpu.VMEM)
    grads = pl.pallas_call(
        functools.partial(unpack_kernel, layout, copies, cut),
        in_specs=[SMEM_SPEC] + [vmem] * len(arrivals),
        out_specs=[vmem] * len(layout),
        out_shape=[shaped((rows, columns), f32) for rows, columns in layout],
        compiler_params=params(),
        cost_estimate=pl.CostEstimate(flops=0, bytes_accessed=6 * 8 * buffer_rows * 1024, transcendentals=0),
        name="unpack",
    )(place, *arrivals)
    extra_sum = None
    if extra is not None:
        extra_sum = jnp.concatenate([item[buffer_rows:] for item in done], axis=0)
    return grads, extra_sum


def on_device(
    hidden, encoder_out, out_grad, slot_len, enc_len, rel_bucket,
    query_weight, key_weight, value_weight, relative_weight, output_weight, self_norm_gain, self_norm_shift,
    cross_query_weight, cross_key_weight, cross_value_weight, cross_output_weight, cross_norm_gain,
    cross_norm_shift, up_weight, down_weight, feed_norm_gain, feed_norm_shift,
):
    lanes, slots, halves, half_rows, width = hidden.shape
    rows = halves * half_rows
    enc_rows = encoder_out.shape[1]
    ctx_count = lax.axis_size("ctx")
    steps = lax.axis_size("fsdp")
    z_index = lax.axis_index("fsdp")
    c_index = lax.axis_index("ctx")
    seq_len = ctx_count * rows
    all_rows = lanes * slots * rows
    slab = (lanes, slots, rows, width)
    paired = ctx_count == 8 and steps % 2 == 0 and query_weight.shape[0] % 256 == 0 and width == 1024

    norms = jnp.stack(
        [self_norm_gain, self_norm_shift, cross_norm_gain, cross_norm_shift, feed_norm_gain, feed_norm_shift]
    )
    norms = lax.all_gather(norms, "fsdp", axis=1, tiled=True).astype(f32)
    gain_one, shift_one, gain_two, shift_two, gain_three, shift_three = [norms[i][None] for i in range(6)]

    self_set = (query_weight, key_weight, value_weight, output_weight, relative_weight)
    cross_set = (cross_query_weight, cross_key_weight, cross_value_weight, cross_output_weight)
    feed_set = (up_weight, down_weight)
    layouts = [tuple(w.shape for w in group) for group in (self_set, cross_set, feed_set)]
    x_all = hidden.reshape(all_rows, width)
    x_rows = hidden.reshape(slab)
    if paired:
        cuts = (64, 64, 128)
        first = gather_group(self_set, layouts[0], cuts[0], z_index, c_index)
        both = jnp.stack([x_rows[0], encoder_out.reshape(slots, rows, width)])
        spread = ctx_spread(both, 0, 1)
        peers = [c_index ^ j for j in range(8)]
        by_peer = {}
        for (offset, part), item in zip(SPREAD_PLAN, spread):
            by_peer.setdefault(offset, []).append((part, item))
        main_rows, enc_all = [], []
        for j in range(8):
            items = by_peer[j]
            if len(items) == 1:
                main_rows.append(items[0][1][0])
                enc_all.append(items[0][1][1])
            else:
                main_rows.append(items[0][1][0])
                enc_all.append(items[1][1][0])
        second = gather_group(cross_set, layouts[1], cuts[1], z_index, c_index)
        third = gather_group(feed_set, layouts[2], cuts[2], z_index, c_index)
    else:
        gather = lambda w: lax.all_gather(w, "fsdp", axis=0, tiled=True)
        first, second, third = [[gather(w) for w in group] for group in (self_set, cross_set, feed_set)]
        peers = [jnp.int32(j) for j in range(ctx_count)]
        main = lax.all_gather(x_rows[0], "ctx", axis=0)
        enc = lax.all_gather(encoder_out, "ctx", axis=0)
        main_rows = [main[j] for j in range(ctx_count)]
        enc_all = [enc[j] for j in range(ctx_count)]
    query_full, key_full, value_full, output_full, relative_full = first
    cquery_full, ckey_full, cvalue_full, coutput_full = second
    up_full, down_full = third

    place = jnp.stack(peers).astype(jnp.int32)
    local = jnp.arange(half_rows, dtype=jnp.int32)

    def both_halves(start):
        return jnp.concatenate([start + local, seq_len - 1 - start - local])

    positions = both_halves(c_index * half_rows)
    key_positions = jnp.concatenate([both_halves(place[j] * half_rows) for j in range(ctx_count)])
    enc_positions = (place[:, None] * enc_rows + jnp.arange(enc_rows, dtype=jnp.int32)[None, :]).reshape(1, -1)
    levels = jnp.arange(BUCKETS + 1, dtype=jnp.int32)
    bounds = jnp.sum((rel_bucket[None, :] < levels[:, None]).astype(jnp.int32), axis=1)
    low_edge = jnp.tile(bounds[:BUCKETS], LANE // BUCKETS)[None]
    high_edge = jnp.tile(bounds[1:], LANE // BUCKETS)[None]

    keyed = jnp.concatenate([jnp.stack(main_rows), x_rows[1:]], axis=0)
    keyed_flat = keyed.reshape(-1, width)
    q = matmul(x_all, query_full).astype(bf16).reshape(slab)
    e = matmul(x_all, relative_full).astype(bf16).reshape(lanes, slots, rows, -1)
    k = matmul(keyed_flat, key_full).astype(bf16).reshape(keyed.shape)
    v = matmul(keyed_flat, value_full).astype(bf16).reshape(keyed.shape)
    o, probs, own = self_forward(slot_len, bounds, positions[:, None], key_positions[None], q, e, k, v)
    o_flat = o.reshape(all_rows, width)
    resid_one = x_all.astype(f32) + matmul(o_flat, output_full)
    normed_one, unit_one, scale_one = norm_forward(resid_one, gain_one, shift_one)
    normed_one_low = normed_one.astype(bf16)

    enc_flat = jnp.stack(enc_all).reshape(-1, width)
    enc_shape = (ctx_count, slots, enc_rows, width)
    ck = matmul(enc_flat, ckey_full).astype(bf16).reshape(enc_shape)
    cv = matmul(enc_flat, cvalue_full).astype(bf16).reshape(enc_shape)
    cq = matmul(normed_one_low, cquery_full).astype(bf16).reshape(slab)
    oc, cprobs = cross_forward(enc_len, enc_positions, cq, ck, cv)
    oc_flat = oc.reshape(all_rows, width)
    resid_two = normed_one + matmul(oc_flat, coutput_full)
    normed_two, unit_two, scale_two = norm_forward(resid_two, gain_two, shift_two)
    normed_two_low = normed_two.astype(bf16)

    pre_act = matmul(normed_two_low, up_full)
    act, gelu_pull = jax.vjp(gelu_exact, pre_act)
    act_low = act.astype(bf16)
    resid_three = normed_two + matmul(act_low, down_full)
    normed_three, unit_three, scale_three = norm_forward(resid_three, gain_three, shift_three)
    layer_out = normed_three.astype(bf16)

    core = c_index & 1

    def split_cores(array):
        parts = array.reshape(array.shape[0], steps, 2, array.shape[1] // (2 * steps))
        pick = lambda which: lax.dynamic_index_in_dim(parts, which, 2, keepdims=False).reshape(array.shape[0], -1)
        return pick(core), pick(1 - core)

    def weight_grad(left, right):
        if not paired:
            return outer_rows(left, right).astype(bf16)
        return [outer_rows(side, right).astype(bf16) for side in left]

    splits = split_cores if paired else (lambda array: array)

    row_valid = (positions[None, None, :] < slot_len[None, :, None]).astype(f32)
    row_valid = jnp.broadcast_to(row_valid, (lanes, slots, rows)).reshape(all_rows, 1)
    cotangent = out_grad.reshape(all_rows, width).astype(f32) * row_valid
    back_three, gain_grad_three, shift_grad_three = norm_backward(unit_three, scale_three, gain_three, cotangent)
    back_feed = back_three.astype(bf16)
    grad_down = weight_grad(splits(act_low), back_feed)
    back_pre = gelu_pull(matmul_back(back_feed, down_full))[0].astype(bf16)
    grad_up = weight_grad(splits(normed_two_low), back_pre)
    back_normed_two = back_three + matmul_back(back_pre, up_full)
    back_two, gain_grad_two, shift_grad_two = norm_backward(unit_two, scale_two, gain_two, back_normed_two)

    back_cross = back_two.astype(bf16)
    grad_coutput = weight_grad(splits(oc_flat), back_cross)
    back_oc = matmul_back(back_cross, coutput_full).astype(bf16).reshape(slab)
    back_cq, back_ck, back_cv = cross_backward(cprobs, back_oc, cq, ck, cv)
    back_cq = back_cq.reshape(all_rows, width)
    back_ck = back_ck.reshape(-1, width)
    back_cv = back_cv.reshape(-1, width)
    enc_split = splits(enc_flat)
    grad_ckey = weight_grad(enc_split, back_ck)
    grad_cvalue = weight_grad(enc_split, back_cv)
    grad_cquery = weight_grad(splits(normed_one_low), back_cq)
    enc_part = (matmul_back(back_ck, ckey_full) + matmul_back(back_cv, cvalue_full)).astype(bf16)
    enc_part = enc_part.reshape(ctx_count, slots * enc_rows, width)
    back_normed_one = back_two + matmul_back(back_cq, cquery_full)
    back_one, gain_grad_one, shift_grad_one = norm_backward(unit_one, scale_one, gain_one, back_normed_one)

    back_self = back_one.astype(bf16)
    grad_output = weight_grad(splits(o_flat), back_self)
    back_o = matmul_back(back_self, output_full).astype(bf16).reshape(slab)
    back_q, back_k, back_v, back_e = self_backward(
        positions[:, None], key_positions[:, None], low_edge, high_edge, probs, own, back_o, q, k, v
    )
    back_q = back_q.reshape(all_rows, width)
    back_e = back_e.reshape(all_rows, -1)
    back_k = back_k.reshape(-1, width)
    back_v = back_v.reshape(-1, width)
    x_split = splits(x_all)
    keyed_split = splits(keyed_flat)
    grad_query = weight_grad(x_split, back_q)
    grad_relative = weight_grad(x_split, back_e)
    grad_key = weight_grad(keyed_split, back_k)
    grad_value = weight_grad(keyed_split, back_v)
    keyed_part = matmul_back(back_k, key_full) + matmul_back(back_v, value_full)
    main_count = ctx_count * slots * rows
    main_part = keyed_part[:main_count].astype(bf16).reshape(ctx_count, slots * rows, width)
    back_x = back_one + matmul_back(back_q, query_full) + matmul_back(back_e, relative_full)

    norm_grads = jnp.stack(
        [gain_grad_one, shift_grad_one, gain_grad_two, shift_grad_two, gain_grad_three, shift_grad_three]
    )
    norm_grads = lax.psum(norm_grads, ("fsdp", "ctx"))
    norm_grads = lax.dynamic_slice_in_dim(norm_grads, z_index * (width // steps), width // steps, 1)

    self_grads = [grad_query, grad_key, grad_value, grad_output, grad_relative]
    cross_grads = [grad_cquery, grad_ckey, grad_cvalue, grad_coutput]
    feed_grads = [grad_up, grad_down]
    if paired:
        def reduce(grads, index, extra):
            keeps = [g[0] for g in grads]
            sends = [g[1] for g in grads]
            return reduce_group(keeps, sends, layouts[index], cuts[index], extra, z_index, c_index)

        third_grads, _ = reduce(feed_grads, 2, None)
        second_grads, enc_sum = reduce(cross_grads, 1, enc_part)
        first_grads, main_sum = reduce(self_grads, 0, main_part)
    else:
        def reduce(g):
            shard = lax.psum_scatter(g, "fsdp", scatter_dimension=0, tiled=True)
            return lax.psum(shard, "ctx").astype(f32)

        first_grads, second_grads, third_grads = [
            [reduce(g) for g in group] for group in (self_grads, cross_grads, feed_grads)
        ]
        scatter = lambda part: lax.psum_scatter(part, "ctx", scatter_dimension=0, tiled=True)
        enc_sum = scatter(enc_part).astype(f32).reshape(-1, width)
        main_sum = scatter(main_part).astype(f32).reshape(-1, width)
    encoder_grad = enc_sum.reshape(slots, enc_rows, width)
    hidden_grad = back_x + jnp.concatenate([main_sum, keyed_part[main_count:]], axis=0)

    out_shape = hidden.shape
    return (
        layer_out.reshape(out_shape), hidden_grad.reshape(out_shape), encoder_grad,
        first_grads[0], first_grads[1], first_grads[2], first_grads[4], first_grads[3], norm_grads[0], norm_grads[1],
        second_grads[0], second_grads[1], second_grads[2], second_grads[3], norm_grads[2], norm_grads[3],
        third_grads[0], third_grads[1], norm_grads[4], norm_grads[5],
    )


def solution(mesh):
    rows = P("fsdp", None)
    vector = P("fsdp")
    slab = P(None, "fsdp", None, "ctx", None)
    encoder = P("fsdp", "ctx", None)
    weights = (rows,) * 5 + (vector,) * 2 + (rows,) * 4 + (vector,) * 2 + (rows,) * 2 + (vector,) * 2
    return jax.shard_map(
        on_device,
        mesh=mesh,
        in_specs=(slab, encoder, slab, vector, vector, P()) + weights,
        out_specs=(slab, slab, encoder) + weights,
        check_vma=False,
    )
```

```python
import functools

import jax
import jax.numpy as jnp
from jax import lax
from jax.experimental import pallas as pl
from jax.experimental.pallas import tpu as pltpu
from jax.sharding import PartitionSpec as P

HEAD_DIM = 64
BUCKETS = 32
LANE = 128
GROUP = 4
SUB = 8
eps_norm = 1e-05
neg_fill = -1e30
bf16 = jnp.bfloat16
f32 = jnp.float32
CORE, XBIT, YBIT = 1, 2, 4
VMEM_LIMIT = 63 * 1024 * 1024


def matmul(left_side, right_side):
    return jnp.dot(left_side, right_side, preferred_element_type=f32)


def matmul_back(left_side, right_side):
    return lax.dot_general(left_side, right_side, (((1,), (1,)), ((), ())), preferred_element_type=f32)


def outer_rows(left_side, right_side):
    return lax.dot_general(left_side, right_side, (((0,), (0,)), ((), ())), preferred_element_type=f32)


def norm_forward(values, gain, shift):
    row_mean = jnp.mean(values, axis=-1, keepdims=True)
    centered = values - row_mean
    scale = lax.rsqrt(jnp.mean(centered * centered, axis=-1, keepdims=True) + eps_norm)
    unit = centered * scale
    return unit * gain + shift, unit, scale


def norm_backward(unit, scale, gain, cotangent):
    back_unit = cotangent * gain
    first = jnp.mean(back_unit, axis=-1, keepdims=True)
    second = jnp.mean(back_unit * unit, axis=-1, keepdims=True)
    back = scale * (back_unit - first - unit * second)
    return back, jnp.sum(cotangent * unit, axis=0), jnp.sum(cotangent, axis=0)


def dot_nt(left_side, right_side):
    return lax.dot_general(left_side, right_side, (((1,), (1,)), ((), ())), preferred_element_type=f32)


def dot_nn(left_side, right_side):
    return lax.dot_general(left_side, right_side, (((1,), (0,)), ((), ())), preferred_element_type=f32)


def dot_tn(left_side, right_side):
    return lax.dot_general(left_side, right_side, (((0,), (0,)), ((), ())), preferred_element_type=f32)


def stack_heads(pair, low_half):
    zero = jnp.zeros_like(pair)
    return jnp.concatenate([jnp.where(low_half, pair, zero), jnp.where(low_half, zero, pair)], axis=0)


def rows_of(ref, first, last, cols):
    block = ref[first:last, 0, :, cols]
    return block.reshape(block.shape[0] * block.shape[1], block.shape[2])


def fill_one_hot(bucket_ref, one_hot_ref):
    keys = bucket_ref.shape[1]
    levels = lax.broadcasted_iota(jnp.int32, (BUCKETS, keys), 0)

    def fill(row, carry):
        line = jnp.broadcast_to(bucket_ref[pl.ds(row, 1), :], (BUCKETS, keys))
        start = pl.multiple_of(lax.rem(row, SUB) * BUCKETS, BUCKETS)
        one_hot_ref[row // SUB, pl.ds(start, BUCKETS), :] = jnp.where(line == levels, 1.0, 0.0).astype(bf16)
        return carry

    lax.fori_loop(0, bucket_ref.shape[0], fill, 0)


def fill_buckets(distance, bounds_ref, bucket_ref):
    bucket_ref[...] = jnp.zeros(distance.shape, jnp.int32)

    def fill(level, carry):
        bucket_ref[...] += (distance >= bounds_ref[level]).astype(jnp.int32)
        return carry

    lax.fori_loop(1, BUCKETS, fill, 0)


def own_block_mask(rows):
    row = lax.broadcasted_iota(jnp.int32, (rows, SUB * BUCKETS), 0)
    col = lax.broadcasted_iota(jnp.int32, (rows, SUB * BUCKETS), 1)
    return (row & (SUB - 1)) == (col // BUCKETS)


def self_forward_kernel(
    length_ref, bounds_ref, posq_ref, posk_ref, q_ref, e_ref, k_ref, v_ref, o_ref, p_ref, own_ref,
    bucket_ref, one_hot_ref, spread_ref, bias_ref,
):
    slot = pl.program_id(0)
    group = pl.program_id(1)
    lanes, _, rows, _ = q_ref.shape
    pieces = k_ref.shape[0] - (lanes - 1)
    keys = pieces * k_ref.shape[2]
    heads = bias_ref.shape[0]
    span = SUB * BUCKETS

    @pl.when((slot == 0) & (group == 0))
    def _():
        fill_buckets(posq_ref[...] - posk_ref[...], bounds_ref, bucket_ref)
        fill_one_hot(bucket_ref, one_hot_ref)

    @pl.when(group == 0)
    def _():
        keep = own_block_mask(lanes * rows)
        source = lax.broadcasted_iota(jnp.int32, (LANE, span), 0)
        target = lax.broadcasted_iota(jnp.int32, (LANE, span), 1) & (BUCKETS - 1)
        for part in range(LANE // BUCKETS):
            copy = jnp.where(source == target + part * BUCKETS, 1.0, 0.0).astype(bf16)
            for block in range(heads * BUCKETS // LANE):
                rows_e = rows_of(e_ref, 0, lanes, slice(block * LANE, (block + 1) * LANE))
                head = block * (LANE // BUCKETS) + part
                spread_ref[head] = jnp.where(keep, dot_nn(rows_e, copy), 0.0)
        distance = posq_ref[...] - posk_ref[...]
        valid = posk_ref[...] < length_ref[slot]
        fills = [jnp.where(valid & (distance >= edge), 0.0, neg_fill) for edge in (0, 1)]
        for g in range(rows // SUB):
            starts = [lane * rows + g * SUB for lane in range(lanes)]
            left = [spread_ref[:, start : start + SUB, :].reshape(heads * SUB, span) for start in starts]
            bias = dot_nn(jnp.concatenate(left, axis=0).astype(bf16), one_hot_ref[g])
            bias = bias.reshape(lanes, heads, SUB, keys)
            for lane, start in enumerate(starts):
                fill = fills[min(lane, 1)][None, g * SUB : (g + 1) * SUB, :]
                bias_ref[:, start : start + SUB, :] = bias[lane] + fill

    low_half = lax.broadcasted_iota(jnp.int32, (1, LANE), 1) < HEAD_DIM
    lane_id = lax.broadcasted_iota(jnp.int32, (1, LANE), 1)
    own_all = [jnp.zeros((rows, LANE), f32) for _ in range(lanes)]
    e_cols = pl.ds(pl.multiple_of(group * (GROUP * BUCKETS), LANE), GROUP * BUCKETS)
    tables = [None] + [e_ref[lane, 0, :, e_cols].astype(f32) for lane in range(1, lanes)]
    for pair in range(GROUP // 2):
        cols = slice(pair * LANE, (pair + 1) * LANE)
        q_pair = rows_of(q_ref, 0, lanes, cols) * jnp.asarray(HEAD_DIM**-0.5, bf16)
        k_main = rows_of(k_ref, 0, pieces, cols)
        v_main = rows_of(v_ref, 0, pieces, cols)
        scores = dot_nt(stack_heads(q_pair, low_half), k_main)
        own_pair = []
        for half in range(2):
            head = pair * 2 + half
            keep = low_half if half == 0 else jnp.logical_not(low_half)
            for lane in range(lanes):
                start = (half * lanes + lane) * rows
                part = scores[start : start + rows]
                part = part + bias_ref[group * GROUP + head, lane * rows : (lane + 1) * rows, :]
                top = jnp.max(part, axis=1, keepdims=True)
                if lane > 0:
                    q_row = q_pair[lane * rows : (lane + 1) * rows].astype(f32)
                    k_row = k_ref[pieces + lane - 1, 0, :, cols].astype(f32)
                    own = jnp.sum(jnp.where(keep, q_row * k_row, 0.0), axis=1, keepdims=True)
                    own = own + tables[lane][:, head * BUCKETS : head * BUCKETS + 1]
                    top = jnp.maximum(top, own)
                    own_exp = jnp.exp(own - top)
                terms = jnp.exp(part - top)
                total = jnp.sum(terms, axis=1, keepdims=True)
                if lane > 0:
                    total = total + own_exp
                inverse = 1.0 / total
                p_ref[0, head, lane * rows : (lane + 1) * rows, :] = (terms * inverse).astype(bf16)
                if lane > 0:
                    own_prob = own_exp * inverse
                    own_all[lane] = jnp.where(lane_id == head, own_prob, own_all[lane])
                else:
                    own_prob = jnp.zeros((rows, 1), f32)
                own_pair.append(own_prob)
        p_low = p_ref[0, pair * 2 : pair * 2 + 2].reshape(2 * lanes * rows, keys)
        mixed = dot_nn(p_low, v_main)
        for lane in range(lanes):
            first = lane * rows
            second = (lanes + lane) * rows
            out = jnp.where(low_half, mixed[first : first + rows], mixed[second : second + rows])
            if lane > 0:
                own_prob = jnp.where(low_half, own_pair[lane], own_pair[lanes + lane])
                v_row = v_ref[pieces + lane - 1, 0, :, cols].astype(f32)
                out = out + own_prob.astype(bf16).astype(f32) * v_row
            o_ref[lane, 0, :, cols] = out.astype(bf16)
    for lane in range(lanes):
        own_ref[0, 0, lane * rows : (lane + 1) * rows, :] = own_all[lane]


def self_backward_kernel(
    held, bounds_ref, posq_ref, posk_ref, p_ref, own_ref, do_ref, q_ref, k_ref, v_ref, *refs,
):
    dq_ref, dk_ref, dv_ref, de_ref = refs[held : held + 4]
    bucket_ref, one_hot_ref, turned_ref, scores_ref, down_ref, wide_ref = refs[held + 4 :]
    group = pl.program_id(1)
    lanes, _, rows, _ = q_ref.shape
    pieces = k_ref.shape[0] - (lanes - 1)
    piece_rows = k_ref.shape[2]
    keys = pieces * piece_rows
    scale = HEAD_DIM**-0.5

    heads = scores_ref.shape[0]
    span = SUB * BUCKETS

    @pl.when((pl.program_id(0) == 0) & (group == 0))
    def _():
        fill_buckets(posq_ref[...] - posk_ref[...], bounds_ref, bucket_ref)
        fill_one_hot(bucket_ref, one_hot_ref)
        for g in range(rows // SUB):
            turned_ref[g] = one_hot_ref[g].T

    lane_id = lax.broadcasted_iota(jnp.int32, (1, LANE), 1)
    low_half = lane_id < HEAD_DIM
    downs = [jnp.zeros((rows, LANE), f32) for _ in range(lanes)]
    for pair in range(GROUP // 2):
        cols = slice(pair * LANE, (pair + 1) * LANE)
        q_pair = rows_of(q_ref, 0, lanes, cols) * jnp.asarray(scale, bf16)
        do_pair = rows_of(do_ref, 0, lanes, cols)
        k_main = rows_of(k_ref, 0, pieces, cols)
        v_main = rows_of(v_ref, 0, pieces, cols)
        q_stack = stack_heads(q_pair, low_half)
        do_stack = stack_heads(do_pair, low_half)
        back_probs = dot_nt(do_stack, v_main)
        p_low = p_ref[0, pair * 2 : pair * 2 + 2].reshape(2 * lanes * rows, keys)
        probs = p_low.astype(f32)
        weighted = probs * back_probs
        delta = jnp.sum(weighted, axis=1, keepdims=True)
        down_pair = []
        delta_list = []
        for half in range(2):
            head = pair * 2 + half
            keep = low_half if half == 0 else jnp.logical_not(low_half)
            for lane in range(lanes):
                start = (half * lanes + lane) * rows
                part = delta[start : start + rows]
                if lane > 0:
                    do_row = do_pair[lane * rows : (lane + 1) * rows].astype(f32)
                    v_row = v_ref[pieces + lane - 1, 0, :, cols].astype(f32)
                    back_own = jnp.sum(jnp.where(keep, do_row * v_row, 0.0), axis=1, keepdims=True)
                    own_prob = own_ref[0, 0, lane * rows : (lane + 1) * rows, head : head + 1]
                    part = part + own_prob * back_own
                    down_pair.append((own_prob * (back_own - part)).astype(bf16).astype(f32))
                else:
                    down_pair.append(None)
                delta_list.append(part)
        delta = jnp.concatenate(delta_list, axis=0)
        back_scores = (weighted - probs * delta).astype(bf16)
        back_q = dot_nn(back_scores, k_main)
        back_k = dot_tn(q_stack, back_scores)
        back_v = dot_tn(do_stack, p_low)
        dk_ref[:pieces, 0, :, cols] = back_k.T.astype(bf16).reshape(pieces, piece_rows, LANE)
        dv_ref[:pieces, 0, :, cols] = back_v.T.astype(bf16).reshape(pieces, piece_rows, LANE)
        scores_ref[pl.ds(group * GROUP + pair * 2, 2)] = back_scores.astype(f32).reshape(2, lanes * rows, keys)
        for lane in range(lanes):
            first = lane * rows
            second = (lanes + lane) * rows
            back = jnp.where(low_half, back_q[first : first + rows], back_q[second : second + rows])
            if lane > 0:
                k_row = k_ref[pieces + lane - 1, 0, :, cols].astype(f32)
                down = jnp.where(low_half, down_pair[lane], down_pair[lanes + lane])
                back = back + down * k_row
                own_low = jnp.where(
                    low_half,
                    own_ref[0, 0, lane * rows : (lane + 1) * rows, pair * 2 : pair * 2 + 1],
                    own_ref[0, 0, lane * rows : (lane + 1) * rows, pair * 2 + 1 : pair * 2 + 2],
                )
                own_low = own_low.astype(bf16).astype(f32)
                dk_ref[pieces + lane - 1, 0, :, cols] = (
                    down * q_pair[first : first + rows].astype(f32)
                ).astype(bf16)
                dv_ref[pieces + lane - 1, 0, :, cols] = (
                    own_low * do_pair[first : first + rows].astype(f32)
                ).astype(bf16)
            dq_ref[lane, 0, :, cols] = (back * scale).astype(bf16)
            if lane > 0:
                for half in range(2):
                    spot = (pair * 2 + half) * BUCKETS
                    downs[lane] = jnp.where(lane_id == spot, down_pair[half * lanes + lane], downs[lane])
    for lane in range(1, lanes):
        down_ref[group, lane] = downs[lane]

    @pl.when(group == pl.num_programs(1) - 1)
    def _():
        keep = own_block_mask(lanes * heads * SUB)
        source = lax.broadcasted_iota(jnp.int32, (span, LANE), 0) & (BUCKETS - 1)
        target = lax.broadcasted_iota(jnp.int32, (span, LANE), 1) & (BUCKETS - 1)
        fold = jnp.where(source == target, 1.0, 0.0).astype(bf16)
        per_block = LANE // BUCKETS
        for g in range(rows // SUB):
            starts = [lane * rows + g * SUB for lane in range(lanes)]
            left = [scores_ref[:, start : start + SUB, :].reshape(heads * SUB, keys) for start in starts]
            sums = dot_nn(jnp.concatenate(left, axis=0).astype(bf16), turned_ref[g])
            embed = dot_nn(jnp.where(keep, sums, 0.0).astype(bf16), fold).reshape(lanes, heads, SUB, LANE)
            for lane in range(lanes):
                for block in range(heads // per_block):
                    out = embed[lane, block * per_block]
                    for part in range(1, per_block):
                        out = jnp.where(lane_id // BUCKETS == part, embed[lane, block * per_block + part], out)
                    if lane > 0:
                        out = out + down_ref[block, lane, g * SUB : (g + 1) * SUB, :]
                    wide_ref[lane, g * SUB : (g + 1) * SUB, block * LANE : (block + 1) * LANE] = out
        for lane in range(lanes):
            de_ref[lane, 0] = wide_ref[lane].astype(bf16)


def cross_forward_kernel(length_ref, posk_ref, q_ref, k_ref, v_ref, o_ref, p_ref):
    slot = pl.program_id(0)
    lanes, _, rows, _ = q_ref.shape
    pieces = k_ref.shape[0]
    keys = pieces * k_ref.shape[2]
    low_half = lax.broadcasted_iota(jnp.int32, (1, LANE), 1) < HEAD_DIM
    fill = jnp.where(posk_ref[...] < length_ref[slot], 0.0, neg_fill)
    count = lanes * rows
    for pair in range(GROUP // 2):
        cols = slice(pair * LANE, (pair + 1) * LANE)
        q_pair = rows_of(q_ref, 0, lanes, cols) * jnp.asarray(HEAD_DIM**-0.5, bf16)
        k_main = rows_of(k_ref, 0, pieces, cols)
        v_main = rows_of(v_ref, 0, pieces, cols)
        scores = dot_nt(stack_heads(q_pair, low_half), k_main) + fill
        top = jnp.max(scores, axis=1, keepdims=True)
        terms = jnp.exp(scores - top)
        inverse = 1.0 / jnp.sum(terms, axis=1, keepdims=True)
        p_low = (terms * inverse).astype(bf16)
        p_ref[0, pair * 2 : pair * 2 + 2] = p_low.reshape(2, count, keys)
        mixed = dot_nn(p_low, v_main)
        out = jnp.where(low_half, mixed[:count], mixed[count:]).astype(bf16)
        o_ref[:, 0, :, cols] = out.reshape(lanes, rows, LANE)


def cross_backward_kernel(p_ref, do_ref, q_ref, k_ref, v_ref, dq_ref, dk_ref, dv_ref):
    lanes, _, rows, _ = q_ref.shape
    pieces = k_ref.shape[0]
    piece_rows = k_ref.shape[2]
    keys = pieces * piece_rows
    count = lanes * rows
    scale = HEAD_DIM**-0.5
    low_half = lax.broadcasted_iota(jnp.int32, (1, LANE), 1) < HEAD_DIM
    for pair in range(GROUP // 2):
        cols = slice(pair * LANE, (pair + 1) * LANE)
        q_pair = rows_of(q_ref, 0, lanes, cols) * jnp.asarray(scale, bf16)
        do_pair = rows_of(do_ref, 0, lanes, cols)
        k_main = rows_of(k_ref, 0, pieces, cols)
        v_main = rows_of(v_ref, 0, pieces, cols)
        q_stack = stack_heads(q_pair, low_half)
        do_stack = stack_heads(do_pair, low_half)
        back_probs = dot_nt(do_stack, v_main)
        p_low = p_ref[0, pair * 2 : pair * 2 + 2].reshape(2 * count, keys)
        probs = p_low.astype(f32)
        weighted = probs * back_probs
        delta = jnp.sum(weighted, axis=1, keepdims=True)
        back_scores = (weighted - probs * delta).astype(bf16)
        back_q = dot_nn(back_scores, k_main)
        back_k = dot_tn(q_stack, back_scores)
        back_v = dot_tn(do_stack, p_low)
        dk_ref[:, 0, :, cols] = back_k.T.astype(bf16).reshape(pieces, piece_rows, LANE)
        dv_ref[:, 0, :, cols] = back_v.T.astype(bf16).reshape(pieces, piece_rows, LANE)
        back = jnp.where(low_half, back_q[:count], back_q[count:]) * scale
        dq_ref[:, 0, :, cols] = back.astype(bf16).reshape(lanes, rows, LANE)


def head_block(array, width=GROUP * HEAD_DIM):
    return pl.BlockSpec((array.shape[0], 1, array.shape[2], width), lambda s, g: (0, s, 0, g))


def slot_block(array):
    return pl.BlockSpec((array.shape[0], 1) + array.shape[2:], lambda s, g: (0, s, 0, 0))


def whole_block(array):
    return pl.BlockSpec(array.shape, lambda s, g: (0,) * array.ndim)


SMALL = pl.CostEstimate(flops=1000, bytes_accessed=1000, transcendentals=0)
SMEM_SPEC = pl.BlockSpec(memory_space=pltpu.SMEM)


def params():
    return pltpu.CompilerParams(vmem_limit_bytes=VMEM_LIMIT)


def shaped(shape, dtype):
    return jax.ShapeDtypeStruct(shape, dtype)


def self_forward(length, bounds, posq, posk, q, e, k, v):
    lanes, slots, rows, width = q.shape
    heads = width // HEAD_DIM
    keys = posk.shape[1]
    count = lanes * rows
    groups = heads // GROUP
    return pl.pallas_call(
        self_forward_kernel,
        grid=(slots, groups),
        in_specs=[
            SMEM_SPEC, SMEM_SPEC, whole_block(posq), whole_block(posk),
            head_block(q), slot_block(e), head_block(k), head_block(v),
        ],
        out_specs=[
            head_block(q),
            pl.BlockSpec((1, GROUP, count, keys), lambda s, g: (s, g, 0, 0)),
            pl.BlockSpec((1, 1, count, LANE), lambda s, g: (s, g, 0, 0)),
        ],
        out_shape=[
            shaped(q.shape, bf16),
            shaped((slots, heads, count, keys), bf16),
            shaped((slots, groups, count, LANE), f32),
        ],
        scratch_shapes=[
            pltpu.VMEM((rows, keys), jnp.int32),
            pltpu.VMEM((rows // SUB, SUB * BUCKETS, keys), bf16),
            pltpu.VMEM((heads, count, SUB * BUCKETS), f32),
            pltpu.VMEM((heads, count, keys), f32),
        ],
        compiler_params=params(),
        cost_estimate=SMALL,
        name="self_forward",
    )(length, bounds, posq, posk, q, e, k, v)


def self_backward(bounds, posq, posk, p, own, do, q, k, v, part, parts, made=()):
    lanes, slots, rows, width = q.shape
    heads = width // HEAD_DIM // parts
    keys = p.shape[3]
    count = lanes * rows
    groups = heads // GROUP
    base = part * groups

    def block(array):
        return pl.BlockSpec((array.shape[0], 1, array.shape[2], GROUP * HEAD_DIM), lambda s, g: (0, s, 0, base + g))

    inputs = [bounds, posq, posk, p, own, do, q, k, v]
    return pl.pallas_call(
        functools.partial(self_backward_kernel, len(made)),
        grid=(slots, groups),
        in_specs=[
            SMEM_SPEC, whole_block(posq), whole_block(posk),
            pl.BlockSpec((1, GROUP, count, keys), lambda s, g: (s, base + g, 0, 0)),
            pl.BlockSpec((1, 1, count, LANE), lambda s, g: (s, base + g, 0, 0)),
            block(do), block(q), block(k), block(v),
        ] + [pl.BlockSpec(memory_space=pl.ANY)] * len(made),
        out_specs=[
            block(q), block(k), block(v),
            pl.BlockSpec((lanes, 1, rows, heads * BUCKETS), lambda s, g: (0, s, 0, part)),
        ],
        out_shape=[
            shaped(q.shape, bf16), shaped(k.shape, bf16), shaped(v.shape, bf16),
            shaped((lanes, slots, rows, heads * parts * BUCKETS), bf16),
        ],
        scratch_shapes=[
            pltpu.VMEM((rows, keys), jnp.int32),
            pltpu.VMEM((rows // SUB, SUB * BUCKETS, keys), bf16),
            pltpu.VMEM((rows // SUB, keys, SUB * BUCKETS), bf16),
            pltpu.VMEM((heads, count, keys), f32),
            pltpu.VMEM((groups, lanes, rows, LANE), f32),
            pltpu.VMEM((lanes, rows, heads * BUCKETS), f32),
        ],
        input_output_aliases={len(inputs) + i: i for i in range(len(made))},
        compiler_params=params(),
        cost_estimate=SMALL,
        name="self_backward",
    )(*inputs, *made)


def cross_forward(length, posk, q, k, v):
    lanes, slots, rows, width = q.shape
    heads = width // HEAD_DIM
    keys = posk.shape[1]
    count = lanes * rows
    return pl.pallas_call(
        cross_forward_kernel,
        grid=(slots, heads // GROUP),
        in_specs=[SMEM_SPEC, whole_block(posk), head_block(q), head_block(k), head_block(v)],
        out_specs=[head_block(q), pl.BlockSpec((1, GROUP, count, keys), lambda s, g: (s, g, 0, 0))],
        out_shape=[shaped(q.shape, bf16), shaped((slots, heads, count, keys), bf16)],
        compiler_params=params(),
        cost_estimate=SMALL,
        name="cross_forward",
    )(length, posk, q, k, v)


def cross_backward(p, do, q, k, v):
    lanes, slots, rows, width = q.shape
    heads = width // HEAD_DIM
    keys = p.shape[3]
    count = lanes * rows
    return pl.pallas_call(
        cross_backward_kernel,
        grid=(slots, heads // GROUP),
        in_specs=[
            pl.BlockSpec((1, GROUP, count, keys), lambda s, g: (s, g, 0, 0)),
            head_block(do), head_block(q), head_block(k), head_block(v),
        ],
        out_specs=[head_block(q), head_block(k), head_block(v)],
        out_shape=[shaped(q.shape, bf16), shaped(k.shape, bf16), shaped(v.shape, bf16)],
        compiler_params=params(),
        cost_estimate=SMALL,
        name="cross_backward",
    )(p, do, q, k, v)


FEED_BLOCK = 512


def norm_parts(values):
    row_mean = jnp.mean(values, axis=-1, keepdims=True)
    centered = values - row_mean
    scale = lax.rsqrt(jnp.mean(centered * centered, axis=-1, keepdims=True) + eps_norm)
    return centered * scale, scale


def feed_kernel(
    sending, loading, core_ref, base_ref, mixed_ref, outer_ref, norms_ref, cot_ref, valid_ref, *refs,
):
    layout, copies, cut, parts, number_in = loading
    sources, refs = refs[:number_in], refs[number_in:]
    feed_body(sending, (layout, copies, cut, parts, sources), core_ref, base_ref, mixed_ref, outer_ref, norms_ref, cot_ref, valid_ref, *refs)


def feed_body(
    sending, loading, core_ref, base_ref, mixed_ref, outer_ref, norms_ref, cot_ref, valid_ref,
    out_ref, low_ref, act_ref, back_pre_ref, feed_ref, back_ref, cross_ref, back_mixed_ref, grads_ref, *rest,
):
    if sending:
        up_send_ref, down_send_ref, outer_send_ref, *rest = rest
    unit_ref, total_ref, turned_ref, act_all_ref, slope_ref, row_scale_ref, up_all_ref, down_all_ref, sems = rest
    phase, block = pl.program_id(0), pl.program_id(1)
    last = pl.num_programs(1) - 1
    cols = pl.ds(pl.multiple_of(block * FEED_BLOCK, FEED_BLOCK), FEED_BLOCK)

    up_ref = lambda: up_all_ref[:, cols]
    down_ref = lambda: down_all_ref[cols, :]
    layout, copies, cut, parts, sources = loading

    def loads():
        return group_loads(layout, copies, cut, parts, core_ref, sources, (up_all_ref, down_all_ref), sems, 1)

    @pl.when((phase == 0) & (block == 0))
    def _():
        for _, load in loads():
            load.start()
        unit, scale = norm_parts(base_ref[...] + dot_nn(mixed_ref[...], outer_ref[...]))
        normed = unit * norms_ref[2:3, :] + norms_ref[3:4, :]
        unit_ref[...] = unit
        row_scale_ref[...] = scale
        total_ref[...] = normed
        low_ref[...] = normed.astype(bf16)
        if sending:
            turned_ref[...] = core_columns(low_ref, 1 - core_ref[0], sending).T
        for _, load in loads():
            load.wait()

    @pl.when(phase == 0)
    def _():
        pre = dot_nn(low_ref[...], up_ref())
        below = 0.5 * (1.0 + lax.erf(pre * 0.7071067811865476))
        act = (pre * below).astype(bf16)
        slope_ref[:, cols] = below + pre * (jnp.exp(-0.5 * pre * pre) * 0.3989422804014327)
        act_all_ref[:, cols] = act
        act_ref[...] = act
        total_ref[...] += dot_nn(act, down_ref())

    @pl.when((phase == 0) & (block == last))
    def _():
        unit, scale = norm_parts(total_ref[...])
        gain = norms_ref[4:5, :]
        out_ref[...] = (unit * gain + norms_ref[5:6, :]).astype(bf16)
        cotangent = cot_ref[...].astype(f32) * valid_ref[...]
        back, gain_grad, shift_grad = norm_backward(unit, scale, gain, cotangent)
        grads_ref[2:3, :] = gain_grad[None]
        grads_ref[3:4, :] = shift_grad[None]
        total_ref[...] = back
        feed_ref[...] = back.astype(bf16)

    @pl.when(phase == 1)
    def _():
        back_act = dot_nt(feed_ref[...], down_ref())
        back_pre = (back_act * slope_ref[:, cols]).astype(bf16)
        back_pre_ref[...] = back_pre
        total_ref[...] += dot_nt(back_pre, up_ref())
        if sending:
            up_send_ref[...] = dot_nn(turned_ref[...], back_pre).astype(bf16)

            @pl.when((block & 1) == 1 - core_ref[0])
            def _():
                down_send_ref[...] = dot_tn(act_all_ref[:, cols], feed_ref[...]).astype(bf16)

    @pl.when((phase == 1) & (block == last))
    def _():
        back, gain_grad, shift_grad = norm_backward(
            unit_ref[...], row_scale_ref[...], norms_ref[2:3, :], total_ref[...]
        )
        back_ref[...] = back
        cross_ref[...] = back.astype(bf16)
        back_mixed_ref[...] = dot_nt(cross_ref[...], outer_ref[...]).astype(bf16)
        if sending:
            outer_send_ref[...] = dot_tn(core_columns(mixed_ref, 1 - core_ref[0], sending), cross_ref[...]).astype(bf16)
        grads_ref[0:1, :] = gain_grad[None]
        grads_ref[1:2, :] = shift_grad[None]


def feed_forward_backward(base, mixed, outer, norms, cot, valid, weights, arrivals, layout, cut, place, steps, sending):
    rows, width = base.shape
    hidden = layout[0][1]
    blocks = hidden // FEED_BLOCK
    copies, _ = block_copies(layout)
    sources = [*weights, *arrivals]
    parts = steps if arrivals else 1
    single = pl.Buffered(1)
    whole = lambda array: pl.BlockSpec(array.shape, lambda p, b, c: (0, 0), pipeline_mode=single)
    full = pl.BlockSpec((rows, width), lambda p, b, c: (0, 0))
    first = lambda p, b: jnp.where(p == 0, b, blocks - 1)
    second = lambda p, b: jnp.where(p == 0, 0, b)
    out_specs = [
        full, full,
        pl.BlockSpec((rows, FEED_BLOCK), lambda p, b, c: (0, first(p, b))),
        pl.BlockSpec((rows, FEED_BLOCK), lambda p, b, c: (0, second(p, b))),
        full, full, full, full,
        pl.BlockSpec((4, width), lambda p, b, c: (0, 0)),
    ]
    low = shaped((rows, width), bf16)
    wide = shaped((rows, hidden), bf16)
    out_shape = [low, low, wide, wide, low, shaped((rows, width), f32), low, low, shaped((4, width), f32)]
    if sending:
        assert hidden // (2 * steps) == FEED_BLOCK
        out_specs += [
            pl.BlockSpec((width // 2, FEED_BLOCK), lambda p, b, c: (0, second(p, b))),
            pl.BlockSpec((FEED_BLOCK, width), lambda p, b, c: (second(p, b) // 2, 0)),
            pl.BlockSpec((width // 2, width), lambda p, b, c: (0, 0)),
        ]
        out_shape += [
            shaped((width // 2, hidden), bf16), shaped((hidden // 2, width), bf16), shaped((width // 2, width), bf16),
        ]
    return pl.pallas_call(
        functools.partial(feed_kernel, steps if sending else 0, (layout, copies, cut, parts, len(sources))),
        grid_spec=pltpu.PrefetchScalarGridSpec(
            num_scalar_prefetch=1,
            grid=(2, blocks),
            in_specs=[
                whole(base), whole(mixed), whole(outer), whole(norms), whole(cot), whole(valid),
            ] + [pl.BlockSpec(memory_space=pl.ANY)] * len(sources),
            out_specs=out_specs,
            scratch_shapes=[
                pltpu.VMEM((rows, width), f32), pltpu.VMEM((rows, width), f32),
                pltpu.VMEM((width // 2, rows), bf16), pltpu.VMEM((rows, hidden), bf16), pltpu.VMEM((rows, hidden), f32),
                pltpu.VMEM((rows, 1), f32),
                pltpu.VMEM((width, hidden), bf16), pltpu.VMEM((hidden, width), bf16), pltpu.SemaphoreType.DMA((2,)),
            ],
        ),
        out_shape=out_shape,
        compiler_params=params(),
        cost_estimate=SMALL,
        name="feed",
    )(place, base, mixed, outer, norms, cot, valid, *sources)


def middle_kernel(
    sending, core_ref, back_cq_ref, query_ref, back_two_ref, unit_ref, scale_ref, norms_ref, outer_ref, *refs
):
    if sending:
        normed_ref, mixed_ref, back_ref, low_ref, back_mixed_ref, grads_ref, query_send_ref, outer_send_ref = refs
    else:
        back_ref, low_ref, back_mixed_ref, grads_ref = refs
    total = back_two_ref[...] + dot_nt(back_cq_ref[...], query_ref[...])
    back, gain_grad, shift_grad = norm_backward(unit_ref[...], scale_ref[...], norms_ref[0:1, :], total)
    back_ref[...] = back
    low_ref[...] = back.astype(bf16)
    grads_ref[0:1, :] = gain_grad[None]
    grads_ref[1:2, :] = shift_grad[None]
    back_mixed_ref[...] = dot_nt(low_ref[...], outer_ref[...]).astype(bf16)
    if sending:
        for left, right, out in ((normed_ref, back_cq_ref, query_send_ref), (mixed_ref, low_ref, outer_send_ref)):
            out[...] = dot_tn(core_columns(left, 1 - core_ref[0], sending), right[...]).astype(bf16)


def middle_backward(back_cq, query, back_two, unit, scale, norms, outer, normed, mixed, core, steps, sending):
    rows, width = back_two.shape
    low = shaped((rows, width), bf16)
    out_shape = [shaped((rows, width), f32), low, low, shaped((2, width), f32)]
    inputs = [back_cq, query, back_two, unit, scale, norms, outer]
    if sending:
        out_shape += [shaped((width // 2, width), bf16)] * 2
        inputs += [normed, mixed]
    vmem = pl.BlockSpec(memory_space=pltpu.VMEM)
    return pl.pallas_call(
        functools.partial(middle_kernel, steps if sending else 0),
        in_specs=[SMEM_SPEC] + [vmem] * len(inputs),
        out_specs=[vmem] * len(out_shape),
        out_shape=out_shape,
        compiler_params=params(),
        cost_estimate=SMALL,
        name="middle_backward",
    )(core, *inputs)


def pair_rows_kernel(tiles, back_k_ref, back_v_ref, key_ref, value_ref, even_ref, odd_ref, *rest):
    total = dot_nt(back_k_ref[...], key_ref[...]) + dot_nt(back_v_ref[...], value_ref[...])
    half = even_ref.shape[1]
    step = pl.program_id(0)

    @pl.when(step < tiles)
    def _():
        even_ref[0] = total[:half].astype(bf16)
        odd_ref[0] = total[half:].astype(bf16)

    if rest:

        @pl.when(step >= tiles)
        def _():
            rest[0][...] = total


def pair_rows(back_k, back_v, key, value, pieces, piece_rows):
    count, width = back_k.shape[0], key.shape[0]
    tile = 2 * piece_rows
    tiles = pieces // 2
    steps = count // tile
    resident = lambda array: pl.BlockSpec(array.shape, lambda t: (0, 0), pipeline_mode=pl.Buffered(1))
    rows = pl.BlockSpec((tile, back_k.shape[1]), lambda t: (t, 0))
    part = pl.BlockSpec((1, piece_rows, width), lambda t: (jnp.minimum(t, tiles - 1), 0, 0))
    out_specs, out_shape = [part, part], [shaped((tiles, piece_rows, width), bf16)] * 2
    if steps > tiles:
        out_specs.append(pl.BlockSpec((tile, width), lambda t: (jnp.maximum(t - tiles, 0), 0)))
        out_shape.append(shaped((count - tiles * tile, width), f32))
    return pl.pallas_call(
        functools.partial(pair_rows_kernel, tiles),
        grid=(steps,),
        in_specs=[rows, rows, resident(key), resident(value)],
        out_specs=out_specs,
        out_shape=out_shape,
        compiler_params=params(),
        cost_estimate=SMALL,
        name="pair_rows",
    )(back_k, back_v, key, value)


def own_rows_kernel(back_ref, back_q_ref, back_e_ref, query_ref, relative_ref, other_ref, out_ref):
    total = back_ref[...] + dot_nt(back_q_ref[...], query_ref[...]) + dot_nt(back_e_ref[...], relative_ref[...])
    skip = total.shape[0] - other_ref.shape[0]
    out_ref[:skip, :] = total[:skip]
    out_ref[skip:, :] = total[skip:] + other_ref[...]


def own_rows(back, back_q, back_e, query, relative, other):
    vmem = pl.BlockSpec(memory_space=pltpu.VMEM)
    return pl.pallas_call(
        own_rows_kernel,
        in_specs=[vmem] * 6,
        out_specs=vmem,
        out_shape=shaped(back.shape, f32),
        compiler_params=params(),
        cost_estimate=SMALL,
        name="own_rows",
    )(back, back_q, back_e, query, relative, other)


def after(value, *others):
    return lax.optimization_barrier((value,) + others)[0]


def ctx_hop(array, bit):
    size = lax.axis_size("ctx")
    return lax.ppermute(array, "ctx", [(i, i ^ bit) for i in range(size)])


def z_hop(array, step):
    size = lax.axis_size("fsdp")
    return lax.ppermute(array, "fsdp", [(i, (i + step) % size) for i in range(size)])


def first_spread(array):
    return array, ctx_hop(array, XBIT), ctx_hop(array, YBIT)


def corner_spread(firsts, axis, cut, *held):
    array, from_x, from_y = firsts
    if held:
        from_x, from_y, *_ = lax.optimization_barrier((from_x, from_y, *held))
    size = array.shape[axis]
    corner_one = ctx_hop(lax.slice_in_dim(from_y, 0, cut, axis=axis), XBIT)
    corner_two = ctx_hop(lax.slice_in_dim(from_x, cut, size, axis=axis), YBIT)
    return [array, from_x, from_y, corner_one, corner_two]


def core_spread(near):
    return near + [ctx_hop(item, CORE) for item in near]


def ctx_spread(array, axis, cut):
    return core_spread(corner_spread(first_spread(array), axis, cut))


SPREAD_PLAN = tuple(
    (offset + core, part) for core in (0, 1) for offset, part in ((0, 0), (XBIT, 0), (YBIT, 0), (XBIT + YBIT, 1), (XBIT + YBIT, 2))
)


def piece_number(index):
    return (index & 1) * 4 + (index >> 1)


def block_copies(layout):
    copies = []
    row = 0
    for number, (shard_rows, columns) in enumerate(layout):
        piece_rows = shard_rows // 8
        if columns >= 1024:
            for block in range(columns // 1024):
                copies.append((row, piece_rows, 0, 1024, number, 0, block * 1024))
                row += piece_rows
        else:
            parts = 1024 // columns
            rows = piece_rows // parts
            for part in range(parts):
                copies.append((row, rows, part * columns, columns, number, part * rows, 0))
            row += rows
    return tuple(copies), row


def place_copies(copies, cut):
    def chosen(part):
        if part == 0:
            return copies
        if part == 1:
            return tuple(item for item in copies if item[0] < cut)
        return tuple((item[0] - cut,) + item[1:] for item in copies if item[0] >= cut)

    return chosen


def group_loads(layout, copies, cut, steps, place_ref, sources, stages, sems, base=0):
    count = len(layout)
    chosen = place_copies(copies, cut)
    loads = []
    for number, (shard_rows, _) in enumerate(layout):
        target = stages[number]
        if steps > 1:
            start = pl.multiple_of(place_ref[base] * shard_rows, shard_rows)
            target = target.at[pl.ds(start, shard_rows), :]
        loads.append((number, pltpu.make_async_copy(sources[number], target, sems.at[number])))
    for arrival, (offset, part) in zip(sources[count:], SPREAD_PLAN):
        for step in range(1, steps):
            for row, rows, col, cols, number, prow, wcol in chosen(part):
                shard_rows = layout[number][0]
                start = place_ref[base + step] * shard_rows
                start = start + place_ref[base + steps + offset] * (shard_rows // 8) + prow
                source = arrival.at[step - 1, pl.ds(row, rows), pl.ds(col, cols)]
                target = stages[number].at[pl.ds(pl.multiple_of(start, 16), rows), pl.ds(wcol, cols)]
                loads.append((number, pltpu.make_async_copy(source, target, sems.at[number])))
    return loads


def place_of(z_index, c_index, steps):
    return jnp.stack(
        [(z_index - step) % steps for step in range(steps)] + [piece_number(c_index ^ j) for j in range(8)]
    ).astype(jnp.int32)


def project_kernel(layout, copies, cut, steps, products, pieces, tail, place_ref, *refs):
    count = len(layout)
    number_in = count + len(SPREAD_PLAN)
    own_ref, refs = (refs[0], refs[1:]) if tail else (None, refs)
    parts, sources, refs = refs[:pieces], refs[pieces : pieces + number_in], refs[pieces + number_in :]
    outs, refs = refs[: len(products)], refs[len(products) :]
    rows_out, weights_out, refs = refs[0], refs[1 : 1 + count], refs[1 + count :]
    rows_ref, stages, sems, row_sem, out_sem = refs[0], refs[1 : 1 + count], refs[-3], refs[-2], refs[-1]
    step = pl.program_id(0)
    piece_rows = parts[0].shape[0]

    def stores():
        moves = [pltpu.make_async_copy(rows_ref, rows_out, out_sem.at[count])]
        return moves + [pltpu.make_async_copy(stages[i], weights_out[i], out_sem.at[i]) for i in range(count)]

    @pl.when(step == 0)
    def _():
        loads = [
            pltpu.make_async_copy(part, rows_ref.at[pl.ds(j * piece_rows, piece_rows), :], row_sem)
            for j, part in enumerate(parts)
        ]
        loads += [load for _, load in group_loads(layout, copies, cut, steps, place_ref, sources, stages, sems)]
        for load in loads:
            load.start()
        if tail:
            rows_ref[pieces * piece_rows :, :] = own_ref[piece_rows:, :]
        for load in loads:
            load.wait()
        for move in stores():
            move.start()

    for out, (from_rows, number) in zip(outs, products):
        block = out.shape[1]
        cols = pl.ds(pl.multiple_of(step * block, LANE), block)
        left = rows_ref[...] if from_rows else own_ref[...]
        out[...] = dot_nn(left, stages[number][:, cols]).astype(bf16)

    @pl.when(step == pl.num_programs(0) - 1)
    def _():
        for move in stores():
            move.wait()


def project(own, parts, weights, arrivals, layout, cut, products, place, steps):
    copies, _ = block_copies(layout)
    count = len(layout)
    piece_rows, width = parts[0].shape
    rows = piece_rows * len(parts) + (own.shape[0] - piece_rows if own is not None else 0)
    blocks = 4
    hbm = pl.BlockSpec(memory_space=pl.ANY)
    first = [] if own is None else [own]
    shapes = [(shard_rows * steps, columns) for shard_rows, columns in layout]
    out_shape, out_specs = [], []
    for from_rows, number in products:
        left_rows = rows if from_rows else own.shape[0]
        out_shape.append(shaped((left_rows, shapes[number][1]), bf16))
        out_specs.append(pl.BlockSpec((left_rows, shapes[number][1] // blocks), lambda t: (0, t)))
    out_shape += [shaped((rows, width), bf16)] + [shaped(item, bf16) for item in shapes]
    outs = pl.pallas_call(
        functools.partial(project_kernel, layout, copies, cut, steps, products, len(parts), own is not None),
        grid=(blocks,),
        in_specs=[SMEM_SPEC]
        + [pl.BlockSpec(item.shape, lambda t: (0, 0), pipeline_mode=pl.Buffered(1)) for item in first]
        + [hbm] * (len(parts) + len(weights) + len(arrivals)),
        out_specs=out_specs + [hbm] * (1 + count),
        out_shape=out_shape,
        scratch_shapes=[pltpu.VMEM((rows, width), bf16)]
        + [pltpu.VMEM(item, bf16) for item in shapes]
        + [pltpu.SemaphoreType.DMA((count,)), pltpu.SemaphoreType.DMA, pltpu.SemaphoreType.DMA((count + 1,))],
        compiler_params=params(),
        cost_estimate=SMALL,
        name="project",
    )(place, *first, *parts, *weights, *arrivals)
    return outs[: len(products)], outs[len(products)], outs[len(products) + 1 :]


def query_kernel(norm_count, x_ref, mixed_ref, outer_ref, query_ref, vectors_ref, total_ref, unit_ref, scale_ref, low_ref, out_ref, norms_ref):
    pieces = vectors_ref.shape[0] // 16
    width = x_ref.shape[1]
    part = width // pieces
    copy_row = lax.broadcasted_iota(jnp.int32, (LANE, width), 0)
    copy_col = lax.broadcasted_iota(jnp.int32, (LANE, width), 1)
    copy = jnp.where(copy_row == lax.rem(copy_col, part), 1.0, 0.0).astype(bf16)
    wide = dot_nn(vectors_ref[...], copy)
    piece = lax.broadcasted_iota(jnp.int32, wide.shape, 0) // 16
    column = lax.broadcasted_iota(jnp.int32, wide.shape, 1) // part
    wide = jnp.where(piece == column, wide, 0.0).astype(bf16)
    pick_row = lax.broadcasted_iota(jnp.int32, (16, pieces * 16), 0)
    pick_col = lax.broadcasted_iota(jnp.int32, (16, pieces * 16), 1)
    pick = jnp.where(pick_row == lax.rem(pick_col, 16), 1.0, 0.0).astype(bf16)
    norms_ref[...] = dot_nn(pick, wide)
    unit, scale = norm_parts(x_ref[...].astype(f32) + dot_nn(mixed_ref[...], outer_ref[...]))
    total = unit * norms_ref[0:1, :] + norms_ref[1:2, :]
    unit_ref[...] = unit
    scale_ref[...] = scale
    total_ref[...] = total
    low_ref[...] = total.astype(bf16)
    out_ref[...] = dot_nn(low_ref[...], query_ref[...]).astype(bf16)


def query_rows(x, mixed, outer, query, vectors, norm_count):
    rows, width = x.shape
    full = lambda array: pl.BlockSpec(array.shape, lambda t: (0, 0))
    wide, low = shaped((rows, width), f32), shaped((rows, width), bf16)
    outs = [wide, wide, shaped((rows, 1), f32), low, low, shaped((16, width), f32)]
    return pl.pallas_call(
        functools.partial(query_kernel, norm_count),
        grid=(1,),
        in_specs=[full(x), full(mixed), full(outer), full(query), pl.BlockSpec((vectors.shape[0], LANE), lambda t: (0, 0))],
        out_specs=[full(item) for item in outs],
        out_shape=outs,
        compiler_params=params(),
        cost_estimate=SMALL,
        name="query_rows",
    )(x, mixed, outer, query, vectors)


def pieces_kernel(layouts, plans, place_ref, *refs):
    count = sum(len(layout) for layout in layouts)
    weights, outs, sem = refs[:count], refs[count:-1], refs[-1]
    moves = []
    first = 0
    for layout, copies, out in zip(layouts, plans, outs):
        for row, rows, col, cols, number, prow, wcol in copies:
            start = pl.multiple_of(place_ref[0] * (layout[number][0] // 8) + prow, 16)
            source = weights[first + number].at[pl.ds(start, rows), pl.ds(wcol, cols)]
            moves.append(pltpu.make_async_copy(source, out.at[pl.ds(row, rows), pl.ds(col, cols)], sem))
        first += len(layout)
    for move in moves:
        move.start()
    for move in moves:
        move.wait()


def own_pieces(groups, layouts, c_index):
    plans = [block_copies(layout) for layout in layouts]
    weights = [w for group in groups for w in group]
    return pl.pallas_call(
        functools.partial(pieces_kernel, layouts, [plan[0] for plan in plans]),
        in_specs=[SMEM_SPEC] + [pl.BlockSpec(memory_space=pl.ANY)] * len(weights),
        out_specs=[pl.BlockSpec(memory_space=pltpu.VMEM)] * len(groups),
        out_shape=[shaped((plan[1], 1024), bf16) for plan in plans],
        scratch_shapes=[pltpu.SemaphoreType.DMA],
        compiler_params=params(),
        cost_estimate=SMALL,
        name="own_pieces",
    )(piece_number(c_index).astype(jnp.int32).reshape(1), *weights)


def stack_kernel(count, *refs):
    out, sem = refs[count], refs[count + 1]
    moves = [pltpu.make_async_copy(refs[i], out.at[i], sem) for i in range(count)]
    for move in moves:
        move.start()
    for move in moves:
        move.wait()


def stack_rows(items):
    return pl.pallas_call(
        functools.partial(stack_kernel, len(items)),
        in_specs=[pl.BlockSpec(memory_space=pl.ANY)] * len(items),
        out_specs=pl.BlockSpec(memory_space=pltpu.VMEM),
        out_shape=shaped((len(items),) + items[0].shape, items[0].dtype),
        scratch_shapes=[pltpu.SemaphoreType.DMA],
        compiler_params=params(),
        cost_estimate=SMALL,
        name="stack_rows",
    )(*items)


def z_spread(mine):
    return [z_hop(mine, step) for step in range(1, lax.axis_size("fsdp"))]


def core_columns(ref, which, steps):
    block = ref.shape[1] // (2 * steps)
    parts = [ref[:, pl.ds(pl.multiple_of((2 * step + which) * block, block), block)] for step in range(steps)]
    return jnp.concatenate(parts, axis=1)


def send_kernel(count, steps, core_ref, left_ref, *refs):
    left = core_columns(left_ref, 1 - core_ref[0], steps)
    for right, out in zip(refs[:count], refs[count:]):
        out[...] = dot_tn(left, right[...]).astype(bf16)


def send_grads(left, rights, core, steps):
    vmem = pl.BlockSpec(memory_space=pltpu.VMEM)
    return pl.pallas_call(
        functools.partial(send_kernel, len(rights), steps),
        in_specs=[SMEM_SPEC] + [vmem] * (1 + len(rights)),
        out_specs=[vmem] * len(rights),
        out_shape=[shaped((left.shape[1] // 2, right.shape[1]), bf16) for right in rights],
        compiler_params=params(),
        cost_estimate=SMALL,
        name="send_grads",
    )(core, left, *rights)


def fold_grads_kernel(groups, steps, extra_rows, plain_rows, place_ref, *refs):
    count = len(groups)
    half = steps // 2
    lefts, refs = refs[: max(groups) + 1], refs[max(groups) + 1 :]
    rights, arrivals, refs = refs[:count], refs[count : 2 * count], refs[2 * count :]
    if extra_rows:
        extra_keep, extra_got, refs = refs[0], refs[1], refs[2:]
    if plain_rows:
        plain_keep, plain_got, refs = refs[0], refs[1], refs[2:]
    outs, work = refs[:4], refs[4:]
    step = pl.program_id(0)

    for number, group in enumerate(groups):
        work[number][...] = dot_tn(lefts[group][...], rights[number][...])
    for first_x in (True, False):

        @pl.when((step < half) if first_x else (step >= half))
        def _(first_x=first_x):
            send, keep = outs[:2] if first_x else outs[2:]
            for offset in range(4):
                y_bit, x_bit = offset >> 1, offset & 1
                on, other = (x_bit, y_bit) if first_x else (y_bit, x_bit)
                out = send if on else keep
                yx = place_ref[1] ^ offset
                row = extra_rows
                if extra_rows:
                    total = extra_keep[offset, 0].astype(f32) + extra_got[offset, 0].astype(f32)
                    out[other, 0, :extra_rows, :] = total.astype(bf16)
                for number in range(count):
                    piece, columns = arrivals[number].shape[1:]
                    total = work[number][pl.ds(pl.multiple_of(yx * piece, piece), piece), :]
                    total = (total + arrivals[number][yx].astype(f32)).astype(bf16)
                    if columns >= 1024:
                        for block in range(columns // 1024):
                            out[other, 0, row : row + piece, :] = total[:, block * 1024 : (block + 1) * 1024]
                            row += piece
                    else:
                        parts = 1024 // columns
                        low = piece // parts
                        for part in range(parts):
                            out[other, 0, row : row + low, part * columns : (part + 1) * columns] = total[
                                part * low : (part + 1) * low
                            ]
                        row += low
                if plain_rows:
                    total = plain_keep[yx].astype(f32) + plain_got[yx].astype(f32)
                    out[other, 0, row : row + plain_rows, :] = total.astype(bf16)


def fold_grads(pairs, arrivals, extra, plain, place, steps):
    half = steps // 2
    lefts = [left for left, _ in pairs]
    groups = [number for number, (_, rights) in enumerate(pairs) for _ in rights]
    rights = [right for _, some in pairs for right in some]

    def around(t, p):
        return lax.rem(p[0] + t, steps)

    def resident(array):
        return pl.BlockSpec(array.shape, lambda t, p: (0, 0), pipeline_mode=pl.Buffered(1))

    def by_z(array):
        return pl.BlockSpec((4,) + array.shape[1:], lambda t, p: (around(t, p), 0, 0))

    in_specs = [
        pl.BlockSpec((left.shape[0], left.shape[1] // (2 * steps)), lambda t, p: (0, 2 * around(t, p) + p[2]))
        for left in lefts
    ]
    in_specs += [resident(item) for item in rights] + [by_z(item) for item in arrivals]
    total_rows = sum(item.shape[1] * item.shape[2] // 1024 for item in arrivals)
    extra_rows = plain_rows = 0
    if extra is not None:
        extra_rows = extra[0].shape[2]
        in_specs += [pl.BlockSpec((4, 1, extra_rows, 1024), lambda t, p: (0, t, 0, 0))] * 2
    if plain is not None:
        plain_rows = plain[0].shape[1]
        in_specs += [by_z(item) for item in plain]
    total_rows += extra_rows + plain_rows
    a_spec = pl.BlockSpec((2, 1, total_rows, 1024), lambda t, p: (0, jnp.minimum(t, half - 1), 0, 0))
    b_spec = pl.BlockSpec((2, 1, total_rows, 1024), lambda t, p: (0, jnp.maximum(t - half, 0), 0, 0))
    return pl.pallas_call(
        functools.partial(fold_grads_kernel, groups, steps, extra_rows, plain_rows),
        grid_spec=pltpu.PrefetchScalarGridSpec(
            num_scalar_prefetch=1,
            grid=(steps,),
            in_specs=in_specs,
            out_specs=[a_spec, a_spec, b_spec, b_spec],
            scratch_shapes=[
                pltpu.VMEM((lefts[group].shape[1] // (2 * steps), right.shape[1]), f32)
                for group, right in zip(groups, rights)
            ],
        ),
        out_shape=[shaped((2, half, total_rows, 1024), bf16)] * 4,
        compiler_params=params(),
        cost_estimate=SMALL,
        name="fold_grads",
    )(place, *lefts, *rights, *arrivals, *(extra or ()), *(plain or ()))


def unpack_kernel(layout, copies, cut, place_ref, *refs):
    arrivals = refs[: len(SPREAD_PLAN)]
    outs = refs[len(SPREAD_PLAN) :]
    chosen = place_copies(copies, cut)
    for arrival, (offset, part) in zip(arrivals, SPREAD_PLAN):
        for row, rows, col, cols, number, prow, wcol in chosen(part):
            piece_rows = layout[number][0] // 8
            start = pl.multiple_of(place_ref[offset] * piece_rows + prow, 8)
            outs[number][pl.ds(start, rows), wcol : wcol + cols] = arrival[row : row + rows, col : col + cols].astype(f32)


def add_low(a, b):
    return (a.astype(f32) + b.astype(f32)).astype(bf16)


class Reduction:
    def __init__(self, pairs, sends, layout, cut, extra, plain, z_index, c_index):
        self.pairs = pairs
        self.layout, self.cut, self.c_index = layout, cut, c_index
        self.steps = steps = lax.axis_size("fsdp")
        self.half = steps // 2
        self.copies, self.rows = block_copies(layout)
        arrivals = [
            ctx_hop(s, CORE).reshape(steps * 4, rows // 8, columns) for s, (rows, columns) in zip(sends, layout)
        ]
        self.lead = 0
        if extra is not None:
            keep, send = extra
            self.lead = keep.shape[1] // steps
            split = (4, steps, self.lead, 1024)
            extra = (keep.reshape(split), ctx_hop(send, CORE).reshape(split))
        if plain is not None:
            plain = (plain[0], ctx_hop(plain[1], CORE))
        self.inputs = arrivals, extra, plain
        self.place = jnp.stack([z_index, c_index >> 1, c_index & 1]).astype(jnp.int32)

    def fold(self, *held):
        place = after(self.place, *held) if held else self.place
        self.folded = list(fold_grads(self.pairs, *self.inputs, place, self.steps))

    def first_hops(self, *held):
        self.folded[0], self.folded[2] = after(self.folded[0], *held), after(self.folded[2], *held)
        send_x, _, send_y, _ = self.folded
        self.first = ctx_hop(send_x, XBIT), ctx_hop(send_y, YBIT)

    def second_sums(self, *held):
        _, keep_x, _, keep_y = self.folded
        got_x, got_y = self.first
        if held:
            got_x, got_y, *_ = lax.optimization_barrier((got_x, got_y, *held))
        self.sums = add_low(keep_x[1], got_x[1]), add_low(keep_y[1], got_y[1])

    def second_hops(self):
        self.second = ctx_hop(self.sums[0], YBIT), ctx_hop(self.sums[1], XBIT)

    def z_sums(self, *held):
        _, keep_x, _, keep_y = self.folded
        second = lax.optimization_barrier((*self.second, *held))[:2] if held else self.second
        done = []
        for keep, got, late in ((keep_x, self.first[0], second[0]), (keep_y, self.first[1], second[1])):
            for kk in range(self.half):
                done.append(keep[0, kk].astype(f32) + got[0, kk].astype(f32) + late[kk].astype(f32))
        self.extra = [item[: self.lead] for item in done]
        self.mine = done[0][self.lead :]
        self.sums = [item[self.lead :].astype(bf16) for item in done[1:]]

    def z_hops(self):
        self.third = tuple(z_hop(item, k + 1) for k, item in enumerate(self.sums))

    def spread(self, *held):
        total = self.mine
        for item in (lax.optimization_barrier((*self.third, *held))[: len(self.third)] if held else self.third):
            total = total + item.astype(f32)
        self.arrivals = ctx_spread(total.astype(bf16), 0, self.cut)

    def grads(self):
        place = jnp.stack([piece_number(self.c_index ^ j) for j in range(8)]).astype(jnp.int32)
        vmem = pl.BlockSpec(memory_space=pltpu.VMEM)
        return pl.pallas_call(
            functools.partial(unpack_kernel, self.layout, self.copies, self.cut),
            in_specs=[SMEM_SPEC] + [vmem] * len(self.arrivals),
            out_specs=[vmem] * len(self.layout),
            out_shape=[shaped((rows, columns), f32) for rows, columns in self.layout],
            compiler_params=params(),
            cost_estimate=SMALL,
            name="unpack",
        )(place, *self.arrivals)

    def extra_sum(self):
        return jnp.concatenate(self.extra, axis=0)


def on_device(
    hidden, encoder_out, out_grad, slot_len, enc_len, rel_bucket,
    query_weight, key_weight, value_weight, relative_weight, output_weight, self_norm_gain, self_norm_shift,
    cross_query_weight, cross_key_weight, cross_value_weight, cross_output_weight, cross_norm_gain,
    cross_norm_shift, up_weight, down_weight, feed_norm_gain, feed_norm_shift,
):
    lanes, slots, halves, half_rows, width = hidden.shape
    rows = halves * half_rows
    enc_rows = encoder_out.shape[1]
    ctx_count = lax.axis_size("ctx")
    steps = lax.axis_size("fsdp")
    z_index = lax.axis_index("fsdp")
    c_index = lax.axis_index("ctx")
    seq_len = ctx_count * rows
    all_rows = lanes * slots * rows
    slab = (lanes, slots, rows, width)
    paired = ctx_count == 8 and steps % 2 == 0 and query_weight.shape[0] % 256 == 0 and width == 1024
    paired = paired and enc_rows == rows

    norms = jnp.stack(
        [self_norm_gain, self_norm_shift, cross_norm_gain, cross_norm_shift, feed_norm_gain, feed_norm_shift]
    )
    norm_count, norm_shard = norms.shape

    self_set = (query_weight, relative_weight, key_weight, value_weight)
    cross_set = (output_weight, cross_query_weight, cross_key_weight, cross_value_weight, cross_output_weight)
    feed_set = (up_weight, down_weight)
    layouts = [tuple(w.shape for w in group) for group in (self_set, cross_set, feed_set)]
    x_all = hidden.reshape(all_rows, width)
    x_rows = hidden.reshape(slab)
    if paired:
        cuts = (48, 96, 128)
        vectors = norms.reshape(norm_count, 8, norm_shard // 8).transpose(1, 0, 2)
        vectors = jnp.pad(vectors, ((0, 0), (0, 16 - norm_count), (0, 1024 - norm_shard // 8))).reshape(128, 1024)
        second_set = (*cross_set, vectors)
        second_layout = layouts[1] + (vectors.shape,)
        where = place_of(z_index, c_index, steps)
        main, enc = x_all[: slots * rows], encoder_out.reshape(slots * rows, width)
        main_x, enc_x = ctx_hop(main, XBIT), ctx_hop(enc, XBIT)
        main_y, enc_y = ctx_hop(main, YBIT), ctx_hop(enc, YBIT)
        mine = own_pieces((self_set, second_set, feed_set), (layouts[0], second_layout, layouts[2]), c_index)
        by_offset = lambda near: [item for pair in zip(near, [ctx_hop(n, CORE) for n in near]) for item in pair]
        stack = stack_rows(z_spread(mine[0]))
        main_near = [main, main_x, main_y, ctx_hop(main_y, XBIT)]
        enc_near = [enc, enc_x, enc_y, ctx_hop(enc_x, YBIT)]
        second_hops = z_spread(after(mine[1], stack))
        arrivals = ctx_spread(stack, 1, cuts[0])
        second_stack = stack_rows(second_hops)
        second_first = first_spread(second_stack)
        third_hops = z_spread(after(mine[2], second_stack))
        (q, e, k, v), keyed_flat, first = project(
            x_all, by_offset(main_near), self_set, arrivals, layouts[0], cuts[0],
            ((False, 0), (False, 1), (True, 2), (True, 3)), after(where, second_stack), steps,
        )
        peers = [c_index ^ j for j in range(8)]
    else:
        norms = lax.all_gather(norms, "fsdp", axis=1, tiled=True)
        gather = lambda w: lax.all_gather(w, "fsdp", axis=0, tiled=True)
        first, second, third = [[gather(w) for w in group] for group in (self_set, cross_set, feed_set)]
        peers = [jnp.int32(j) for j in range(ctx_count)]
        main = lax.all_gather(x_rows[0], "ctx", axis=0)
        keyed_flat = jnp.concatenate([main, x_rows[1:]], axis=0).reshape(-1, width)
        enc_flat = lax.all_gather(encoder_out, "ctx", axis=0).reshape(-1, width)
        q, e = matmul(x_all, first[0]).astype(bf16), matmul(x_all, first[1]).astype(bf16)
        k, v = matmul(keyed_flat, first[2]).astype(bf16), matmul(keyed_flat, first[3]).astype(bf16)
        ck, cv = matmul(enc_flat, second[2]).astype(bf16), matmul(enc_flat, second[3]).astype(bf16)
    query_full, relative_full, key_full, value_full = first

    place = jnp.stack(peers).astype(jnp.int32)
    local = jnp.arange(half_rows, dtype=jnp.int32)

    def both_halves(start):
        return jnp.concatenate([start + local, seq_len - 1 - start - local])

    positions = both_halves(c_index * half_rows)
    key_positions = jnp.concatenate([both_halves(place[j] * half_rows) for j in range(ctx_count)])
    enc_positions = (place[:, None] * enc_rows + jnp.arange(enc_rows, dtype=jnp.int32)[None, :]).reshape(1, -1)
    levels = jnp.arange(BUCKETS + 1, dtype=jnp.int32)
    bounds = jnp.sum((rel_bucket[None, :] < levels[:, None]).astype(jnp.int32), axis=1)

    q, e = q.reshape(slab), e.reshape(lanes, slots, rows, -1)
    k, v = k.reshape(-1, slots, rows, width), v.reshape(-1, slots, rows, width)
    o, probs, own = self_forward(slot_len, bounds, positions[:, None], key_positions[None], q, e, k, v)
    o_flat = o.reshape(all_rows, width)
    if paired:
        second_near = corner_spread(second_first, 1, cuts[1], o)
        third_stack = stack_rows(lax.optimization_barrier((*third_hops, *second_near[3:]))[: steps - 1])
        third_first = first_spread(third_stack)
        (ck, cv), enc_flat, second = project(
            None, by_offset(enc_near), second_set, core_spread(second_near), second_layout, cuts[1],
            ((True, 2), (True, 3)), after(where, third_stack), steps,
        )
        output_full, cquery_full, ckey_full, cvalue_full, coutput_full, vectors = second
        normed_one, unit_one, scale_one, normed_one_low, cq, norms = query_rows(
            x_all, o_flat, output_full, cquery_full, vectors, norm_count
        )
    else:
        output_full, cquery_full, ckey_full, cvalue_full, coutput_full = second
        norms = norms.astype(f32)
        resid_one = x_all.astype(f32) + matmul(o_flat, output_full)
        normed_one, unit_one, scale_one = norm_forward(resid_one, norms[0:1], norms[1:2])
        normed_one_low = normed_one.astype(bf16)
        cq = matmul(normed_one_low, cquery_full).astype(bf16)

    enc_shape = (ctx_count, slots, enc_rows, width)
    cq, ck, cv = cq.reshape(slab), ck.reshape(enc_shape), cv.reshape(enc_shape)
    oc, cprobs = cross_forward(enc_len, enc_positions, cq, ck, cv)
    oc_flat = oc.reshape(all_rows, width)

    core = (c_index & 1).astype(jnp.int32).reshape(1)

    def reduction(pairs, sent, index, extra=None, plain=None):
        layout = layouts[index] + (((128, 1024),) if plain is not None else ())
        return Reduction(pairs, sent, layout, cuts[index], extra, plain, z_index, c_index)

    def norm_pieces(grads):
        parts = grads.reshape(norm_count, steps, 2, 4, norm_shard // 8).transpose(2, 1, 3, 0, 4)
        parts = parts.astype(bf16).reshape(2, steps * 4, norm_count, norm_shard // 8)
        parts = jnp.where(core[0] == 0, parts, parts[::-1])
        parts = jnp.pad(parts, ((0, 0), (0, 0), (0, 16 - norm_count), (0, 1024 - norm_shard // 8)))
        return parts[0], parts[1]

    row_valid = (positions[None, None, :] < slot_len[None, :, None]).astype(f32)
    row_valid = jnp.broadcast_to(row_valid, (lanes, slots, rows)).reshape(all_rows, 1)
    if paired:
        third = core_spread(corner_spread(third_first, 1, cuts[2], oc_flat))
        feed_inputs = (feed_set, third, layouts[2], cuts[2], jnp.concatenate([core, where]))
    else:
        feed_inputs = (third, (), tuple(w.shape for w in third), 0, core)
    layer_out, normed_two_low, act_low, back_pre, back_feed, back_two, back_cross, back_oc, feed_norms, *sent = (
        feed_forward_backward(
            normed_one, oc_flat, coutput_full, norms, out_grad.reshape(all_rows, width), row_valid, *feed_inputs, steps, paired
        )
    )
    if paired:
        sent_up, sent_down, sent_coutput = sent
        third_sum = reduction([(normed_two_low, [back_pre]), (act_low, [back_feed])], [sent_up, sent_down], 2)
    back_cq, back_ck, back_cv = cross_backward(cprobs, back_oc.reshape(slab), cq, ck, cv)
    back_cq = back_cq.reshape(all_rows, width)
    back_ck = back_ck.reshape(-1, width)
    back_cv = back_cv.reshape(-1, width)
    if paired:
        third_sum.fold(back_cq)
        third_sum.first_hops()
        back_cq, back_ck = after(back_cq, *third_sum.folded), after(back_ck, *third_sum.folded)
        sent_ckey, sent_cvalue = send_grads(enc_flat, (back_ck, back_cv), core, steps)
    enc_part = pair_rows(back_ck, back_cv, ckey_full, cvalue_full, ctx_count, slots * enc_rows)
    back_one, back_self, back_o, norm_grads, *sent = middle_backward(
        back_cq, cquery_full, back_two, unit_one, scale_one, norms, output_full, normed_one_low, o_flat, core, steps, paired
    )
    norm_grads = jnp.concatenate([norm_grads, feed_norms], axis=0)
    if paired:
        sent_cquery, sent_output = sent
        second_sum = reduction(
            [(o_flat, [back_self]), (normed_one_low, [back_cq]), (enc_flat, [back_ck, back_cv]), (oc_flat, [back_cross])],
            [sent_output, sent_cquery, sent_ckey, sent_cvalue, sent_coutput],
            1,
            enc_part,
            norm_pieces(norm_grads),
        )
        back_o = after(back_o, sent_ckey, *enc_part)
    self_inputs = (bounds, positions[:, None], key_positions[None], probs, own)
    part_one = self_backward(*self_inputs, back_o.reshape(slab), q, k, v, 0, 2)
    if paired:
        second_sum.fold(part_one[0])
        third_sum.second_sums(second_sum.folded[0])
        third_sum.second_hops()
        second_sum.first_hops(*third_sum.sums)
        back_o = after(back_o, second_sum.folded[0], *third_sum.sums)
    back_q, back_k, back_v, back_e = self_backward(*self_inputs, back_o.reshape(slab), q, k, v, 1, 2, part_one)
    back_q = back_q.reshape(all_rows, width)
    back_e = back_e.reshape(all_rows, -1)
    back_k = back_k.reshape(-1, width)
    back_v = back_v.reshape(-1, width)

    if paired:
        sent_keyed = send_grads(keyed_flat, (back_k, back_v), core, steps)
        third_sum.z_sums(sent_keyed[0])
        third_sum.z_hops()
        back_q = after(back_q, *third_sum.sums)
        sent_query, sent_relative = send_grads(x_all, (back_q, back_e), core, steps)
        back_k = after(back_k, *third_sum.sums)
    *main_part, other_part = pair_rows(back_k, back_v, key_full, value_full, ctx_count, slots * rows)
    if paired:
        first_sum = reduction(
            [(x_all, [back_q, back_e]), (keyed_flat, [back_k, back_v])],
            [sent_query, sent_relative, *sent_keyed],
            0,
            main_part,
        )
        first_sum.fold()
        second_sum.second_sums(first_sum.folded[0])
        second_sum.second_hops()
        first_sum.first_hops(*second_sum.sums)
        back_q = after(back_q, *second_sum.sums)
    back_x = own_rows(back_one, back_q, back_e, query_full, relative_full, other_part)

    if paired:
        third_sum.spread(back_x)
        first_sum.second_sums()
        first_sum.second_hops()
        second_sum.z_sums()
        second_sum.z_hops()
        second_sum.spread()
        first_sum.z_sums()
        first_sum.z_hops()
        first_sum.spread()
        third_grads = third_sum.grads()
        *second_grads, norm_sums = second_sum.grads()
        norm_sums = norm_sums.reshape(8, 16, 1024)[:, :norm_count, : norm_shard // 8]
        norm_grads = norm_sums.transpose(1, 0, 2).reshape(norm_count, norm_shard)
        first_grads = first_sum.grads()
        enc_sum = second_sum.extra_sum()
        main_sum = first_sum.extra_sum()
    else:
        norm_grads = lax.psum(norm_grads, ("fsdp", "ctx"))
        norm_grads = lax.dynamic_slice_in_dim(norm_grads, z_index * norm_shard, norm_shard, 1)

        def reduce(left, right):
            shard = lax.psum_scatter(outer_rows(left, right).astype(bf16), "fsdp", scatter_dimension=0, tiled=True)
            return lax.psum(shard, "ctx").astype(f32)

        def scatter(parts):
            whole = jnp.stack(parts, axis=1).reshape(ctx_count, -1, width)
            return lax.psum_scatter(whole, "ctx", scatter_dimension=0, tiled=True).astype(f32).reshape(-1, width)

        first_grads = [
            reduce(x_all, back_q), reduce(x_all, back_e), reduce(keyed_flat, back_k), reduce(keyed_flat, back_v),
        ]
        second_grads = [
            reduce(o_flat, back_self), reduce(normed_one_low, back_cq), reduce(enc_flat, back_ck),
            reduce(enc_flat, back_cv), reduce(oc_flat, back_cross),
        ]
        third_grads = [reduce(normed_two_low, back_pre), reduce(act_low, back_feed)]
        enc_sum = scatter(enc_part)
        main_sum = scatter(main_part)
    encoder_grad = enc_sum.reshape(slots, enc_rows, width)
    own_main = main_sum.shape[0]
    hidden_grad = jnp.concatenate([back_x[:own_main] + main_sum, back_x[own_main:]], axis=0)

    out_shape = hidden.shape
    return (
        layer_out.reshape(out_shape), hidden_grad.reshape(out_shape), encoder_grad,
        first_grads[0], first_grads[2], first_grads[3], first_grads[1], second_grads[0], norm_grads[0], norm_grads[1],
        second_grads[1], second_grads[2], second_grads[3], second_grads[4], norm_grads[2], norm_grads[3],
        third_grads[0], third_grads[1], norm_grads[4], norm_grads[5],
    )


def solution(mesh):
    rows = P("fsdp", None)
    vector = P("fsdp")
    slab = P(None, "fsdp", None, "ctx", None)
    encoder = P("fsdp", "ctx", None)
    weights = (rows,) * 5 + (vector,) * 2 + (rows,) * 4 + (vector,) * 2 + (rows,) * 2 + (vector,) * 2
    return jax.shard_map(
        on_device,
        mesh=mesh,
        in_specs=(slab, encoder, slab, vector, vector, P()) + weights,
        out_specs=(slab, slab, encoder) + weights,
        check_vma=False,
    )
```

```python
import functools

import jax
import jax.numpy as jnp
from jax import lax
from jax.experimental import pallas as pl
from jax.experimental.pallas import tpu as pltpu
from jax.sharding import PartitionSpec as P

HEAD_DIM = 64
BUCKETS = 32
LANE = 128
GROUP = 4
SUB = 8
eps_norm = 1e-05
neg_fill = -1e30
bf16 = jnp.bfloat16
f32 = jnp.float32
CORE, XBIT, YBIT = 1, 2, 4
VMEM_LIMIT = 63 * 1024 * 1024


def matmul(left_side, right_side):
    return jnp.dot(left_side, right_side, preferred_element_type=f32)


def matmul_back(left_side, right_side):
    return lax.dot_general(left_side, right_side, (((1,), (1,)), ((), ())), preferred_element_type=f32)


def outer_rows(left_side, right_side):
    return lax.dot_general(left_side, right_side, (((0,), (0,)), ((), ())), preferred_element_type=f32)


def norm_forward(values, gain, shift):
    row_mean = jnp.mean(values, axis=-1, keepdims=True)
    centered = values - row_mean
    scale = lax.rsqrt(jnp.mean(centered * centered, axis=-1, keepdims=True) + eps_norm)
    unit = centered * scale
    return unit * gain + shift, unit, scale


def norm_backward(unit, scale, gain, cotangent):
    back_unit = cotangent * gain
    first = jnp.mean(back_unit, axis=-1, keepdims=True)
    second = jnp.mean(back_unit * unit, axis=-1, keepdims=True)
    back = scale * (back_unit - first - unit * second)
    return back, jnp.sum(cotangent * unit, axis=0), jnp.sum(cotangent, axis=0)


def dot_nt(left_side, right_side):
    return lax.dot_general(left_side, right_side, (((1,), (1,)), ((), ())), preferred_element_type=f32)


def dot_nn(left_side, right_side):
    return lax.dot_general(left_side, right_side, (((1,), (0,)), ((), ())), preferred_element_type=f32)


def dot_tn(left_side, right_side):
    return lax.dot_general(left_side, right_side, (((0,), (0,)), ((), ())), preferred_element_type=f32)


def stack_heads(pair, low_half):
    zero = jnp.zeros_like(pair)
    return jnp.concatenate([jnp.where(low_half, pair, zero), jnp.where(low_half, zero, pair)], axis=0)


def rows_of(ref, first, last, cols):
    block = ref[first:last, 0, :, cols]
    return block.reshape(block.shape[0] * block.shape[1], block.shape[2])


def fill_one_hot(bucket_ref, one_hot_ref):
    keys = bucket_ref.shape[1]
    levels = lax.broadcasted_iota(jnp.int32, (BUCKETS, keys), 0)

    def fill(row, carry):
        line = jnp.broadcast_to(bucket_ref[pl.ds(row, 1), :], (BUCKETS, keys))
        start = pl.multiple_of(lax.rem(row, SUB) * BUCKETS, BUCKETS)
        one_hot_ref[row // SUB, pl.ds(start, BUCKETS), :] = jnp.where(line == levels, 1.0, 0.0).astype(bf16)
        return carry

    lax.fori_loop(0, bucket_ref.shape[0], fill, 0)


def fill_buckets(distance, bounds_ref, bucket_ref):
    bucket_ref[...] = jnp.zeros(distance.shape, jnp.int32)

    def fill(level, carry):
        bucket_ref[...] += (distance >= bounds_ref[level]).astype(jnp.int32)
        return carry

    lax.fori_loop(1, BUCKETS, fill, 0)


def own_block_mask(rows):
    row = lax.broadcasted_iota(jnp.int32, (rows, SUB * BUCKETS), 0)
    col = lax.broadcasted_iota(jnp.int32, (rows, SUB * BUCKETS), 1)
    return (row & (SUB - 1)) == (col // BUCKETS)


def self_forward_kernel(
    length_ref, bounds_ref, posq_ref, posk_ref, q_ref, e_ref, k_ref, v_ref, o_ref, p_ref, own_ref,
    bucket_ref, one_hot_ref, spread_ref, bias_ref,
):
    slot = pl.program_id(0)
    group = pl.program_id(1)
    lanes, _, rows, _ = q_ref.shape
    pieces = k_ref.shape[0] - (lanes - 1)
    keys = pieces * k_ref.shape[2]
    heads = bias_ref.shape[0]
    span = SUB * BUCKETS

    @pl.when((slot == 0) & (group == 0))
    def _():
        fill_buckets(posq_ref[...] - posk_ref[...], bounds_ref, bucket_ref)
        fill_one_hot(bucket_ref, one_hot_ref)

    @pl.when(group == 0)
    def _():
        keep = own_block_mask(lanes * rows)
        source = lax.broadcasted_iota(jnp.int32, (LANE, span), 0)
        target = lax.broadcasted_iota(jnp.int32, (LANE, span), 1) & (BUCKETS - 1)
        for part in range(LANE // BUCKETS):
            copy = jnp.where(source == target + part * BUCKETS, 1.0, 0.0).astype(bf16)
            for block in range(heads * BUCKETS // LANE):
                rows_e = rows_of(e_ref, 0, lanes, slice(block * LANE, (block + 1) * LANE))
                head = block * (LANE // BUCKETS) + part
                spread_ref[head] = jnp.where(keep, dot_nn(rows_e, copy), 0.0)
        distance = posq_ref[...] - posk_ref[...]
        valid = posk_ref[...] < length_ref[slot]
        fills = [jnp.where(valid & (distance >= edge), 0.0, neg_fill) for edge in (0, 1)]
        for g in range(rows // SUB):
            starts = [lane * rows + g * SUB for lane in range(lanes)]
            left = [spread_ref[:, start : start + SUB, :].reshape(heads * SUB, span) for start in starts]
            bias = dot_nn(jnp.concatenate(left, axis=0).astype(bf16), one_hot_ref[g])
            bias = bias.reshape(lanes, heads, SUB, keys)
            for lane, start in enumerate(starts):
                fill = fills[min(lane, 1)][None, g * SUB : (g + 1) * SUB, :]
                bias_ref[:, start : start + SUB, :] = bias[lane] + fill

    low_half = lax.broadcasted_iota(jnp.int32, (1, LANE), 1) < HEAD_DIM
    lane_id = lax.broadcasted_iota(jnp.int32, (1, LANE), 1)
    own_all = [jnp.zeros((rows, LANE), f32) for _ in range(lanes)]
    e_cols = pl.ds(pl.multiple_of(group * (GROUP * BUCKETS), LANE), GROUP * BUCKETS)
    tables = [None] + [e_ref[lane, 0, :, e_cols].astype(f32) for lane in range(1, lanes)]
    for pair in range(GROUP // 2):
        cols = slice(pair * LANE, (pair + 1) * LANE)
        q_pair = rows_of(q_ref, 0, lanes, cols) * jnp.asarray(HEAD_DIM**-0.5, bf16)
        k_main = rows_of(k_ref, 0, pieces, cols)
        v_main = rows_of(v_ref, 0, pieces, cols)
        scores = dot_nt(stack_heads(q_pair, low_half), k_main)
        own_pair = []
        for half in range(2):
            head = pair * 2 + half
            keep = low_half if half == 0 else jnp.logical_not(low_half)
            for lane in range(lanes):
                start = (half * lanes + lane) * rows
                part = scores[start : start + rows]
                part = part + bias_ref[group * GROUP + head, lane * rows : (lane + 1) * rows, :]
                top = jnp.max(part, axis=1, keepdims=True)
                if lane > 0:
                    q_row = q_pair[lane * rows : (lane + 1) * rows].astype(f32)
                    k_row = k_ref[pieces + lane - 1, 0, :, cols].astype(f32)
                    own = jnp.sum(jnp.where(keep, q_row * k_row, 0.0), axis=1, keepdims=True)
                    own = own + tables[lane][:, head * BUCKETS : head * BUCKETS + 1]
                    top = jnp.maximum(top, own)
                    own_exp = jnp.exp(own - top)
                terms = jnp.exp(part - top)
                total = jnp.sum(terms, axis=1, keepdims=True)
                if lane > 0:
                    total = total + own_exp
                inverse = 1.0 / total
                p_ref[0, head, lane * rows : (lane + 1) * rows, :] = (terms * inverse).astype(bf16)
                if lane > 0:
                    own_prob = own_exp * inverse
                    own_all[lane] = jnp.where(lane_id == head, own_prob, own_all[lane])
                else:
                    own_prob = jnp.zeros((rows, 1), f32)
                own_pair.append(own_prob)
        p_low = p_ref[0, pair * 2 : pair * 2 + 2].reshape(2 * lanes * rows, keys)
        mixed = dot_nn(p_low, v_main)
        for lane in range(lanes):
            first = lane * rows
            second = (lanes + lane) * rows
            out = jnp.where(low_half, mixed[first : first + rows], mixed[second : second + rows])
            if lane > 0:
                own_prob = jnp.where(low_half, own_pair[lane], own_pair[lanes + lane])
                v_row = v_ref[pieces + lane - 1, 0, :, cols].astype(f32)
                out = out + own_prob.astype(bf16).astype(f32) * v_row
            o_ref[lane, 0, :, cols] = out.astype(bf16)
    for lane in range(lanes):
        own_ref[0, 0, lane * rows : (lane + 1) * rows, :] = own_all[lane]


def self_backward_kernel(
    held, bounds_ref, posq_ref, posk_ref, p_ref, own_ref, do_ref, q_ref, k_ref, v_ref, *refs,
):
    dq_ref, dk_ref, dv_ref, de_ref = refs[held : held + 4]
    bucket_ref, one_hot_ref, turned_ref, scores_ref, down_ref, wide_ref = refs[held + 4 :]
    group = pl.program_id(1)
    lanes, _, rows, _ = q_ref.shape
    pieces = k_ref.shape[0] - (lanes - 1)
    piece_rows = k_ref.shape[2]
    keys = pieces * piece_rows
    scale = HEAD_DIM**-0.5

    heads = scores_ref.shape[0]
    span = SUB * BUCKETS

    @pl.when((pl.program_id(0) == 0) & (group == 0))
    def _():
        fill_buckets(posq_ref[...] - posk_ref[...], bounds_ref, bucket_ref)
        fill_one_hot(bucket_ref, one_hot_ref)
        for g in range(rows // SUB):
            turned_ref[g] = one_hot_ref[g].T

    lane_id = lax.broadcasted_iota(jnp.int32, (1, LANE), 1)
    low_half = lane_id < HEAD_DIM
    downs = [jnp.zeros((rows, LANE), f32) for _ in range(lanes)]
    for pair in range(GROUP // 2):
        cols = slice(pair * LANE, (pair + 1) * LANE)
        q_pair = rows_of(q_ref, 0, lanes, cols) * jnp.asarray(scale, bf16)
        do_pair = rows_of(do_ref, 0, lanes, cols)
        k_main = rows_of(k_ref, 0, pieces, cols)
        v_main = rows_of(v_ref, 0, pieces, cols)
        q_stack = stack_heads(q_pair, low_half)
        do_stack = stack_heads(do_pair, low_half)
        back_probs = dot_nt(do_stack, v_main)
        p_low = p_ref[0, pair * 2 : pair * 2 + 2].reshape(2 * lanes * rows, keys)
        probs = p_low.astype(f32)
        weighted = probs * back_probs
        delta = jnp.sum(weighted, axis=1, keepdims=True)
        down_pair = []
        delta_list = []
        for half in range(2):
            head = pair * 2 + half
            keep = low_half if half == 0 else jnp.logical_not(low_half)
            for lane in range(lanes):
                start = (half * lanes + lane) * rows
                part = delta[start : start + rows]
                if lane > 0:
                    do_row = do_pair[lane * rows : (lane + 1) * rows].astype(f32)
                    v_row = v_ref[pieces + lane - 1, 0, :, cols].astype(f32)
                    back_own = jnp.sum(jnp.where(keep, do_row * v_row, 0.0), axis=1, keepdims=True)
                    own_prob = own_ref[0, 0, lane * rows : (lane + 1) * rows, head : head + 1]
                    part = part + own_prob * back_own
                    down_pair.append((own_prob * (back_own - part)).astype(bf16).astype(f32))
                else:
                    down_pair.append(None)
                delta_list.append(part)
        delta = jnp.concatenate(delta_list, axis=0)
        back_scores = (weighted - probs * delta).astype(bf16)
        back_q = dot_nn(back_scores, k_main)
        back_k = dot_tn(q_stack, back_scores)
        back_v = dot_tn(do_stack, p_low)
        dk_ref[:pieces, 0, :, cols] = back_k.T.astype(bf16).reshape(pieces, piece_rows, LANE)
        dv_ref[:pieces, 0, :, cols] = back_v.T.astype(bf16).reshape(pieces, piece_rows, LANE)
        scores_ref[pl.ds(group * GROUP + pair * 2, 2)] = back_scores.astype(f32).reshape(2, lanes * rows, keys)
        for lane in range(lanes):
            first = lane * rows
            second = (lanes + lane) * rows
            back = jnp.where(low_half, back_q[first : first + rows], back_q[second : second + rows])
            if lane > 0:
                k_row = k_ref[pieces + lane - 1, 0, :, cols].astype(f32)
                down = jnp.where(low_half, down_pair[lane], down_pair[lanes + lane])
                back = back + down * k_row
                own_low = jnp.where(
                    low_half,
                    own_ref[0, 0, lane * rows : (lane + 1) * rows, pair * 2 : pair * 2 + 1],
                    own_ref[0, 0, lane * rows : (lane + 1) * rows, pair * 2 + 1 : pair * 2 + 2],
                )
                own_low = own_low.astype(bf16).astype(f32)
                dk_ref[pieces + lane - 1, 0, :, cols] = (
                    down * q_pair[first : first + rows].astype(f32)
                ).astype(bf16)
                dv_ref[pieces + lane - 1, 0, :, cols] = (
                    own_low * do_pair[first : first + rows].astype(f32)
                ).astype(bf16)
            dq_ref[lane, 0, :, cols] = (back * scale).astype(bf16)
            if lane > 0:
                for half in range(2):
                    spot = (pair * 2 + half) * BUCKETS
                    downs[lane] = jnp.where(lane_id == spot, down_pair[half * lanes + lane], downs[lane])
    for lane in range(1, lanes):
        down_ref[group, lane] = downs[lane]

    @pl.when(group == pl.num_programs(1) - 1)
    def _():
        keep = own_block_mask(lanes * heads * SUB)
        source = lax.broadcasted_iota(jnp.int32, (span, LANE), 0) & (BUCKETS - 1)
        target = lax.broadcasted_iota(jnp.int32, (span, LANE), 1) & (BUCKETS - 1)
        fold = jnp.where(source == target, 1.0, 0.0).astype(bf16)
        per_block = LANE // BUCKETS
        for g in range(rows // SUB):
            starts = [lane * rows + g * SUB for lane in range(lanes)]
            left = [scores_ref[:, start : start + SUB, :].reshape(heads * SUB, keys) for start in starts]
            sums = dot_nn(jnp.concatenate(left, axis=0).astype(bf16), turned_ref[g])
            embed = dot_nn(jnp.where(keep, sums, 0.0).astype(bf16), fold).reshape(lanes, heads, SUB, LANE)
            for lane in range(lanes):
                for block in range(heads // per_block):
                    out = embed[lane, block * per_block]
                    for part in range(1, per_block):
                        out = jnp.where(lane_id // BUCKETS == part, embed[lane, block * per_block + part], out)
                    if lane > 0:
                        out = out + down_ref[block, lane, g * SUB : (g + 1) * SUB, :]
                    wide_ref[lane, g * SUB : (g + 1) * SUB, block * LANE : (block + 1) * LANE] = out
        for lane in range(lanes):
            de_ref[lane, 0] = wide_ref[lane].astype(bf16)


def cross_forward_kernel(length_ref, posk_ref, q_ref, k_ref, v_ref, o_ref, p_ref):
    slot = pl.program_id(0)
    lanes, _, rows, _ = q_ref.shape
    pieces = k_ref.shape[0]
    keys = pieces * k_ref.shape[2]
    low_half = lax.broadcasted_iota(jnp.int32, (1, LANE), 1) < HEAD_DIM
    fill = jnp.where(posk_ref[...] < length_ref[slot], 0.0, neg_fill)
    count = lanes * rows
    for pair in range(GROUP // 2):
        cols = slice(pair * LANE, (pair + 1) * LANE)
        q_pair = rows_of(q_ref, 0, lanes, cols) * jnp.asarray(HEAD_DIM**-0.5, bf16)
        k_main = rows_of(k_ref, 0, pieces, cols)
        v_main = rows_of(v_ref, 0, pieces, cols)
        scores = dot_nt(stack_heads(q_pair, low_half), k_main) + fill
        top = jnp.max(scores, axis=1, keepdims=True)
        terms = jnp.exp(scores - top)
        inverse = 1.0 / jnp.sum(terms, axis=1, keepdims=True)
        p_low = (terms * inverse).astype(bf16)
        p_ref[0, pair * 2 : pair * 2 + 2] = p_low.reshape(2, count, keys)
        mixed = dot_nn(p_low, v_main)
        out = jnp.where(low_half, mixed[:count], mixed[count:]).astype(bf16)
        o_ref[:, 0, :, cols] = out.reshape(lanes, rows, LANE)


def cross_backward_kernel(p_ref, do_ref, q_ref, k_ref, v_ref, dq_ref, dk_ref, dv_ref):
    lanes, _, rows, _ = q_ref.shape
    pieces = k_ref.shape[0]
    piece_rows = k_ref.shape[2]
    keys = pieces * piece_rows
    count = lanes * rows
    scale = HEAD_DIM**-0.5
    low_half = lax.broadcasted_iota(jnp.int32, (1, LANE), 1) < HEAD_DIM
    for pair in range(GROUP // 2):
        cols = slice(pair * LANE, (pair + 1) * LANE)
        q_pair = rows_of(q_ref, 0, lanes, cols) * jnp.asarray(scale, bf16)
        do_pair = rows_of(do_ref, 0, lanes, cols)
        k_main = rows_of(k_ref, 0, pieces, cols)
        v_main = rows_of(v_ref, 0, pieces, cols)
        q_stack = stack_heads(q_pair, low_half)
        do_stack = stack_heads(do_pair, low_half)
        back_probs = dot_nt(do_stack, v_main)
        p_low = p_ref[0, pair * 2 : pair * 2 + 2].reshape(2 * count, keys)
        probs = p_low.astype(f32)
        weighted = probs * back_probs
        delta = jnp.sum(weighted, axis=1, keepdims=True)
        back_scores = (weighted - probs * delta).astype(bf16)
        back_q = dot_nn(back_scores, k_main)
        back_k = dot_tn(q_stack, back_scores)
        back_v = dot_tn(do_stack, p_low)
        dk_ref[:, 0, :, cols] = back_k.T.astype(bf16).reshape(pieces, piece_rows, LANE)
        dv_ref[:, 0, :, cols] = back_v.T.astype(bf16).reshape(pieces, piece_rows, LANE)
        back = jnp.where(low_half, back_q[:count], back_q[count:]) * scale
        dq_ref[:, 0, :, cols] = back.astype(bf16).reshape(lanes, rows, LANE)


def head_block(array, width=GROUP * HEAD_DIM):
    return pl.BlockSpec((array.shape[0], 1, array.shape[2], width), lambda s, g: (0, s, 0, g))


def slot_block(array):
    return pl.BlockSpec((array.shape[0], 1) + array.shape[2:], lambda s, g: (0, s, 0, 0))


def whole_block(array):
    return pl.BlockSpec(array.shape, lambda s, g: (0,) * array.ndim)


SMALL = pl.CostEstimate(flops=1000, bytes_accessed=1000, transcendentals=0)
SMEM_SPEC = pl.BlockSpec(memory_space=pltpu.SMEM)


def params():
    return pltpu.CompilerParams(vmem_limit_bytes=VMEM_LIMIT)


def shaped(shape, dtype):
    return jax.ShapeDtypeStruct(shape, dtype)


def self_forward(length, bounds, posq, posk, q, e, k, v):
    lanes, slots, rows, width = q.shape
    heads = width // HEAD_DIM
    keys = posk.shape[1]
    count = lanes * rows
    groups = heads // GROUP
    return pl.pallas_call(
        self_forward_kernel,
        grid=(slots, groups),
        in_specs=[
            SMEM_SPEC, SMEM_SPEC, whole_block(posq), whole_block(posk),
            head_block(q), slot_block(e), head_block(k), head_block(v),
        ],
        out_specs=[
            head_block(q),
            pl.BlockSpec((1, GROUP, count, keys), lambda s, g: (s, g, 0, 0)),
            pl.BlockSpec((1, 1, count, LANE), lambda s, g: (s, g, 0, 0)),
        ],
        out_shape=[
            shaped(q.shape, bf16),
            shaped((slots, heads, count, keys), bf16),
            shaped((slots, groups, count, LANE), f32),
        ],
        scratch_shapes=[
            pltpu.VMEM((rows, keys), jnp.int32),
            pltpu.VMEM((rows // SUB, SUB * BUCKETS, keys), bf16),
            pltpu.VMEM((heads, count, SUB * BUCKETS), f32),
            pltpu.VMEM((heads, count, keys), f32),
        ],
        compiler_params=params(),
        cost_estimate=SMALL,
        name="self_forward",
    )(length, bounds, posq, posk, q, e, k, v)


def self_backward(bounds, posq, posk, p, own, do, q, k, v, part, parts, made=()):
    lanes, slots, rows, width = q.shape
    heads = width // HEAD_DIM // parts
    keys = p.shape[3]
    count = lanes * rows
    groups = heads // GROUP
    base = part * groups

    def block(array):
        return pl.BlockSpec((array.shape[0], 1, array.shape[2], GROUP * HEAD_DIM), lambda s, g: (0, s, 0, base + g))

    inputs = [bounds, posq, posk, p, own, do, q, k, v]
    return pl.pallas_call(
        functools.partial(self_backward_kernel, len(made)),
        grid=(slots, groups),
        in_specs=[
            SMEM_SPEC, whole_block(posq), whole_block(posk),
            pl.BlockSpec((1, GROUP, count, keys), lambda s, g: (s, base + g, 0, 0)),
            pl.BlockSpec((1, 1, count, LANE), lambda s, g: (s, base + g, 0, 0)),
            block(do), block(q), block(k), block(v),
        ] + [pl.BlockSpec(memory_space=pl.ANY)] * len(made),
        out_specs=[
            block(q), block(k), block(v),
            pl.BlockSpec((lanes, 1, rows, heads * BUCKETS), lambda s, g: (0, s, 0, part)),
        ],
        out_shape=[
            shaped(q.shape, bf16), shaped(k.shape, bf16), shaped(v.shape, bf16),
            shaped((lanes, slots, rows, heads * parts * BUCKETS), bf16),
        ],
        scratch_shapes=[
            pltpu.VMEM((rows, keys), jnp.int32),
            pltpu.VMEM((rows // SUB, SUB * BUCKETS, keys), bf16),
            pltpu.VMEM((rows // SUB, keys, SUB * BUCKETS), bf16),
            pltpu.VMEM((heads, count, keys), f32),
            pltpu.VMEM((groups, lanes, rows, LANE), f32),
            pltpu.VMEM((lanes, rows, heads * BUCKETS), f32),
        ],
        input_output_aliases={len(inputs) + i: i for i in range(len(made))},
        compiler_params=params(),
        cost_estimate=SMALL,
        name="self_backward",
    )(*inputs, *made)


def cross_forward(length, posk, q, k, v):
    lanes, slots, rows, width = q.shape
    heads = width // HEAD_DIM
    keys = posk.shape[1]
    count = lanes * rows
    return pl.pallas_call(
        cross_forward_kernel,
        grid=(slots, heads // GROUP),
        in_specs=[SMEM_SPEC, whole_block(posk), head_block(q), head_block(k), head_block(v)],
        out_specs=[head_block(q), pl.BlockSpec((1, GROUP, count, keys), lambda s, g: (s, g, 0, 0))],
        out_shape=[shaped(q.shape, bf16), shaped((slots, heads, count, keys), bf16)],
        compiler_params=params(),
        cost_estimate=SMALL,
        name="cross_forward",
    )(length, posk, q, k, v)


def cross_backward(p, do, q, k, v):
    lanes, slots, rows, width = q.shape
    heads = width // HEAD_DIM
    keys = p.shape[3]
    count = lanes * rows
    return pl.pallas_call(
        cross_backward_kernel,
        grid=(slots, heads // GROUP),
        in_specs=[
            pl.BlockSpec((1, GROUP, count, keys), lambda s, g: (s, g, 0, 0)),
            head_block(do), head_block(q), head_block(k), head_block(v),
        ],
        out_specs=[head_block(q), head_block(k), head_block(v)],
        out_shape=[shaped(q.shape, bf16), shaped(k.shape, bf16), shaped(v.shape, bf16)],
        compiler_params=params(),
        cost_estimate=SMALL,
        name="cross_backward",
    )(p, do, q, k, v)


FEED_BLOCK = 512


def norm_parts(values):
    row_mean = jnp.mean(values, axis=-1, keepdims=True)
    centered = values - row_mean
    scale = lax.rsqrt(jnp.mean(centered * centered, axis=-1, keepdims=True) + eps_norm)
    return centered * scale, scale


def feed_kernel(
    sending, loading, core_ref, base_ref, mixed_ref, outer_ref, norms_ref, cot_ref, valid_ref, *refs,
):
    layout, copies, cut, parts, number_in = loading
    sources, refs = refs[:number_in], refs[number_in:]
    feed_body(sending, (layout, copies, cut, parts, sources), core_ref, base_ref, mixed_ref, outer_ref, norms_ref, cot_ref, valid_ref, *refs)


def feed_body(
    sending, loading, core_ref, base_ref, mixed_ref, outer_ref, norms_ref, cot_ref, valid_ref,
    out_ref, low_ref, act_ref, back_pre_ref, feed_ref, back_ref, cross_ref, back_mixed_ref, grads_ref, *rest,
):
    if sending:
        up_send_ref, down_send_ref, outer_send_ref, *rest = rest
    unit_ref, total_ref, turned_ref, act_all_ref, slope_ref, row_scale_ref, up_all_ref, down_all_ref, sems = rest
    phase, block = pl.program_id(0), pl.program_id(1)
    last = pl.num_programs(1) - 1
    cols = pl.ds(pl.multiple_of(block * FEED_BLOCK, FEED_BLOCK), FEED_BLOCK)

    up_ref = lambda: up_all_ref[:, cols]
    down_ref = lambda: down_all_ref[cols, :]
    layout, copies, cut, parts, sources = loading

    def loads():
        return group_loads(layout, copies, cut, parts, core_ref, sources, (up_all_ref, down_all_ref), sems, 1)

    @pl.when((phase == 0) & (block == 0))
    def _():
        for _, load in loads():
            load.start()
        unit, scale = norm_parts(base_ref[...] + dot_nn(mixed_ref[...], outer_ref[...]))
        normed = unit * norms_ref[2:3, :] + norms_ref[3:4, :]
        unit_ref[...] = unit
        row_scale_ref[...] = scale
        total_ref[...] = normed
        low_ref[...] = normed.astype(bf16)
        if sending:
            turned_ref[...] = core_columns(low_ref, 1 - core_ref[0], sending).T
        for _, load in loads():
            load.wait()

    @pl.when(phase == 0)
    def _():
        pre = dot_nn(low_ref[...], up_ref())
        below = 0.5 * (1.0 + lax.erf(pre * 0.7071067811865476))
        act = (pre * below).astype(bf16)
        slope_ref[:, cols] = below + pre * (jnp.exp(-0.5 * pre * pre) * 0.3989422804014327)
        act_all_ref[:, cols] = act
        act_ref[...] = act
        total_ref[...] += dot_nn(act, down_ref())

    @pl.when((phase == 0) & (block == last))
    def _():
        unit, scale = norm_parts(total_ref[...])
        gain = norms_ref[4:5, :]
        out_ref[...] = (unit * gain + norms_ref[5:6, :]).astype(bf16)
        cotangent = cot_ref[...].astype(f32) * valid_ref[...]
        back, gain_grad, shift_grad = norm_backward(unit, scale, gain, cotangent)
        grads_ref[2:3, :] = gain_grad[None]
        grads_ref[3:4, :] = shift_grad[None]
        total_ref[...] = back
        feed_ref[...] = back.astype(bf16)

    @pl.when(phase == 1)
    def _():
        back_act = dot_nt(feed_ref[...], down_ref())
        back_pre = (back_act * slope_ref[:, cols]).astype(bf16)
        back_pre_ref[...] = back_pre
        total_ref[...] += dot_nt(back_pre, up_ref())
        if sending:
            up_send_ref[...] = dot_nn(turned_ref[...], back_pre).astype(bf16)

            @pl.when((block & 1) == 1 - core_ref[0])
            def _():
                down_send_ref[...] = dot_tn(act_all_ref[:, cols], feed_ref[...]).astype(bf16)

    @pl.when((phase == 1) & (block == last))
    def _():
        back, gain_grad, shift_grad = norm_backward(
            unit_ref[...], row_scale_ref[...], norms_ref[2:3, :], total_ref[...]
        )
        back_ref[...] = back
        cross_ref[...] = back.astype(bf16)
        back_mixed_ref[...] = dot_nt(cross_ref[...], outer_ref[...]).astype(bf16)
        if sending:
            outer_send_ref[...] = dot_tn(core_columns(mixed_ref, 1 - core_ref[0], sending), cross_ref[...]).astype(bf16)
        grads_ref[0:1, :] = gain_grad[None]
        grads_ref[1:2, :] = shift_grad[None]


def feed_forward_backward(base, mixed, outer, norms, cot, valid, weights, arrivals, layout, cut, place, steps, sending):
    rows, width = base.shape
    hidden = layout[0][1]
    blocks = hidden // FEED_BLOCK
    copies, _ = block_copies(layout)
    sources = [*weights, *arrivals]
    parts = steps if arrivals else 1
    single = pl.Buffered(1)
    whole = lambda array: pl.BlockSpec(array.shape, lambda p, b, c: (0, 0), pipeline_mode=single)
    full = pl.BlockSpec((rows, width), lambda p, b, c: (0, 0))
    first = lambda p, b: jnp.where(p == 0, b, blocks - 1)
    second = lambda p, b: jnp.where(p == 0, 0, b)
    out_specs = [
        full, full,
        pl.BlockSpec((rows, FEED_BLOCK), lambda p, b, c: (0, first(p, b))),
        pl.BlockSpec((rows, FEED_BLOCK), lambda p, b, c: (0, second(p, b))),
        full, full, full, full,
        pl.BlockSpec((4, width), lambda p, b, c: (0, 0)),
    ]
    low = shaped((rows, width), bf16)
    wide = shaped((rows, hidden), bf16)
    out_shape = [low, low, wide, wide, low, shaped((rows, width), f32), low, low, shaped((4, width), f32)]
    if sending:
        assert hidden // (2 * steps) == FEED_BLOCK
        out_specs += [
            pl.BlockSpec((width // 2, FEED_BLOCK), lambda p, b, c: (0, second(p, b))),
            pl.BlockSpec((FEED_BLOCK, width), lambda p, b, c: (second(p, b) // 2, 0)),
            pl.BlockSpec((width // 2, width), lambda p, b, c: (0, 0)),
        ]
        out_shape += [
            shaped((width // 2, hidden), bf16), shaped((hidden // 2, width), bf16), shaped((width // 2, width), bf16),
        ]
    return pl.pallas_call(
        functools.partial(feed_kernel, steps if sending else 0, (layout, copies, cut, parts, len(sources))),
        grid_spec=pltpu.PrefetchScalarGridSpec(
            num_scalar_prefetch=1,
            grid=(2, blocks),
            in_specs=[
                whole(base), whole(mixed), whole(outer), whole(norms), whole(cot), whole(valid),
            ] + [pl.BlockSpec(memory_space=pl.ANY)] * len(sources),
            out_specs=out_specs,
            scratch_shapes=[
                pltpu.VMEM((rows, width), f32), pltpu.VMEM((rows, width), f32),
                pltpu.VMEM((width // 2, rows), bf16), pltpu.VMEM((rows, hidden), bf16), pltpu.VMEM((rows, hidden), f32),
                pltpu.VMEM((rows, 1), f32),
                pltpu.VMEM((width, hidden), bf16), pltpu.VMEM((hidden, width), bf16), pltpu.SemaphoreType.DMA((2,)),
            ],
        ),
        out_shape=out_shape,
        compiler_params=params(),
        cost_estimate=SMALL,
        name="feed",
    )(place, base, mixed, outer, norms, cot, valid, *sources)


def middle_kernel(
    sending, core_ref, back_cq_ref, query_ref, back_two_ref, unit_ref, scale_ref, norms_ref, outer_ref, *refs
):
    if sending:
        normed_ref, mixed_ref, feed_norms_ref, enc_ref, back_k_ref, back_v_ref, key_ref, value_ref, *refs = refs
        back_ref, low_ref, back_mixed_ref, grads_ref, query_send_ref, outer_send_ref, *refs = refs
        norm_keep_ref, norm_send_ref, key_send_ref, value_send_ref, even_ref, odd_ref, pieces_ref = refs
    else:
        back_ref, low_ref, back_mixed_ref, grads_ref = refs
    total = back_two_ref[...] + dot_nt(back_cq_ref[...], query_ref[...])
    back, gain_grad, shift_grad = norm_backward(unit_ref[...], scale_ref[...], norms_ref[0:1, :], total)
    back_ref[...] = back
    low_ref[...] = back.astype(bf16)
    grads_ref[0:1, :] = gain_grad[None]
    grads_ref[1:2, :] = shift_grad[None]
    back_mixed_ref[...] = dot_nt(low_ref[...], outer_ref[...]).astype(bf16)
    if sending:
        for left, right, out in ((normed_ref, back_cq_ref, query_send_ref), (mixed_ref, low_ref, outer_send_ref)):
            out[...] = dot_tn(core_columns(left, 1 - core_ref[0], sending), right[...]).astype(bf16)
        width = back.shape[1]
        pieces = pieces_ref.shape[0] // 16
        part = width // pieces
        vectors = jnp.concatenate(
            [gain_grad[None], shift_grad[None], feed_norms_ref[...], jnp.zeros((16 - 6, width), f32)], axis=0
        )
        pick_row = lax.broadcasted_iota(jnp.int32, (pieces * 16, 16), 0)
        pick_col = lax.broadcasted_iota(jnp.int32, (pieces * 16, 16), 1)
        pick = jnp.where(lax.rem(pick_row, 16) == pick_col, 1.0, 0.0).astype(bf16)
        wide = dot_nn(pick, vectors.astype(bf16))
        piece = lax.broadcasted_iota(jnp.int32, wide.shape, 0) // 16
        column = lax.broadcasted_iota(jnp.int32, wide.shape, 1) // part
        wide = jnp.where(piece == column, wide, 0.0).astype(bf16)
        copy_row = lax.broadcasted_iota(jnp.int32, (width, LANE), 0)
        copy_col = lax.broadcasted_iota(jnp.int32, (width, LANE), 1)
        copy = jnp.where(lax.rem(copy_row, part) == copy_col, 1.0, 0.0).astype(bf16)
        pieces_ref[...] = dot_nn(wide, copy).astype(bf16)
        norm_keep_ref[...] = jnp.zeros(norm_keep_ref.shape, bf16)
        norm_send_ref[...] = jnp.zeros(norm_send_ref.shape, bf16)
        size = pieces * 16 // (2 * sending)
        for step in range(sending):
            for out, which in ((norm_keep_ref, core_ref[0]), (norm_send_ref, 1 - core_ref[0])):
                start = pl.multiple_of((2 * step + which) * size, size)
                out[step * size : (step + 1) * size, :LANE] = pieces_ref[pl.ds(start, size), :]
        columns = core_columns(enc_ref, 1 - core_ref[0], sending)
        key_send_ref[...] = dot_tn(columns, back_k_ref[...]).astype(bf16)
        value_send_ref[...] = dot_tn(columns, back_v_ref[...]).astype(bf16)
        pair_tiles(back_k_ref, back_v_ref, key_ref, value_ref, even_ref, odd_ref)


def pair_tiles(back_k_ref, back_v_ref, key_ref, value_ref, even_ref, odd_ref):
    half = even_ref.shape[1]

    def fill(tile, carry):
        rows = pl.ds(pl.multiple_of(tile * 2 * half, 2 * half), 2 * half)
        total = dot_nt(back_k_ref[rows, :], key_ref[...]) + dot_nt(back_v_ref[rows, :], value_ref[...])
        even_ref[tile] = total[:half].astype(bf16)
        odd_ref[tile] = total[half:].astype(bf16)
        return carry

    lax.fori_loop(0, even_ref.shape[0], fill, 0)


def middle_backward(
    back_cq, query, back_two, unit, scale, norms, outer, core, steps, sending=()
):
    rows, width = back_two.shape
    low = shaped((rows, width), bf16)
    out_shape = [shaped((rows, width), f32), low, low, shaped((2, width), f32)]
    inputs = [back_cq, query, back_two, unit, scale, norms, outer]
    if sending:
        half = shaped((width // 2, width), bf16)
        pair = shaped((4, sending[3].shape[0] // 8, width), bf16)
        out_shape += [half, half] + [shaped((16 * 4 * steps, width), bf16)] * 2 + [half, half, pair, pair]
        inputs += sending
    vmem = pl.BlockSpec(memory_space=pltpu.VMEM)
    return pl.pallas_call(
        functools.partial(middle_kernel, steps if sending else 0),
        in_specs=[SMEM_SPEC] + [vmem] * len(inputs),
        out_specs=[vmem] * len(out_shape),
        out_shape=out_shape,
        scratch_shapes=[pltpu.VMEM((16 * 8 * steps, LANE), bf16)] if sending else [],
        compiler_params=params(),
        cost_estimate=SMALL,
        name="middle_backward",
    )(core, *inputs)


def pair_rows_kernel(tiles, back_k_ref, back_v_ref, key_ref, value_ref, even_ref, odd_ref, *rest):
    total = dot_nt(back_k_ref[...], key_ref[...]) + dot_nt(back_v_ref[...], value_ref[...])
    half = even_ref.shape[1]
    step = pl.program_id(0)

    @pl.when(step < tiles)
    def _():
        even_ref[0] = total[:half].astype(bf16)
        odd_ref[0] = total[half:].astype(bf16)

    if rest:

        @pl.when(step >= tiles)
        def _():
            rest[0][...] = total


def pair_rows(back_k, back_v, key, value, pieces, piece_rows):
    count, width = back_k.shape[0], key.shape[0]
    tile = 2 * piece_rows
    tiles = pieces // 2
    steps = count // tile
    resident = lambda array: pl.BlockSpec(array.shape, lambda t: (0, 0), pipeline_mode=pl.Buffered(1))
    rows = pl.BlockSpec((tile, back_k.shape[1]), lambda t: (t, 0))
    part = pl.BlockSpec((1, piece_rows, width), lambda t: (jnp.minimum(t, tiles - 1), 0, 0))
    out_specs, out_shape = [part, part], [shaped((tiles, piece_rows, width), bf16)] * 2
    if steps > tiles:
        out_specs.append(pl.BlockSpec((tile, width), lambda t: (jnp.maximum(t - tiles, 0), 0)))
        out_shape.append(shaped((count - tiles * tile, width), f32))
    return pl.pallas_call(
        functools.partial(pair_rows_kernel, tiles),
        grid=(steps,),
        in_specs=[rows, rows, resident(key), resident(value)],
        out_specs=out_specs,
        out_shape=out_shape,
        compiler_params=params(),
        cost_estimate=SMALL,
        name="pair_rows",
    )(back_k, back_v, key, value)


def last_kernel(
    steps, core_ref, x_ref, keyed_ref, back_ref, back_q_ref, back_e_ref, back_k_ref, back_v_ref,
    query_ref, relative_ref, key_ref, value_ref,
    key_send_ref, value_send_ref, query_send_ref, embed_send_ref, even_ref, odd_ref, out_ref,
):
    columns = core_columns(keyed_ref, 1 - core_ref[0], steps)
    key_send_ref[...] = dot_tn(columns, back_k_ref[...]).astype(bf16)
    value_send_ref[...] = dot_tn(columns, back_v_ref[...]).astype(bf16)
    columns = core_columns(x_ref, 1 - core_ref[0], steps)
    query_send_ref[...] = dot_tn(columns, back_q_ref[...]).astype(bf16)
    embed_send_ref[...] = dot_tn(columns, back_e_ref[...]).astype(bf16)
    pair_tiles(back_k_ref, back_v_ref, key_ref, value_ref, even_ref, odd_ref)
    main = even_ref.shape[0] * 2 * even_ref.shape[1]
    skip = out_ref.shape[0] - (back_k_ref.shape[0] - main)
    total = back_ref[...] + dot_nt(back_q_ref[...], query_ref[...]) + dot_nt(back_e_ref[...], relative_ref[...])
    out_ref[:skip, :] = total[:skip]
    lanes = dot_nt(back_k_ref[main:, :], key_ref[...]) + dot_nt(back_v_ref[main:, :], value_ref[...])
    out_ref[skip:, :] = total[skip:] + lanes


def last_backward(x, keyed, back, back_q, back_e, back_k, back_v, query, relative, key, value, core, steps, pieces):
    width = x.shape[1]
    half = shaped((width // 2, width), bf16)
    pair = shaped((pieces // 2, x.shape[0] // 3, width), bf16)
    out_shape = [half, half, half, shaped((width // 2, back_e.shape[1]), bf16), pair, pair, shaped(back.shape, f32)]
    vmem = pl.BlockSpec(memory_space=pltpu.VMEM)
    return pl.pallas_call(
        functools.partial(last_kernel, steps),
        in_specs=[SMEM_SPEC] + [vmem] * 11,
        out_specs=[vmem] * len(out_shape),
        out_shape=out_shape,
        compiler_params=params(),
        cost_estimate=SMALL,
        name="last_backward",
    )(core, x, keyed, back, back_q, back_e, back_k, back_v, query, relative, key, value)


def after(value, *others):
    return lax.optimization_barrier((value,) + others)[0]


def tie(*values):
    return lax.optimization_barrier(values)


def ctx_hop(array, bit):
    size = lax.axis_size("ctx")
    return lax.ppermute(array, "ctx", [(i, i ^ bit) for i in range(size)])


def z_hop(array, step):
    size = lax.axis_size("fsdp")
    return lax.ppermute(array, "fsdp", [(i, (i + step) % size) for i in range(size)])


def first_spread(array):
    return array, ctx_hop(array, XBIT), ctx_hop(array, YBIT)


def corner_spread(firsts, axis, cut, *held):
    array, from_x, from_y = firsts
    if held:
        from_x, from_y, *_ = lax.optimization_barrier((from_x, from_y, *held))
    size = array.shape[axis]
    corner_one = ctx_hop(lax.slice_in_dim(from_y, 0, cut, axis=axis), XBIT)
    corner_two = ctx_hop(lax.slice_in_dim(from_x, cut, size, axis=axis), YBIT)
    return [array, from_x, from_y, corner_one, corner_two]


SPREAD_PLAN = tuple(
    (offset + core, part) for core in (0, 1) for offset, part in ((0, 0), (XBIT, 0), (YBIT, 0), (XBIT + YBIT, 1), (XBIT + YBIT, 2))
)


def piece_number(index):
    return (index & 1) * 4 + (index >> 1)


def block_copies(layout):
    copies = []
    row = 0
    for number, (shard_rows, columns) in enumerate(layout):
        piece_rows = shard_rows // 8
        if columns >= 1024:
            for block in range(columns // 1024):
                copies.append((row, piece_rows, 0, 1024, number, 0, block * 1024))
                row += piece_rows
        else:
            parts = 1024 // columns
            rows = piece_rows // parts
            for part in range(parts):
                copies.append((row, rows, part * columns, columns, number, part * rows, 0))
            row += rows
    return tuple(copies), row


def place_copies(copies, cut):
    def chosen(part):
        if part == 0:
            return copies
        if part == 1:
            return tuple(item for item in copies if item[0] < cut)
        return tuple((item[0] - cut,) + item[1:] for item in copies if item[0] >= cut)

    return chosen


def group_loads(layout, copies, cut, steps, place_ref, sources, stages, sems, base=0):
    count = len(layout)
    chosen = place_copies(copies, cut)
    loads = []
    for number, (shard_rows, _) in enumerate(layout):
        target = stages[number]
        if steps > 1:
            start = pl.multiple_of(place_ref[base] * shard_rows, shard_rows)
            target = target.at[pl.ds(start, shard_rows), :]
        loads.append((number, pltpu.make_async_copy(sources[number], target, sems.at[number])))
    for arrival, (offset, part) in zip(sources[count:], SPREAD_PLAN):
        for step in range(1, steps):
            for row, rows, col, cols, number, prow, wcol in chosen(part):
                shard_rows = layout[number][0]
                start = place_ref[base + step] * shard_rows
                start = start + place_ref[base + steps + offset] * (shard_rows // 8) + prow
                source = arrival.at[step - 1, pl.ds(row, rows), pl.ds(col, cols)]
                target = stages[number].at[pl.ds(pl.multiple_of(start, 16), rows), pl.ds(wcol, cols)]
                loads.append((number, pltpu.make_async_copy(source, target, sems.at[number])))
    return loads


def place_of(z_index, c_index, steps):
    return jnp.stack(
        [(z_index - step) % steps for step in range(steps)] + [piece_number(c_index ^ j) for j in range(8)]
    ).astype(jnp.int32)


def project_kernel(layout, copies, cut, steps, products, pieces, tail, place_ref, *refs):
    count = len(layout)
    number_in = count + len(SPREAD_PLAN)
    own_ref, refs = (refs[0], refs[1:]) if tail else (None, refs)
    parts, sources, refs = refs[:pieces], refs[pieces : pieces + number_in], refs[pieces + number_in :]
    outs, refs = refs[: len(products)], refs[len(products) :]
    rows_out, weights_out, refs = refs[0], refs[1 : 1 + count], refs[1 + count :]
    rows_ref, stages, sems, row_sem, out_sem = refs[0], refs[1 : 1 + count], refs[-3], refs[-2], refs[-1]
    step = pl.program_id(0)
    piece_rows = parts[0].shape[0]

    def stores():
        moves = [pltpu.make_async_copy(rows_ref, rows_out, out_sem.at[count])]
        return moves + [pltpu.make_async_copy(stages[i], weights_out[i], out_sem.at[i]) for i in range(count)]

    @pl.when(step == 0)
    def _():
        loads = [
            pltpu.make_async_copy(part, rows_ref.at[pl.ds(j * piece_rows, piece_rows), :], row_sem)
            for j, part in enumerate(parts)
        ]
        loads += [load for _, load in group_loads(layout, copies, cut, steps, place_ref, sources, stages, sems)]
        for load in loads:
            load.start()
        if tail:
            rows_ref[pieces * piece_rows :, :] = own_ref[piece_rows:, :]
        for load in loads:
            load.wait()
        for move in stores():
            move.start()

    for out, (from_rows, number) in zip(outs, products):
        block = out.shape[1]
        cols = pl.ds(pl.multiple_of(step * block, LANE), block)
        left = rows_ref[...] if from_rows else own_ref[...]
        out[...] = dot_nn(left, stages[number][:, cols]).astype(bf16)

    @pl.when(step == pl.num_programs(0) - 1)
    def _():
        for move in stores():
            move.wait()


def project(own, parts, weights, arrivals, layout, cut, products, place, steps):
    copies, _ = block_copies(layout)
    count = len(layout)
    piece_rows, width = parts[0].shape
    rows = piece_rows * len(parts) + (own.shape[0] - piece_rows if own is not None else 0)
    blocks = 4
    hbm = pl.BlockSpec(memory_space=pl.ANY)
    first = [] if own is None else [own]
    shapes = [(shard_rows * steps, columns) for shard_rows, columns in layout]
    out_shape, out_specs = [], []
    for from_rows, number in products:
        left_rows = rows if from_rows else own.shape[0]
        out_shape.append(shaped((left_rows, shapes[number][1]), bf16))
        out_specs.append(pl.BlockSpec((left_rows, shapes[number][1] // blocks), lambda t: (0, t)))
    out_shape += [shaped((rows, width), bf16)] + [shaped(item, bf16) for item in shapes]
    outs = pl.pallas_call(
        functools.partial(project_kernel, layout, copies, cut, steps, products, len(parts), own is not None),
        grid=(blocks,),
        in_specs=[SMEM_SPEC]
        + [pl.BlockSpec(item.shape, lambda t: (0, 0), pipeline_mode=pl.Buffered(1)) for item in first]
        + [hbm] * (len(parts) + len(weights) + len(arrivals)),
        out_specs=out_specs + [hbm] * (1 + count),
        out_shape=out_shape,
        scratch_shapes=[pltpu.VMEM((rows, width), bf16)]
        + [pltpu.VMEM(item, bf16) for item in shapes]
        + [pltpu.SemaphoreType.DMA((count,)), pltpu.SemaphoreType.DMA, pltpu.SemaphoreType.DMA((count + 1,))],
        compiler_params=params(),
        cost_estimate=SMALL,
        name="project",
    )(place, *first, *parts, *weights, *arrivals)
    return outs[: len(products)], outs[len(products)], outs[len(products) + 1 :]


def query_kernel(norm_count, x_ref, mixed_ref, outer_ref, query_ref, vectors_ref, total_ref, unit_ref, scale_ref, low_ref, out_ref, norms_ref):
    pieces = vectors_ref.shape[0] // 16
    width = x_ref.shape[1]
    part = width // pieces
    copy_row = lax.broadcasted_iota(jnp.int32, (LANE, width), 0)
    copy_col = lax.broadcasted_iota(jnp.int32, (LANE, width), 1)
    copy = jnp.where(copy_row == lax.rem(copy_col, part), 1.0, 0.0).astype(bf16)
    wide = dot_nn(vectors_ref[...], copy)
    piece = lax.broadcasted_iota(jnp.int32, wide.shape, 0) // 16
    column = lax.broadcasted_iota(jnp.int32, wide.shape, 1) // part
    wide = jnp.where(piece == column, wide, 0.0).astype(bf16)
    pick_row = lax.broadcasted_iota(jnp.int32, (16, pieces * 16), 0)
    pick_col = lax.broadcasted_iota(jnp.int32, (16, pieces * 16), 1)
    pick = jnp.where(pick_row == lax.rem(pick_col, 16), 1.0, 0.0).astype(bf16)
    norms_ref[...] = dot_nn(pick, wide)
    unit, scale = norm_parts(x_ref[...].astype(f32) + dot_nn(mixed_ref[...], outer_ref[...]))
    total = unit * norms_ref[0:1, :] + norms_ref[1:2, :]
    unit_ref[...] = unit
    scale_ref[...] = scale
    total_ref[...] = total
    low_ref[...] = total.astype(bf16)
    out_ref[...] = dot_nn(low_ref[...], query_ref[...]).astype(bf16)


def query_rows(x, mixed, outer, query, vectors, norm_count):
    rows, width = x.shape
    full = lambda array: pl.BlockSpec(array.shape, lambda t: (0, 0))
    wide, low = shaped((rows, width), f32), shaped((rows, width), bf16)
    outs = [wide, wide, shaped((rows, 1), f32), low, low, shaped((16, width), f32)]
    return pl.pallas_call(
        functools.partial(query_kernel, norm_count),
        grid=(1,),
        in_specs=[full(x), full(mixed), full(outer), full(query), pl.BlockSpec((vectors.shape[0], LANE), lambda t: (0, 0))],
        out_specs=[full(item) for item in outs],
        out_shape=outs,
        compiler_params=params(),
        cost_estimate=SMALL,
        name="query_rows",
    )(x, mixed, outer, query, vectors)


def pieces_kernel(layouts, plans, place_ref, *refs):
    count = sum(len(layout) for layout in layouts)
    weights, outs, sem = refs[:count], refs[count:-1], refs[-1]
    moves = []
    first = 0
    for layout, copies, out in zip(layouts, plans, outs):
        for row, rows, col, cols, number, prow, wcol in copies:
            start = pl.multiple_of(place_ref[0] * (layout[number][0] // 8) + prow, 16)
            source = weights[first + number].at[pl.ds(start, rows), pl.ds(wcol, cols)]
            moves.append(pltpu.make_async_copy(source, out.at[pl.ds(row, rows), pl.ds(col, cols)], sem))
        first += len(layout)
    for move in moves:
        move.start()
    for move in moves:
        move.wait()


def own_pieces(groups, layouts, c_index):
    plans = [block_copies(layout) for layout in layouts]
    weights = [w for group in groups for w in group]
    return pl.pallas_call(
        functools.partial(pieces_kernel, layouts, [plan[0] for plan in plans]),
        in_specs=[SMEM_SPEC] + [pl.BlockSpec(memory_space=pl.ANY)] * len(weights),
        out_specs=[pl.BlockSpec(memory_space=pltpu.VMEM)] * len(groups),
        out_shape=[shaped((plan[1], 1024), bf16) for plan in plans],
        scratch_shapes=[pltpu.SemaphoreType.DMA],
        compiler_params=params(),
        cost_estimate=SMALL,
        name="own_pieces",
    )(piece_number(c_index).astype(jnp.int32).reshape(1), *weights)


def stack_kernel(count, *refs):
    out, sem = refs[count], refs[count + 1]
    moves = [pltpu.make_async_copy(refs[i], out.at[i], sem) for i in range(count)]
    for move in moves:
        move.start()
    for move in moves:
        move.wait()


def stack_rows(items):
    return pl.pallas_call(
        functools.partial(stack_kernel, len(items)),
        in_specs=[pl.BlockSpec(memory_space=pl.ANY)] * len(items),
        out_specs=pl.BlockSpec(memory_space=pltpu.VMEM),
        out_shape=shaped((len(items),) + items[0].shape, items[0].dtype),
        scratch_shapes=[pltpu.SemaphoreType.DMA],
        compiler_params=params(),
        cost_estimate=SMALL,
        name="stack_rows",
    )(*items)


def z_spread(mine):
    return [z_hop(mine, step) for step in range(1, lax.axis_size("fsdp"))]


def core_columns(ref, which, steps):
    block = ref.shape[1] // (2 * steps)
    parts = [ref[:, pl.ds(pl.multiple_of((2 * step + which) * block, block), block)] for step in range(steps)]
    return jnp.concatenate(parts, axis=1)


def fold_grads_kernel(groups, steps, extra_rows, plain_rows, place_ref, *refs):
    count = len(groups)
    half = steps // 2
    lefts, refs = refs[: max(groups) + 1], refs[max(groups) + 1 :]
    rights, arrivals, refs = refs[:count], refs[count : 2 * count], refs[2 * count :]
    if extra_rows:
        extra_keep, extra_got, refs = refs[0], refs[1], refs[2:]
    if plain_rows:
        plain_keep, plain_got, refs = refs[0], refs[1], refs[2:]
    outs, work = refs[:8], refs[8:]
    step = pl.program_id(0)

    for number, group in enumerate(groups):
        work[number][...] = dot_tn(lefts[group][...], rights[number][...])
    for first_x in (True, False):

        @pl.when((step < half) if first_x else (step >= half))
        def _(first_x=first_x):
            some = outs[:4] if first_x else outs[4:]
            for offset in range(4):
                y_bit, x_bit = offset >> 1, offset & 1
                on, other = (x_bit, y_bit) if first_x else (y_bit, x_bit)
                out = some[2 * (1 - on) + other]
                yx = place_ref[1] ^ offset
                row = extra_rows
                if extra_rows:
                    total = extra_keep[offset, 0].astype(f32) + extra_got[offset, 0].astype(f32)
                    out[0, :extra_rows, :] = total.astype(bf16)
                for number in range(count):
                    piece, columns = arrivals[number].shape[1:]
                    total = work[number][pl.ds(pl.multiple_of(yx * piece, piece), piece), :]
                    total = (total + arrivals[number][yx].astype(f32)).astype(bf16)
                    if columns >= 1024:
                        for block in range(columns // 1024):
                            out[0, row : row + piece, :] = total[:, block * 1024 : (block + 1) * 1024]
                            row += piece
                    else:
                        parts = 1024 // columns
                        low = piece // parts
                        for part in range(parts):
                            out[0, row : row + low, part * columns : (part + 1) * columns] = total[
                                part * low : (part + 1) * low
                            ]
                        row += low
                if plain_rows:
                    total = plain_keep[yx].astype(f32) + plain_got[yx].astype(f32)
                    out[0, row : row + plain_rows, :] = total.astype(bf16)


def fold_grads(pairs, arrivals, extra, plain, place, steps):
    half = steps // 2
    lefts = [left for left, _ in pairs]
    groups = [number for number, (_, rights) in enumerate(pairs) for _ in rights]
    rights = [right for _, some in pairs for right in some]

    def around(t, p):
        return lax.rem(p[0] + t, steps)

    def resident(array):
        return pl.BlockSpec(array.shape, lambda t, p: (0, 0), pipeline_mode=pl.Buffered(1))

    def by_z(array):
        return pl.BlockSpec((4,) + array.shape[1:], lambda t, p: (around(t, p), 0, 0))

    in_specs = [
        pl.BlockSpec((left.shape[0], left.shape[1] // (2 * steps)), lambda t, p: (0, 2 * around(t, p) + p[2]))
        for left in lefts
    ]
    in_specs += [resident(item) for item in rights] + [by_z(item) for item in arrivals]
    total_rows = sum(item.shape[1] * item.shape[2] // 1024 for item in arrivals)
    extra_rows = plain_rows = 0
    if extra is not None:
        extra_rows = extra[0].shape[2]
        in_specs += [pl.BlockSpec((4, 1, extra_rows, 1024), lambda t, p: (0, t, 0, 0))] * 2
    if plain is not None:
        plain_rows = plain[0].shape[1]
        in_specs += [by_z(item) for item in plain]
    total_rows += extra_rows + plain_rows
    a_spec = pl.BlockSpec((1, total_rows, 1024), lambda t, p: (jnp.minimum(t, half - 1), 0, 0))
    b_spec = pl.BlockSpec((1, total_rows, 1024), lambda t, p: (jnp.maximum(t - half, 0), 0, 0))
    return pl.pallas_call(
        functools.partial(fold_grads_kernel, groups, steps, extra_rows, plain_rows),
        grid_spec=pltpu.PrefetchScalarGridSpec(
            num_scalar_prefetch=1,
            grid=(steps,),
            in_specs=in_specs,
            out_specs=[a_spec] * 4 + [b_spec] * 4,
            scratch_shapes=[
                pltpu.VMEM((lefts[group].shape[1] // (2 * steps), right.shape[1]), f32)
                for group, right in zip(groups, rights)
            ],
        ),
        out_shape=[shaped((half, total_rows, 1024), bf16)] * 8,
        compiler_params=params(),
        cost_estimate=SMALL,
        name="fold_grads",
    )(place, *lefts, *rights, *arrivals, *(extra or ()), *(plain or ()))


def unpack_kernel(layout, copies, cut, place_ref, *refs):
    arrivals = refs[: len(SPREAD_PLAN)]
    outs = refs[len(SPREAD_PLAN) :]
    chosen = place_copies(copies, cut)
    for arrival, (offset, part) in zip(arrivals, SPREAD_PLAN):
        for row, rows, col, cols, number, prow, wcol in chosen(part):
            piece_rows = layout[number][0] // 8
            start = pl.multiple_of(place_ref[offset] * piece_rows + prow, 8)
            outs[number][pl.ds(start, rows), wcol : wcol + cols] = arrival[row : row + rows, col : col + cols].astype(f32)


def add_low(a, b):
    return (a.astype(f32) + b.astype(f32)).astype(bf16)


class Reduction:
    def __init__(self, pairs, layout, cut, z_index, c_index):
        self.pairs, self.layout, self.cut, self.c_index = pairs, layout, cut, c_index
        self.steps = lax.axis_size("fsdp")
        self.half = self.steps // 2
        self.copies, self.rows = block_copies(layout)
        self.place = jnp.stack([z_index, c_index >> 1, c_index & 1]).astype(jnp.int32)

    def fold(self, arrivals, extra, plain, *held):
        steps = self.steps
        arrivals = [a.reshape(steps * 4, rows // 8, columns) for a, (rows, columns) in zip(arrivals, self.layout)]
        self.lead = 0
        if extra is not None:
            self.lead = extra[0].shape[1] // steps
            extra = [item.reshape(4, steps, self.lead, 1024) for item in extra]
        place = after(self.place, *held)
        self.folded = list(fold_grads(self.pairs, arrivals, extra, plain, place, steps))

    def first_hops(self, part):
        return ctx_hop(self.folded[part], XBIT), ctx_hop(self.folded[4 + part], YBIT)

    def second_sums(self, got_x, got_y):
        self.sums = add_low(self.folded[3], got_x), add_low(self.folded[7], got_y)

    def second_hops(self):
        return ctx_hop(self.sums[0], YBIT), ctx_hop(self.sums[1], XBIT)

    def z_sums(self, got_x, got_y, late_x, late_y):
        done = []
        for keep, got, late in ((self.folded[2], got_x, late_x), (self.folded[6], got_y, late_y)):
            for kk in range(self.half):
                done.append(keep[kk].astype(f32) + got[kk].astype(f32) + late[kk].astype(f32))
        self.extra = [item[: self.lead] for item in done]
        self.terms = [item[self.lead :] for item in done]
        self.total = self.terms[-1].astype(bf16)

    def z_step(self, step, got=None):
        if got is not None:
            self.total = (self.terms[self.steps - step].astype(f32) + got.astype(f32)).astype(bf16)
        return z_hop(self.total, 1)

    def z_end(self, got):
        self.total = (self.terms[0] + got.astype(f32)).astype(bf16)

    def spread(self):
        self.near = list(first_spread(self.total))
        return self.near[1:]

    def corners(self, from_x, from_y):
        self.near = corner_spread([self.near[0], from_x, from_y], 0, self.cut)
        return self.near[3:]

    def grads(self, arrivals):
        place = jnp.stack([piece_number(self.c_index ^ j) for j in range(8)]).astype(jnp.int32)
        vmem = pl.BlockSpec(memory_space=pltpu.VMEM)
        return pl.pallas_call(
            functools.partial(unpack_kernel, self.layout, self.copies, self.cut),
            in_specs=[SMEM_SPEC] + [vmem] * len(arrivals),
            out_specs=[vmem] * len(self.layout),
            out_shape=[shaped((rows, columns), f32) for rows, columns in self.layout],
            compiler_params=params(),
            cost_estimate=SMALL,
            name="unpack",
        )(place, *arrivals)

    def extra_sum(self):
        return jnp.concatenate(self.extra, axis=0)


def on_device(
    hidden, encoder_out, out_grad, slot_len, enc_len, rel_bucket,
    query_weight, key_weight, value_weight, relative_weight, output_weight, self_norm_gain, self_norm_shift,
    cross_query_weight, cross_key_weight, cross_value_weight, cross_output_weight, cross_norm_gain,
    cross_norm_shift, up_weight, down_weight, feed_norm_gain, feed_norm_shift,
):
    lanes, slots, halves, half_rows, width = hidden.shape
    rows = halves * half_rows
    enc_rows = encoder_out.shape[1]
    ctx_count = lax.axis_size("ctx")
    steps = lax.axis_size("fsdp")
    z_index = lax.axis_index("fsdp")
    c_index = lax.axis_index("ctx")
    seq_len = ctx_count * rows
    all_rows = lanes * slots * rows
    slab = (lanes, slots, rows, width)
    paired = ctx_count == 8 and steps % 2 == 0 and query_weight.shape[0] % 256 == 0 and width == 1024
    paired = paired and enc_rows == rows

    norms = jnp.stack(
        [self_norm_gain, self_norm_shift, cross_norm_gain, cross_norm_shift, feed_norm_gain, feed_norm_shift]
    )
    norm_count, norm_shard = norms.shape

    self_set = (query_weight, relative_weight, key_weight, value_weight)
    cross_set = (output_weight, cross_query_weight, cross_key_weight, cross_value_weight, cross_output_weight)
    feed_set = (up_weight, down_weight)
    layouts = [tuple(w.shape for w in group) for group in (self_set, cross_set, feed_set)]
    x_all = hidden.reshape(all_rows, width)
    x_rows = hidden.reshape(slab)
    if paired:
        cuts = (48, 96, 128)
        where = place_of(z_index, c_index, steps)
        main, enc = x_all[: slots * rows], encoder_out.reshape(slots * rows, width)
        (piece,) = own_pieces((self_set,), layouts[:1], c_index)
        ring = [z_hop(piece, 1)]
        main_x, enc_x = ctx_hop(main, XBIT), ctx_hop(enc, XBIT)
        main_y, enc_y = ctx_hop(main, YBIT), ctx_hop(enc, YBIT)
        vectors = norms.reshape(norm_count, 8, norm_shard // 8).transpose(1, 0, 2)
        vectors = jnp.pad(vectors, ((0, 0), (0, 16 - norm_count), (0, 1024 - norm_shard // 8))).reshape(128, 1024)
        second_set = (*cross_set, vectors)
        second_layout = layouts[1] + (vectors.shape,)
        second_piece, feed_piece = own_pieces((second_set, feed_set), (second_layout, layouts[2]), c_index)
        held, main_x, main_y, enc_x, enc_y = tie(ring[0], main_x, main_y, enc_x, enc_y)
        ring.append(z_hop(held, 1))
        main_corner, enc_corner = ctx_hop(main_y, XBIT), ctx_hop(enc_x, YBIT)
        main_far, enc_far = [ctx_hop(main, CORE)], [ctx_hop(enc, CORE)]
        held, main_corner, enc_corner, main_far[0], enc_far[0] = tie(
            ring[1], main_corner, enc_corner, main_far[0], enc_far[0]
        )
        ring.append(z_hop(held, 1))
        main_far += [ctx_hop(main_x, CORE), ctx_hop(main_y, CORE)]
        enc_far += [ctx_hop(enc_x, CORE), ctx_hop(enc_y, CORE)]
        last, main_far[1], main_far[2], enc_far[1], enc_far[2] = tie(
            ring[2], main_far[1], main_far[2], enc_far[1], enc_far[2]
        )
        first_stack = stack_rows([*ring[:2], last])
        main_far.append(ctx_hop(main_corner, CORE))
        enc_far.append(ctx_hop(enc_corner, CORE))
        main_parts = [item for pair in zip([main, main_x, main_y, main_corner], main_far) for item in pair]
        enc_parts = [item for pair in zip([enc, enc_x, enc_y, enc_corner], enc_far) for item in pair]

        ring = [z_hop(after(second_piece, first_stack), 1)]
        near = list(first_spread(first_stack))
        held, near[1], near[2], main_parts[7], enc_parts[7] = tie(ring[0], near[1], near[2], main_parts[7], enc_parts[7])
        ring.append(z_hop(held, 1))
        near = corner_spread(near, 1, cuts[0])
        far = [ctx_hop(near[0], CORE), ctx_hop(near[1], CORE)]
        held, *near[2:], far[0], far[1] = tie(ring[1], *near[2:], far[0], far[1])
        ring.append(z_hop(held, 1))
        far += [ctx_hop(item, CORE) for item in near[2:]]
        (q, e, k, v), keyed_flat, first = project(
            x_all, main_parts, self_set, near + far, layouts[0], cuts[0],
            ((False, 0), (False, 1), (True, 2), (True, 3)), where, steps,
        )
        second_stack = stack_rows(tie(*ring, q)[: steps - 1])
        second_near = list(first_spread(second_stack))
        feed_hops = [z_hop(after(feed_piece, second_stack), step) for step in range(1, steps - 1)]
        k = after(k, second_stack)
        peers = [c_index ^ j for j in range(8)]
    else:
        norms = lax.all_gather(norms, "fsdp", axis=1, tiled=True)
        gather = lambda w: lax.all_gather(w, "fsdp", axis=0, tiled=True)
        first, second, third = [[gather(w) for w in group] for group in (self_set, cross_set, feed_set)]
        peers = [jnp.int32(j) for j in range(ctx_count)]
        main = lax.all_gather(x_rows[0], "ctx", axis=0)
        keyed_flat = jnp.concatenate([main, x_rows[1:]], axis=0).reshape(-1, width)
        enc_flat = lax.all_gather(encoder_out, "ctx", axis=0).reshape(-1, width)
        q, e = matmul(x_all, first[0]).astype(bf16), matmul(x_all, first[1]).astype(bf16)
        k, v = matmul(keyed_flat, first[2]).astype(bf16), matmul(keyed_flat, first[3]).astype(bf16)
        ck, cv = matmul(enc_flat, second[2]).astype(bf16), matmul(enc_flat, second[3]).astype(bf16)
    query_full, relative_full, key_full, value_full = first

    place = jnp.stack(peers).astype(jnp.int32)
    local = jnp.arange(half_rows, dtype=jnp.int32)

    def both_halves(start):
        return jnp.concatenate([start + local, seq_len - 1 - start - local])

    positions = both_halves(c_index * half_rows)
    key_positions = jnp.concatenate([both_halves(place[j] * half_rows) for j in range(ctx_count)])
    enc_positions = (place[:, None] * enc_rows + jnp.arange(enc_rows, dtype=jnp.int32)[None, :]).reshape(1, -1)
    levels = jnp.arange(BUCKETS + 1, dtype=jnp.int32)
    bounds = jnp.sum((rel_bucket[None, :] < levels[:, None]).astype(jnp.int32), axis=1)

    q, e = q.reshape(slab), e.reshape(lanes, slots, rows, -1)
    k, v = k.reshape(-1, slots, rows, width), v.reshape(-1, slots, rows, width)
    o, probs, own = self_forward(slot_len, bounds, positions[:, None], key_positions[None], q, e, k, v)
    o_flat = o.reshape(all_rows, width)
    if paired:
        second_near[1], second_near[2], feed_hops[0], feed_piece, _ = tie(
            second_near[1], second_near[2], feed_hops[0], feed_piece, o
        )
        feed_hops.append(z_hop(feed_piece, steps - 1))
        second_near = corner_spread(second_near, 1, cuts[1])
        second_far = [ctx_hop(second_near[0], CORE)]
        *feed_hops, second_near[1], second_near[2], second_near[3], second_near[4], second_far[0] = tie(
            *feed_hops, *second_near[1:], second_far[0]
        )
        second_far += [ctx_hop(item, CORE) for item in second_near[1:]]
        third_stack = stack_rows(tie(*feed_hops, *second_far[2:])[: steps - 1])
        third_near = list(first_spread(third_stack))
        (ck, cv), enc_flat, second = project(
            None, enc_parts, second_set, second_near + second_far, second_layout, cuts[1],
            ((True, 2), (True, 3)), after(where, third_stack), steps,
        )
        output_full, cquery_full, ckey_full, cvalue_full, coutput_full, vectors = second
        normed_one, unit_one, scale_one, normed_one_low, cq, norms = query_rows(
            x_all, o_flat, output_full, cquery_full, vectors, norm_count
        )
    else:
        output_full, cquery_full, ckey_full, cvalue_full, coutput_full = second
        norms = norms.astype(f32)
        resid_one = x_all.astype(f32) + matmul(o_flat, output_full)
        normed_one, unit_one, scale_one = norm_forward(resid_one, norms[0:1], norms[1:2])
        normed_one_low = normed_one.astype(bf16)
        cq = matmul(normed_one_low, cquery_full).astype(bf16)

    enc_shape = (ctx_count, slots, enc_rows, width)
    cq, ck, cv = cq.reshape(slab), ck.reshape(enc_shape), cv.reshape(enc_shape)
    oc, cprobs = cross_forward(enc_len, enc_positions, cq, ck, cv)
    oc_flat = oc.reshape(all_rows, width)

    core = (c_index & 1).astype(jnp.int32).reshape(1)

    def reduction(pairs, index, *more):
        return Reduction(pairs, layouts[index] + more, cuts[index], z_index, c_index)

    far = lambda *items: [ctx_hop(item, CORE) for item in items]

    row_valid = (positions[None, None, :] < slot_len[None, :, None]).astype(f32)
    row_valid = jnp.broadcast_to(row_valid, (lanes, slots, rows)).reshape(all_rows, 1)
    if paired:
        third_near[1], third_near[2], _ = tie(third_near[1], third_near[2], oc_flat)
        third_near = corner_spread(third_near, 1, cuts[2])
        third_far = [ctx_hop(item, CORE) for item in third_near[:3]]
        third_near[3], third_near[4], *third_far = tie(third_near[3], third_near[4], *third_far)
        third_far += [ctx_hop(item, CORE) for item in third_near[3:]]
        third = third_near + third_far
        feed_inputs = (feed_set, third, layouts[2], cuts[2], jnp.concatenate([core, where]))
    else:
        feed_inputs = (third, (), tuple(w.shape for w in third), 0, core)
    layer_out, normed_two_low, act_low, back_pre, back_feed, back_two, back_cross, back_oc, feed_norms, *sent = (
        feed_forward_backward(
            normed_one, oc_flat, coutput_full, norms, out_grad.reshape(all_rows, width), row_valid, *feed_inputs, steps, paired
        )
    )
    if paired:
        sent_up, sent_down, sent_coutput = sent
        third_sum = reduction([(normed_two_low, [back_pre]), (act_low, [back_feed])], 2)
        far_feed = far(sent_up, sent_down, sent_coutput)
    back_cq, back_ck, back_cv = cross_backward(cprobs, back_oc.reshape(slab), cq, ck, cv)
    back_cq = back_cq.reshape(all_rows, width)
    back_ck = back_ck.reshape(-1, width)
    back_cv = back_cv.reshape(-1, width)
    sending = ()
    if paired:
        *far_feed, back_cq = tie(*far_feed, back_cq)
        third_sum.fold(far_feed[:2], None, None, back_cq)
        third_first = third_sum.first_hops(1)
        back_cq = after(back_cq, third_sum.folded[0])
        sending = (normed_one_low, o_flat, feed_norms, enc_flat, back_ck, back_cv, ckey_full, cvalue_full)
    back_one, back_self, back_o, norm_grads, *sent = middle_backward(
        back_cq, cquery_full, back_two, unit_one, scale_one, norms, output_full, core, steps, sending
    )
    if paired:
        second_sum = reduction(
            [(o_flat, [back_self]), (normed_one_low, [back_cq]), (enc_flat, [back_ck, back_cv]), (oc_flat, [back_cross])],
            1,
            (128, 1024),
        )
        got_x, got_y, back_o, *sent = tie(*third_first, back_o, *sent)
        sent_cquery, sent_output, norm_keep, norm_send, sent_ckey, sent_cvalue, enc_keep, enc_send = sent
        third_sum.second_sums(got_x, got_y)
        third_late = third_sum.second_hops()
        far_some = far(sent_cquery, sent_output, sent_ckey)
        back_o = after(back_o, *third_sum.sums)
    else:
        enc_part = pair_rows(back_ck, back_cv, ckey_full, cvalue_full, ctx_count, slots * enc_rows)
    self_inputs = (bounds, positions[:, None], key_positions[None], probs, own)
    part_one = self_backward(*self_inputs, back_o.reshape(slab), q, k, v, 0, 2)
    if paired:
        late_x, late_y, *far_some, sent_cvalue, norm_send, enc_send, third_sum.folded[0], third_sum.folded[4], _ = tie(
            *third_late, *far_some, sent_cvalue, norm_send, enc_send, third_sum.folded[0], third_sum.folded[4], part_one[0]
        )
        third_got = third_sum.first_hops(0)
        norm_shape = (4 * steps, 16, width)
        far_rest = far(sent_cvalue, norm_send.reshape(norm_shape), enc_send)
        second_sum.fold(
            [far_some[1], far_some[0], far_some[2], far_rest[0], far_feed[2]],
            [enc_keep, far_rest[2]],
            [norm_keep.reshape(norm_shape), far_rest[1]],
        )
        *third_got, second_sum.folded[1], second_sum.folded[5] = tie(
            *third_got, second_sum.folded[1], second_sum.folded[5]
        )
        third_sum.z_sums(*third_got, late_x, late_y)
        hop = third_sum.z_step(1)
        second_first = second_sum.first_hops(1)
        back_o = after(back_o, second_sum.folded[1], third_sum.total)
    back_q, back_k, back_v, back_e = self_backward(*self_inputs, back_o.reshape(slab), q, k, v, 1, 2, part_one)
    back_q = back_q.reshape(all_rows, width)
    back_e = back_e.reshape(all_rows, -1)
    back_k = back_k.reshape(-1, width)
    back_v = back_v.reshape(-1, width)

    if paired:
        first_sum = reduction([(x_all, [back_q, back_e]), (keyed_flat, [back_k, back_v])], 0)
        hop, got_x, got_y, back_q, back_k = tie(hop, *second_first, back_q, back_k)
        hop = third_sum.z_step(2, hop)
        second_sum.second_sums(got_x, got_y)
        second_late = second_sum.second_hops()
        back_q = after(back_q, third_sum.total, *second_sum.sums)
        *sent_first, main_keep, main_send, back_x = last_backward(
            x_all, keyed_flat, back_one, back_q, back_e, back_k, back_v, query_full, relative_full, key_full, value_full,
            core, steps, ctx_count,
        )
        hop, late_x, late_y, main_send, second_sum.folded[0], second_sum.folded[4], *sent_first = tie(
            hop, *second_late, main_send, second_sum.folded[0], second_sum.folded[4], *sent_first
        )
        far_keys, far_values, far_query, far_main = far(*sent_first[:3], main_send)
        far_embed, hop, far_keys = tie(*far(sent_first[3]), hop, far_keys)
        hop = third_sum.z_step(3, hop)
        second_got = second_sum.first_hops(0)
        first_sum.fold([far_query, far_embed, far_keys, far_values], [main_keep, far_main], None, third_sum.total)
        got_x, got_y, hop, first_sum.folded[1], first_sum.folded[5] = tie(
            *second_got, hop, first_sum.folded[1], first_sum.folded[5]
        )
        first_first = first_sum.first_hops(1)
        third_sum.z_end(hop)
        second_sum.z_sums(got_x, got_y, late_x, late_y)
        hop = second_sum.z_step(1)
        hop, got_x, got_y = tie(hop, *first_first)
        first_sum.second_sums(got_x, got_y)
        first_late = first_sum.second_hops()
        first_sum.folded[0], first_sum.folded[4], hop, _ = tie(
            first_sum.folded[0], first_sum.folded[4], hop, first_sum.sums[0]
        )
        first_got = first_sum.first_hops(0)
        hop = second_sum.z_step(2, hop)
        hop, *rest, third_total = tie(hop, *first_got, *first_late, third_sum.total)
        third_sum.total = third_total
        first_sum.z_sums(*rest)
        first_hop = first_sum.z_step(1)
        hop = second_sum.z_step(3, hop)
        main_sum = jnp.concatenate(first_sum.extra, axis=0)
        hidden_grad = jnp.concatenate([back_x[: main_sum.shape[0]] + main_sum, back_x[main_sum.shape[0] :]], axis=0)
        encoder_grad = jnp.concatenate(second_sum.extra, axis=0)
        hop, first_hop, third_x, third_y = tie(hop, first_hop, *third_sum.spread())
        second_sum.z_end(hop)
        first_hop = first_sum.z_step(2, first_hop)
        corners = third_sum.corners(third_x, third_y)
        spread = second_sum.spread()
        first_hop, second_x, second_y, *third_sum.near[1:], hidden_grad = tie(
            first_hop, *spread, third_x, third_y, *corners, hidden_grad
        )
        first_hop = first_sum.z_step(3, first_hop)
        corners = second_sum.corners(second_x, second_y)
        third_far = far(*third_sum.near[1:3])
        first_hop, *second_sum.near[1:], third_far[0], third_far[1], encoder_grad = tie(
            first_hop, second_x, second_y, *corners, *third_far, encoder_grad
        )
        first_sum.z_end(first_hop)
        spread = first_sum.spread()
        more = far(third_sum.near[0], *third_sum.near[3:])
        *more, held = tie(*more, second_sum.near[0])
        third_far = [more[0], *third_far, *more[1:]]
        second_sum.near[0] = held
        second_far = far(*second_sum.near[:3])
        third_grads = third_sum.grads(third_sum.near + third_far)
        first_x, first_y, *second_far, _ = tie(*spread, *second_far, third_grads[0])
        corners = first_sum.corners(first_x, first_y)
        second_far += far(*second_sum.near[3:])
        *second_grads, norm_sums = second_sum.grads(second_sum.near + second_far)
        norm_sums = norm_sums.reshape(8, 16, 1024)[:, :norm_count, : norm_shard // 8]
        norm_grads = [item for item in norm_sums.transpose(1, 0, 2).reshape(norm_count, norm_shard)]
        *first_sum.near[1:], second_grads[0], norm_grads = tie(first_x, first_y, *corners, second_grads[0], norm_grads)
        first_grads = first_sum.grads(first_sum.near + far(*first_sum.near))
    else:
        *main_part, other_part = pair_rows(back_k, back_v, key_full, value_full, ctx_count, slots * rows)
        back_x = back_one + matmul_back(back_q, query_full) + matmul_back(back_e, relative_full)
        back_x = jnp.concatenate([back_x[: slots * rows], back_x[slots * rows :] + other_part], axis=0)
        norm_grads = lax.psum(jnp.concatenate([norm_grads, feed_norms], axis=0), ("fsdp", "ctx"))
        norm_grads = lax.dynamic_slice_in_dim(norm_grads, z_index * norm_shard, norm_shard, 1)

        def reduce(left, right):
            shard = lax.psum_scatter(outer_rows(left, right).astype(bf16), "fsdp", scatter_dimension=0, tiled=True)
            return lax.psum(shard, "ctx").astype(f32)

        def scatter(parts):
            whole = jnp.stack(parts, axis=1).reshape(ctx_count, -1, width)
            return lax.psum_scatter(whole, "ctx", scatter_dimension=0, tiled=True).astype(f32).reshape(-1, width)

        first_grads = [
            reduce(x_all, back_q), reduce(x_all, back_e), reduce(keyed_flat, back_k), reduce(keyed_flat, back_v),
        ]
        second_grads = [
            reduce(o_flat, back_self), reduce(normed_one_low, back_cq), reduce(enc_flat, back_ck),
            reduce(enc_flat, back_cv), reduce(oc_flat, back_cross),
        ]
        third_grads = [reduce(normed_two_low, back_pre), reduce(act_low, back_feed)]
        encoder_grad = scatter(enc_part)
        main_sum = scatter(main_part)
        hidden_grad = jnp.concatenate([back_x[: main_sum.shape[0]] + main_sum, back_x[main_sum.shape[0] :]], axis=0)
    out_shape = hidden.shape
    return (
        layer_out.reshape(out_shape), hidden_grad.reshape(out_shape), encoder_grad.reshape(encoder_out.shape),
        first_grads[0], first_grads[2], first_grads[3], first_grads[1], second_grads[0], norm_grads[0], norm_grads[1],
        second_grads[1], second_grads[2], second_grads[3], second_grads[4], norm_grads[2], norm_grads[3],
        third_grads[0], third_grads[1], norm_grads[4], norm_grads[5],
    )


def solution(mesh):
    rows = P("fsdp", None)
    vector = P("fsdp")
    slab = P(None, "fsdp", None, "ctx", None)
    encoder = P("fsdp", "ctx", None)
    weights = (rows,) * 5 + (vector,) * 2 + (rows,) * 4 + (vector,) * 2 + (rows,) * 2 + (vector,) * 2
    return jax.shard_map(
        on_device,
        mesh=mesh,
        in_specs=(slab, encoder, slab, vector, vector, P()) + weights,
        out_specs=(slab, slab, encoder) + weights,
        check_vma=False,
    )
```

```python
import functools

import jax
import jax.numpy as jnp
from jax import lax
from jax.experimental import pallas as pl
from jax.experimental.pallas import tpu as pltpu
from jax.sharding import PartitionSpec as P

HEAD_DIM = 64
BUCKETS = 32
LANE = 128
GROUP = 4
SUB = 8
eps_norm = 1e-05
neg_fill = -1e30
bf16 = jnp.bfloat16
f32 = jnp.float32
CORE, XBIT, YBIT = 1, 2, 4
VMEM_LIMIT = 63 * 1024 * 1024


def matmul(left_side, right_side):
    return jnp.dot(left_side, right_side, preferred_element_type=f32)


def matmul_back(left_side, right_side):
    return lax.dot_general(left_side, right_side, (((1,), (1,)), ((), ())), preferred_element_type=f32)


def outer_rows(left_side, right_side):
    return lax.dot_general(left_side, right_side, (((0,), (0,)), ((), ())), preferred_element_type=f32)


def norm_forward(values, gain, shift):
    row_mean = jnp.mean(values, axis=-1, keepdims=True)
    centered = values - row_mean
    scale = lax.rsqrt(jnp.mean(centered * centered, axis=-1, keepdims=True) + eps_norm)
    unit = centered * scale
    return unit * gain + shift, unit, scale


def norm_backward(unit, scale, gain, cotangent):
    back_unit = cotangent * gain
    first = jnp.mean(back_unit, axis=-1, keepdims=True)
    second = jnp.mean(back_unit * unit, axis=-1, keepdims=True)
    back = scale * (back_unit - first - unit * second)
    return back, jnp.sum(cotangent * unit, axis=0), jnp.sum(cotangent, axis=0)


def dot_nt(left_side, right_side):
    return lax.dot_general(left_side, right_side, (((1,), (1,)), ((), ())), preferred_element_type=f32)


def dot_nn(left_side, right_side):
    return lax.dot_general(left_side, right_side, (((1,), (0,)), ((), ())), preferred_element_type=f32)


def dot_tn(left_side, right_side):
    return lax.dot_general(left_side, right_side, (((0,), (0,)), ((), ())), preferred_element_type=f32)


def stack_heads(pair, low_half):
    zero = jnp.zeros_like(pair)
    return jnp.concatenate([jnp.where(low_half, pair, zero), jnp.where(low_half, zero, pair)], axis=0)


def rows_of(ref, first, last, cols):
    block = ref[first:last, 0, :, cols]
    return block.reshape(block.shape[0] * block.shape[1], block.shape[2])


def fill_one_hot(bucket_ref, one_hot_ref):
    keys = bucket_ref.shape[1]
    levels = lax.broadcasted_iota(jnp.int32, (BUCKETS, keys), 0)

    def fill(row, carry):
        line = jnp.broadcast_to(bucket_ref[pl.ds(row, 1), :], (BUCKETS, keys))
        start = pl.multiple_of(lax.rem(row, SUB) * BUCKETS, BUCKETS)
        one_hot_ref[row // SUB, pl.ds(start, BUCKETS), :] = jnp.where(line == levels, 1.0, 0.0).astype(bf16)
        return carry

    lax.fori_loop(0, bucket_ref.shape[0], fill, 0)


def fill_buckets(distance, bounds_ref, bucket_ref):
    bucket_ref[...] = jnp.zeros(distance.shape, jnp.int32)

    def fill(level, carry):
        bucket_ref[...] += (distance >= bounds_ref[level]).astype(jnp.int32)
        return carry

    lax.fori_loop(1, BUCKETS, fill, 0)


def own_block_mask(rows):
    row = lax.broadcasted_iota(jnp.int32, (rows, SUB * BUCKETS), 0)
    col = lax.broadcasted_iota(jnp.int32, (rows, SUB * BUCKETS), 1)
    return (row & (SUB - 1)) == (col // BUCKETS)


def self_forward_kernel(
    held, base, length_ref, bounds_ref, posq_ref, posk_ref, q_ref, e_ref, k_ref, v_ref, *refs,
):
    o_ref, p_ref, own_ref, bucket_ref, one_hot_ref, spread_ref, bias_ref = refs[held:]
    slot = pl.program_id(0)
    group = pl.program_id(1)
    lanes, _, rows, _ = q_ref.shape
    pieces = k_ref.shape[0] - (lanes - 1)
    keys = pieces * k_ref.shape[2]
    heads = bias_ref.shape[0]
    span = SUB * BUCKETS

    @pl.when((slot == 0) & (group == 0))
    def _():
        fill_buckets(posq_ref[...] - posk_ref[...], bounds_ref, bucket_ref)
        fill_one_hot(bucket_ref, one_hot_ref)

    @pl.when(group == 0)
    def _():
        keep = own_block_mask(lanes * rows)
        source = lax.broadcasted_iota(jnp.int32, (LANE, span), 0)
        target = lax.broadcasted_iota(jnp.int32, (LANE, span), 1) & (BUCKETS - 1)
        for part in range(LANE // BUCKETS):
            copy = jnp.where(source == target + part * BUCKETS, 1.0, 0.0).astype(bf16)
            for block in range(heads * BUCKETS // LANE):
                column = base * GROUP * BUCKETS + block * LANE
                rows_e = rows_of(e_ref, 0, lanes, slice(column, column + LANE))
                head = block * (LANE // BUCKETS) + part
                spread_ref[head] = jnp.where(keep, dot_nn(rows_e, copy), 0.0)
        distance = posq_ref[...] - posk_ref[...]
        valid = posk_ref[...] < length_ref[slot]
        fills = [jnp.where(valid & (distance >= edge), 0.0, neg_fill) for edge in (0, 1)]
        for g in range(rows // SUB):
            starts = [lane * rows + g * SUB for lane in range(lanes)]
            left = [spread_ref[:, start : start + SUB, :].reshape(heads * SUB, span) for start in starts]
            bias = dot_nn(jnp.concatenate(left, axis=0).astype(bf16), one_hot_ref[g])
            bias = bias.reshape(lanes, heads, SUB, keys)
            for lane, start in enumerate(starts):
                fill = fills[min(lane, 1)][None, g * SUB : (g + 1) * SUB, :]
                bias_ref[:, start : start + SUB, :] = bias[lane] + fill

    low_half = lax.broadcasted_iota(jnp.int32, (1, LANE), 1) < HEAD_DIM
    lane_id = lax.broadcasted_iota(jnp.int32, (1, LANE), 1)
    own_all = [jnp.zeros((rows, LANE), f32) for _ in range(lanes)]
    e_cols = pl.ds(pl.multiple_of((base + group) * (GROUP * BUCKETS), LANE), GROUP * BUCKETS)
    tables = [None] + [e_ref[lane, 0, :, e_cols].astype(f32) for lane in range(1, lanes)]
    for pair in range(GROUP // 2):
        cols = slice(pair * LANE, (pair + 1) * LANE)
        q_pair = rows_of(q_ref, 0, lanes, cols) * jnp.asarray(HEAD_DIM**-0.5, bf16)
        k_main = rows_of(k_ref, 0, pieces, cols)
        v_main = rows_of(v_ref, 0, pieces, cols)
        scores = dot_nt(stack_heads(q_pair, low_half), k_main)
        own_pair = []
        for half in range(2):
            head = pair * 2 + half
            keep = low_half if half == 0 else jnp.logical_not(low_half)
            for lane in range(lanes):
                start = (half * lanes + lane) * rows
                part = scores[start : start + rows]
                part = part + bias_ref[group * GROUP + head, lane * rows : (lane + 1) * rows, :]
                top = jnp.max(part, axis=1, keepdims=True)
                if lane > 0:
                    q_row = q_pair[lane * rows : (lane + 1) * rows].astype(f32)
                    k_row = k_ref[pieces + lane - 1, 0, :, cols].astype(f32)
                    own = jnp.sum(jnp.where(keep, q_row * k_row, 0.0), axis=1, keepdims=True)
                    own = own + tables[lane][:, head * BUCKETS : head * BUCKETS + 1]
                    top = jnp.maximum(top, own)
                    own_exp = jnp.exp(own - top)
                terms = jnp.exp(part - top)
                total = jnp.sum(terms, axis=1, keepdims=True)
                if lane > 0:
                    total = total + own_exp
                inverse = 1.0 / total
                p_ref[0, head, lane * rows : (lane + 1) * rows, :] = (terms * inverse).astype(bf16)
                if lane > 0:
                    own_prob = own_exp * inverse
                    own_all[lane] = jnp.where(lane_id == head, own_prob, own_all[lane])
                else:
                    own_prob = jnp.zeros((rows, 1), f32)
                own_pair.append(own_prob)
        p_low = p_ref[0, pair * 2 : pair * 2 + 2].reshape(2 * lanes * rows, keys)
        mixed = dot_nn(p_low, v_main)
        for lane in range(lanes):
            first = lane * rows
            second = (lanes + lane) * rows
            out = jnp.where(low_half, mixed[first : first + rows], mixed[second : second + rows])
            if lane > 0:
                own_prob = jnp.where(low_half, own_pair[lane], own_pair[lanes + lane])
                v_row = v_ref[pieces + lane - 1, 0, :, cols].astype(f32)
                out = out + own_prob.astype(bf16).astype(f32) * v_row
            o_ref[lane, 0, :, cols] = out.astype(bf16)
    for lane in range(lanes):
        own_ref[0, 0, lane * rows : (lane + 1) * rows, :] = own_all[lane]


def self_backward_kernel(
    held, bounds_ref, posq_ref, posk_ref, p_ref, own_ref, do_ref, q_ref, k_ref, v_ref, *refs,
):
    dq_ref, dk_ref, dv_ref, de_ref = refs[held : held + 4]
    bucket_ref, one_hot_ref, turned_ref, scores_ref, down_ref, wide_ref = refs[held + 4 :]
    group = pl.program_id(1)
    lanes, _, rows, _ = q_ref.shape
    pieces = k_ref.shape[0] - (lanes - 1)
    piece_rows = k_ref.shape[2]
    keys = pieces * piece_rows
    scale = HEAD_DIM**-0.5

    heads = scores_ref.shape[0]
    span = SUB * BUCKETS

    @pl.when((pl.program_id(0) == 0) & (group == 0))
    def _():
        fill_buckets(posq_ref[...] - posk_ref[...], bounds_ref, bucket_ref)
        fill_one_hot(bucket_ref, one_hot_ref)
        for g in range(rows // SUB):
            turned_ref[g] = one_hot_ref[g].T

    lane_id = lax.broadcasted_iota(jnp.int32, (1, LANE), 1)
    low_half = lane_id < HEAD_DIM
    downs = [jnp.zeros((rows, LANE), f32) for _ in range(lanes)]
    for pair in range(GROUP // 2):
        cols = slice(pair * LANE, (pair + 1) * LANE)
        q_pair = rows_of(q_ref, 0, lanes, cols) * jnp.asarray(scale, bf16)
        do_pair = rows_of(do_ref, 0, lanes, cols)
        k_main = rows_of(k_ref, 0, pieces, cols)
        v_main = rows_of(v_ref, 0, pieces, cols)
        q_stack = stack_heads(q_pair, low_half)
        do_stack = stack_heads(do_pair, low_half)
        back_probs = dot_nt(do_stack, v_main)
        p_low = p_ref[0, pair * 2 : pair * 2 + 2].reshape(2 * lanes * rows, keys)
        probs = p_low.astype(f32)
        weighted = probs * back_probs
        delta = jnp.sum(weighted, axis=1, keepdims=True)
        down_pair = []
        delta_list = []
        for half in range(2):
            head = pair * 2 + half
            keep = low_half if half == 0 else jnp.logical_not(low_half)
            for lane in range(lanes):
                start = (half * lanes + lane) * rows
                part = delta[start : start + rows]
                if lane > 0:
                    do_row = do_pair[lane * rows : (lane + 1) * rows].astype(f32)
                    v_row = v_ref[pieces + lane - 1, 0, :, cols].astype(f32)
                    back_own = jnp.sum(jnp.where(keep, do_row * v_row, 0.0), axis=1, keepdims=True)
                    own_prob = own_ref[0, 0, lane * rows : (lane + 1) * rows, head : head + 1]
                    part = part + own_prob * back_own
                    down_pair.append((own_prob * (back_own - part)).astype(bf16).astype(f32))
                else:
                    down_pair.append(None)
                delta_list.append(part)
        delta = jnp.concatenate(delta_list, axis=0)
        back_scores = (weighted - probs * delta).astype(bf16)
        back_q = dot_nn(back_scores, k_main)
        back_k = dot_tn(q_stack, back_scores)
        back_v = dot_tn(do_stack, p_low)
        dk_ref[:pieces, 0, :, cols] = back_k.T.astype(bf16).reshape(pieces, piece_rows, LANE)
        dv_ref[:pieces, 0, :, cols] = back_v.T.astype(bf16).reshape(pieces, piece_rows, LANE)
        scores_ref[pl.ds(group * GROUP + pair * 2, 2)] = back_scores.astype(f32).reshape(2, lanes * rows, keys)
        for lane in range(lanes):
            first = lane * rows
            second = (lanes + lane) * rows
            back = jnp.where(low_half, back_q[first : first + rows], back_q[second : second + rows])
            if lane > 0:
                k_row = k_ref[pieces + lane - 1, 0, :, cols].astype(f32)
                down = jnp.where(low_half, down_pair[lane], down_pair[lanes + lane])
                back = back + down * k_row
                own_low = jnp.where(
                    low_half,
                    own_ref[0, 0, lane * rows : (lane + 1) * rows, pair * 2 : pair * 2 + 1],
                    own_ref[0, 0, lane * rows : (lane + 1) * rows, pair * 2 + 1 : pair * 2 + 2],
                )
                own_low = own_low.astype(bf16).astype(f32)
                dk_ref[pieces + lane - 1, 0, :, cols] = (
                    down * q_pair[first : first + rows].astype(f32)
                ).astype(bf16)
                dv_ref[pieces + lane - 1, 0, :, cols] = (
                    own_low * do_pair[first : first + rows].astype(f32)
                ).astype(bf16)
            dq_ref[lane, 0, :, cols] = (back * scale).astype(bf16)
            if lane > 0:
                for half in range(2):
                    spot = (pair * 2 + half) * BUCKETS
                    downs[lane] = jnp.where(lane_id == spot, down_pair[half * lanes + lane], downs[lane])
    for lane in range(1, lanes):
        down_ref[group, lane] = downs[lane]

    @pl.when(group == pl.num_programs(1) - 1)
    def _():
        keep = own_block_mask(lanes * heads * SUB)
        source = lax.broadcasted_iota(jnp.int32, (span, LANE), 0) & (BUCKETS - 1)
        target = lax.broadcasted_iota(jnp.int32, (span, LANE), 1) & (BUCKETS - 1)
        fold = jnp.where(source == target, 1.0, 0.0).astype(bf16)
        per_block = LANE // BUCKETS
        for g in range(rows // SUB):
            starts = [lane * rows + g * SUB for lane in range(lanes)]
            left = [scores_ref[:, start : start + SUB, :].reshape(heads * SUB, keys) for start in starts]
            sums = dot_nn(jnp.concatenate(left, axis=0).astype(bf16), turned_ref[g])
            embed = dot_nn(jnp.where(keep, sums, 0.0).astype(bf16), fold).reshape(lanes, heads, SUB, LANE)
            for lane in range(lanes):
                for block in range(heads // per_block):
                    out = embed[lane, block * per_block]
                    for part in range(1, per_block):
                        out = jnp.where(lane_id // BUCKETS == part, embed[lane, block * per_block + part], out)
                    if lane > 0:
                        out = out + down_ref[block, lane, g * SUB : (g + 1) * SUB, :]
                    wide_ref[lane, g * SUB : (g + 1) * SUB, block * LANE : (block + 1) * LANE] = out
        for lane in range(lanes):
            de_ref[lane, 0] = wide_ref[lane].astype(bf16)


def cross_forward_kernel(length_ref, posk_ref, q_ref, k_ref, v_ref, o_ref, p_ref):
    slot = pl.program_id(0)
    lanes, _, rows, _ = q_ref.shape
    pieces = k_ref.shape[0]
    keys = pieces * k_ref.shape[2]
    low_half = lax.broadcasted_iota(jnp.int32, (1, LANE), 1) < HEAD_DIM
    fill = jnp.where(posk_ref[...] < length_ref[slot], 0.0, neg_fill)
    count = lanes * rows
    for pair in range(GROUP // 2):
        cols = slice(pair * LANE, (pair + 1) * LANE)
        q_pair = rows_of(q_ref, 0, lanes, cols) * jnp.asarray(HEAD_DIM**-0.5, bf16)
        k_main = rows_of(k_ref, 0, pieces, cols)
        v_main = rows_of(v_ref, 0, pieces, cols)
        scores = dot_nt(stack_heads(q_pair, low_half), k_main) + fill
        top = jnp.max(scores, axis=1, keepdims=True)
        terms = jnp.exp(scores - top)
        inverse = 1.0 / jnp.sum(terms, axis=1, keepdims=True)
        p_low = (terms * inverse).astype(bf16)
        p_ref[0, pair * 2 : pair * 2 + 2] = p_low.reshape(2, count, keys)
        mixed = dot_nn(p_low, v_main)
        out = jnp.where(low_half, mixed[:count], mixed[count:]).astype(bf16)
        o_ref[:, 0, :, cols] = out.reshape(lanes, rows, LANE)


def cross_backward_kernel(p_ref, do_ref, q_ref, k_ref, v_ref, dq_ref, dk_ref, dv_ref):
    lanes, _, rows, _ = q_ref.shape
    pieces = k_ref.shape[0]
    piece_rows = k_ref.shape[2]
    keys = pieces * piece_rows
    count = lanes * rows
    scale = HEAD_DIM**-0.5
    low_half = lax.broadcasted_iota(jnp.int32, (1, LANE), 1) < HEAD_DIM
    for pair in range(GROUP // 2):
        cols = slice(pair * LANE, (pair + 1) * LANE)
        q_pair = rows_of(q_ref, 0, lanes, cols) * jnp.asarray(scale, bf16)
        do_pair = rows_of(do_ref, 0, lanes, cols)
        k_main = rows_of(k_ref, 0, pieces, cols)
        v_main = rows_of(v_ref, 0, pieces, cols)
        q_stack = stack_heads(q_pair, low_half)
        do_stack = stack_heads(do_pair, low_half)
        back_probs = dot_nt(do_stack, v_main)
        p_low = p_ref[0, pair * 2 : pair * 2 + 2].reshape(2 * count, keys)
        probs = p_low.astype(f32)
        weighted = probs * back_probs
        delta = jnp.sum(weighted, axis=1, keepdims=True)
        back_scores = (weighted - probs * delta).astype(bf16)
        back_q = dot_nn(back_scores, k_main)
        back_k = dot_tn(q_stack, back_scores)
        back_v = dot_tn(do_stack, p_low)
        dk_ref[:, 0, :, cols] = back_k.T.astype(bf16).reshape(pieces, piece_rows, LANE)
        dv_ref[:, 0, :, cols] = back_v.T.astype(bf16).reshape(pieces, piece_rows, LANE)
        back = jnp.where(low_half, back_q[:count], back_q[count:]) * scale
        dq_ref[:, 0, :, cols] = back.astype(bf16).reshape(lanes, rows, LANE)


def head_block(array, width=GROUP * HEAD_DIM):
    return pl.BlockSpec((array.shape[0], 1, array.shape[2], width), lambda s, g: (0, s, 0, g))


def slot_block(array):
    return pl.BlockSpec((array.shape[0], 1) + array.shape[2:], lambda s, g: (0, s, 0, 0))


def whole_block(array):
    return pl.BlockSpec(array.shape, lambda s, g: (0,) * array.ndim)


SMALL = pl.CostEstimate(flops=1000, bytes_accessed=1000, transcendentals=0)
SMEM_SPEC = pl.BlockSpec(memory_space=pltpu.SMEM)


def params():
    return pltpu.CompilerParams(vmem_limit_bytes=VMEM_LIMIT)


def shaped(shape, dtype):
    return jax.ShapeDtypeStruct(shape, dtype)


def self_forward(length, bounds, posq, posk, q, e, k, v, part, parts, made=()):
    lanes, slots, rows, width = q.shape
    all_heads = width // HEAD_DIM
    heads = all_heads // parts
    keys = posk.shape[1]
    count = lanes * rows
    groups = heads // GROUP
    base = part * groups

    def block(array):
        return pl.BlockSpec((array.shape[0], 1, array.shape[2], GROUP * HEAD_DIM), lambda s, g: (0, s, 0, base + g))

    inputs = [length, bounds, posq, posk, q, e, k, v]
    return pl.pallas_call(
        functools.partial(self_forward_kernel, len(made), base),
        grid=(slots, groups),
        in_specs=[
            SMEM_SPEC, SMEM_SPEC, whole_block(posq), whole_block(posk), block(q), slot_block(e), block(k), block(v),
        ] + [pl.BlockSpec(memory_space=pl.ANY)] * len(made),
        out_specs=[
            block(q),
            pl.BlockSpec((1, GROUP, count, keys), lambda s, g: (s, base + g, 0, 0)),
            pl.BlockSpec((1, 1, count, LANE), lambda s, g: (s, base + g, 0, 0)),
        ],
        out_shape=[
            shaped(q.shape, bf16),
            shaped((slots, all_heads, count, keys), bf16),
            shaped((slots, all_heads // GROUP, count, LANE), f32),
        ],
        scratch_shapes=[
            pltpu.VMEM((rows, keys), jnp.int32),
            pltpu.VMEM((rows // SUB, SUB * BUCKETS, keys), bf16),
            pltpu.VMEM((heads, count, SUB * BUCKETS), f32),
            pltpu.VMEM((heads, count, keys), f32),
        ],
        input_output_aliases={len(inputs) + i: i for i in range(len(made))},
        compiler_params=params(),
        cost_estimate=SMALL,
        name="self_forward",
    )(*inputs, *made)


def self_backward(bounds, posq, posk, p, own, do, q, k, v, part, parts, made=()):
    lanes, slots, rows, width = q.shape
    heads = width // HEAD_DIM // parts
    keys = p.shape[3]
    count = lanes * rows
    groups = heads // GROUP
    base = part * groups

    def block(array):
        return pl.BlockSpec((array.shape[0], 1, array.shape[2], GROUP * HEAD_DIM), lambda s, g: (0, s, 0, base + g))

    inputs = [bounds, posq, posk, p, own, do, q, k, v]
    return pl.pallas_call(
        functools.partial(self_backward_kernel, len(made)),
        grid=(slots, groups),
        in_specs=[
            SMEM_SPEC, whole_block(posq), whole_block(posk),
            pl.BlockSpec((1, GROUP, count, keys), lambda s, g: (s, base + g, 0, 0)),
            pl.BlockSpec((1, 1, count, LANE), lambda s, g: (s, base + g, 0, 0)),
            block(do), block(q), block(k), block(v),
        ] + [pl.BlockSpec(memory_space=pl.ANY)] * len(made),
        out_specs=[
            block(q), block(k), block(v),
            pl.BlockSpec((lanes, 1, rows, heads * BUCKETS), lambda s, g: (0, s, 0, part)),
        ],
        out_shape=[
            shaped(q.shape, bf16), shaped(k.shape, bf16), shaped(v.shape, bf16),
            shaped((lanes, slots, rows, heads * parts * BUCKETS), bf16),
        ],
        scratch_shapes=[
            pltpu.VMEM((rows, keys), jnp.int32),
            pltpu.VMEM((rows // SUB, SUB * BUCKETS, keys), bf16),
            pltpu.VMEM((rows // SUB, keys, SUB * BUCKETS), bf16),
            pltpu.VMEM((heads, count, keys), f32),
            pltpu.VMEM((groups, lanes, rows, LANE), f32),
            pltpu.VMEM((lanes, rows, heads * BUCKETS), f32),
        ],
        input_output_aliases={len(inputs) + i: i for i in range(len(made))},
        compiler_params=params(),
        cost_estimate=SMALL,
        name="self_backward",
    )(*inputs, *made)


def cross_forward(length, posk, q, k, v):
    lanes, slots, rows, width = q.shape
    heads = width // HEAD_DIM
    keys = posk.shape[1]
    count = lanes * rows
    return pl.pallas_call(
        cross_forward_kernel,
        grid=(slots, heads // GROUP),
        in_specs=[SMEM_SPEC, whole_block(posk), head_block(q), head_block(k), head_block(v)],
        out_specs=[head_block(q), pl.BlockSpec((1, GROUP, count, keys), lambda s, g: (s, g, 0, 0))],
        out_shape=[shaped(q.shape, bf16), shaped((slots, heads, count, keys), bf16)],
        compiler_params=params(),
        cost_estimate=SMALL,
        name="cross_forward",
    )(length, posk, q, k, v)


def cross_backward(p, do, q, k, v):
    lanes, slots, rows, width = q.shape
    heads = width // HEAD_DIM
    keys = p.shape[3]
    count = lanes * rows
    return pl.pallas_call(
        cross_backward_kernel,
        grid=(slots, heads // GROUP),
        in_specs=[
            pl.BlockSpec((1, GROUP, count, keys), lambda s, g: (s, g, 0, 0)),
            head_block(do), head_block(q), head_block(k), head_block(v),
        ],
        out_specs=[head_block(q), head_block(k), head_block(v)],
        out_shape=[shaped(q.shape, bf16), shaped(k.shape, bf16), shaped(v.shape, bf16)],
        compiler_params=params(),
        cost_estimate=SMALL,
        name="cross_backward",
    )(p, do, q, k, v)


FEED_BLOCK = 512


def norm_parts(values):
    row_mean = jnp.mean(values, axis=-1, keepdims=True)
    centered = values - row_mean
    scale = lax.rsqrt(jnp.mean(centered * centered, axis=-1, keepdims=True) + eps_norm)
    return centered * scale, scale


def feed_kernel(
    sending, loading, core_ref, base_ref, mixed_ref, outer_ref, norms_ref, cot_ref, valid_ref, *refs,
):
    layout, copies, cut, parts, number_in = loading
    sources, refs = refs[:number_in], refs[number_in:]
    feed_body(sending, (layout, copies, cut, parts, sources), core_ref, base_ref, mixed_ref, outer_ref, norms_ref, cot_ref, valid_ref, *refs)


def feed_body(
    sending, loading, core_ref, base_ref, mixed_ref, outer_ref, norms_ref, cot_ref, valid_ref,
    out_ref, low_ref, act_ref, back_pre_ref, feed_ref, back_ref, cross_ref, back_mixed_ref, grads_ref, *rest,
):
    if sending:
        up_send_ref, down_send_ref, outer_send_ref, *rest = rest
    unit_ref, total_ref, turned_ref, act_all_ref, slope_ref, row_scale_ref, up_all_ref, down_all_ref, sems = rest
    phase, block = pl.program_id(0), pl.program_id(1)
    last = pl.num_programs(1) - 1
    cols = pl.ds(pl.multiple_of(block * FEED_BLOCK, FEED_BLOCK), FEED_BLOCK)

    up_ref = lambda: up_all_ref[:, cols]
    down_ref = lambda: down_all_ref[cols, :]
    layout, copies, cut, parts, sources = loading

    def loads():
        return group_loads(layout, copies, cut, parts, core_ref, sources, (up_all_ref, down_all_ref), sems, 1)

    @pl.when((phase == 0) & (block == 0))
    def _():
        for _, load in loads():
            load.start()
        unit, scale = norm_parts(base_ref[...] + dot_nn(mixed_ref[...], outer_ref[...]))
        normed = unit * norms_ref[2:3, :] + norms_ref[3:4, :]
        unit_ref[...] = unit
        row_scale_ref[...] = scale
        total_ref[...] = normed
        low_ref[...] = normed.astype(bf16)
        if sending:
            turned_ref[...] = core_columns(low_ref, 1 - core_ref[0], sending).T
        for _, load in loads():
            load.wait()

    @pl.when(phase == 0)
    def _():
        pre = dot_nn(low_ref[...], up_ref())
        below = 0.5 * (1.0 + lax.erf(pre * 0.7071067811865476))
        act = (pre * below).astype(bf16)
        slope_ref[:, cols] = below + pre * (jnp.exp(-0.5 * pre * pre) * 0.3989422804014327)
        act_all_ref[:, cols] = act
        act_ref[...] = act
        total_ref[...] += dot_nn(act, down_ref())

    @pl.when((phase == 0) & (block == last))
    def _():
        unit, scale = norm_parts(total_ref[...])
        gain = norms_ref[4:5, :]
        out_ref[...] = (unit * gain + norms_ref[5:6, :]).astype(bf16)
        cotangent = cot_ref[...].astype(f32) * valid_ref[...]
        back, gain_grad, shift_grad = norm_backward(unit, scale, gain, cotangent)
        grads_ref[2:3, :] = gain_grad[None]
        grads_ref[3:4, :] = shift_grad[None]
        total_ref[...] = back
        feed_ref[...] = back.astype(bf16)

    @pl.when(phase == 1)
    def _():
        back_act = dot_nt(feed_ref[...], down_ref())
        back_pre = (back_act * slope_ref[:, cols]).astype(bf16)
        back_pre_ref[...] = back_pre
        total_ref[...] += dot_nt(back_pre, up_ref())
        if sending:
            up_send_ref[...] = dot_nn(turned_ref[...], back_pre).astype(bf16)

            @pl.when((block & 1) == 1 - core_ref[0])
            def _():
                down_send_ref[...] = dot_tn(act_all_ref[:, cols], feed_ref[...]).astype(bf16)

    @pl.when((phase == 1) & (block == last))
    def _():
        back, gain_grad, shift_grad = norm_backward(
            unit_ref[...], row_scale_ref[...], norms_ref[2:3, :], total_ref[...]
        )
        back_ref[...] = back
        cross_ref[...] = back.astype(bf16)
        back_mixed_ref[...] = dot_nt(cross_ref[...], outer_ref[...]).astype(bf16)
        if sending:
            outer_send_ref[...] = dot_tn(core_columns(mixed_ref, 1 - core_ref[0], sending), cross_ref[...]).astype(bf16)
        grads_ref[0:1, :] = gain_grad[None]
        grads_ref[1:2, :] = shift_grad[None]


def feed_forward_backward(base, mixed, outer, norms, cot, valid, weights, arrivals, layout, cut, place, steps, sending):
    rows, width = base.shape
    hidden = layout[0][1]
    blocks = hidden // FEED_BLOCK
    copies, _ = block_copies(layout)
    sources = [*weights, *arrivals]
    parts = steps if arrivals else 1
    single = pl.Buffered(1)
    whole = lambda array: pl.BlockSpec(array.shape, lambda p, b, c: (0, 0), pipeline_mode=single)
    full = pl.BlockSpec((rows, width), lambda p, b, c: (0, 0))
    first = lambda p, b: jnp.where(p == 0, b, blocks - 1)
    second = lambda p, b: jnp.where(p == 0, 0, b)
    out_specs = [
        full, full,
        pl.BlockSpec((rows, FEED_BLOCK), lambda p, b, c: (0, first(p, b))),
        pl.BlockSpec((rows, FEED_BLOCK), lambda p, b, c: (0, second(p, b))),
        full, full, full, full,
        pl.BlockSpec((4, width), lambda p, b, c: (0, 0)),
    ]
    low = shaped((rows, width), bf16)
    wide = shaped((rows, hidden), bf16)
    out_shape = [low, low, wide, wide, low, shaped((rows, width), f32), low, low, shaped((4, width), f32)]
    if sending:
        assert hidden // (2 * steps) == FEED_BLOCK
        out_specs += [
            pl.BlockSpec((width // 2, FEED_BLOCK), lambda p, b, c: (0, second(p, b))),
            pl.BlockSpec((FEED_BLOCK, width), lambda p, b, c: (second(p, b) // 2, 0)),
            pl.BlockSpec((width // 2, width), lambda p, b, c: (0, 0)),
        ]
        out_shape += [
            shaped((width // 2, hidden), bf16), shaped((hidden // 2, width), bf16), shaped((width // 2, width), bf16),
        ]
    return pl.pallas_call(
        functools.partial(feed_kernel, steps if sending else 0, (layout, copies, cut, parts, len(sources))),
        grid_spec=pltpu.PrefetchScalarGridSpec(
            num_scalar_prefetch=1,
            grid=(2, blocks),
            in_specs=[
                whole(base), whole(mixed), whole(outer), whole(norms), whole(cot), whole(valid),
            ] + [pl.BlockSpec(memory_space=pl.ANY)] * len(sources),
            out_specs=out_specs,
            scratch_shapes=[
                pltpu.VMEM((rows, width), f32), pltpu.VMEM((rows, width), f32),
                pltpu.VMEM((width // 2, rows), bf16), pltpu.VMEM((rows, hidden), bf16), pltpu.VMEM((rows, hidden), f32),
                pltpu.VMEM((rows, 1), f32),
                pltpu.VMEM((width, hidden), bf16), pltpu.VMEM((hidden, width), bf16), pltpu.SemaphoreType.DMA((2,)),
            ],
        ),
        out_shape=out_shape,
        compiler_params=params(),
        cost_estimate=SMALL,
        name="feed",
    )(place, base, mixed, outer, norms, cot, valid, *sources)


def middle_kernel(
    sending, core_ref, back_cq_ref, query_ref, back_two_ref, unit_ref, scale_ref, norms_ref, outer_ref, *refs
):
    if sending:
        normed_ref, mixed_ref, feed_norms_ref, enc_ref, back_k_ref, back_v_ref, key_ref, value_ref, *refs = refs
        back_ref, low_ref, back_mixed_ref, grads_ref, query_send_ref, outer_send_ref, *refs = refs
        norm_keep_ref, norm_send_ref, key_send_ref, value_send_ref, even_ref, odd_ref, pieces_ref = refs
    else:
        back_ref, low_ref, back_mixed_ref, grads_ref = refs
    total = back_two_ref[...] + dot_nt(back_cq_ref[...], query_ref[...])
    back, gain_grad, shift_grad = norm_backward(unit_ref[...], scale_ref[...], norms_ref[0:1, :], total)
    back_ref[...] = back
    low_ref[...] = back.astype(bf16)
    grads_ref[0:1, :] = gain_grad[None]
    grads_ref[1:2, :] = shift_grad[None]
    back_mixed_ref[...] = dot_nt(low_ref[...], outer_ref[...]).astype(bf16)
    if sending:
        for left, right, out in ((normed_ref, back_cq_ref, query_send_ref), (mixed_ref, low_ref, outer_send_ref)):
            out[...] = dot_tn(core_columns(left, 1 - core_ref[0], sending), right[...]).astype(bf16)
        width = back.shape[1]
        pieces = pieces_ref.shape[0] // 16
        part = width // pieces
        vectors = jnp.concatenate(
            [gain_grad[None], shift_grad[None], feed_norms_ref[...], jnp.zeros((16 - 6, width), f32)], axis=0
        )
        pick_row = lax.broadcasted_iota(jnp.int32, (pieces * 16, 16), 0)
        pick_col = lax.broadcasted_iota(jnp.int32, (pieces * 16, 16), 1)
        pick = jnp.where(lax.rem(pick_row, 16) == pick_col, 1.0, 0.0).astype(bf16)
        wide = dot_nn(pick, vectors.astype(bf16))
        piece = lax.broadcasted_iota(jnp.int32, wide.shape, 0) // 16
        column = lax.broadcasted_iota(jnp.int32, wide.shape, 1) // part
        wide = jnp.where(piece == column, wide, 0.0).astype(bf16)
        copy_row = lax.broadcasted_iota(jnp.int32, (width, LANE), 0)
        copy_col = lax.broadcasted_iota(jnp.int32, (width, LANE), 1)
        copy = jnp.where(lax.rem(copy_row, part) == copy_col, 1.0, 0.0).astype(bf16)
        pieces_ref[...] = dot_nn(wide, copy).astype(bf16)
        norm_keep_ref[...] = jnp.zeros(norm_keep_ref.shape, bf16)
        norm_send_ref[...] = jnp.zeros(norm_send_ref.shape, bf16)
        size = pieces * 16 // (2 * sending)
        for step in range(sending):
            for out, which in ((norm_keep_ref, core_ref[0]), (norm_send_ref, 1 - core_ref[0])):
                start = pl.multiple_of((2 * step + which) * size, size)
                out[step * size : (step + 1) * size, :LANE] = pieces_ref[pl.ds(start, size), :]
        columns = core_columns(enc_ref, 1 - core_ref[0], sending)
        key_send_ref[...] = dot_tn(columns, back_k_ref[...]).astype(bf16)
        value_send_ref[...] = dot_tn(columns, back_v_ref[...]).astype(bf16)
        pair_tiles(back_k_ref, back_v_ref, key_ref, value_ref, even_ref, odd_ref)


def pair_tiles(back_k_ref, back_v_ref, key_ref, value_ref, even_ref, odd_ref):
    half = even_ref.shape[1]

    def fill(tile, carry):
        rows = pl.ds(pl.multiple_of(tile * 2 * half, 2 * half), 2 * half)
        total = dot_nt(back_k_ref[rows, :], key_ref[...]) + dot_nt(back_v_ref[rows, :], value_ref[...])
        even_ref[tile] = total[:half].astype(bf16)
        odd_ref[tile] = total[half:].astype(bf16)
        return carry

    lax.fori_loop(0, even_ref.shape[0], fill, 0)


def middle_backward(
    back_cq, query, back_two, unit, scale, norms, outer, core, steps, sending=()
):
    rows, width = back_two.shape
    low = shaped((rows, width), bf16)
    out_shape = [shaped((rows, width), f32), low, low, shaped((2, width), f32)]
    inputs = [back_cq, query, back_two, unit, scale, norms, outer]
    if sending:
        half = shaped((width // 2, width), bf16)
        pair = shaped((4, sending[3].shape[0] // 8, width), bf16)
        out_shape += [half, half] + [shaped((16 * 4 * steps, width), bf16)] * 2 + [half, half, pair, pair]
        inputs += sending
    vmem = pl.BlockSpec(memory_space=pltpu.VMEM)
    return pl.pallas_call(
        functools.partial(middle_kernel, steps if sending else 0),
        in_specs=[SMEM_SPEC] + [vmem] * len(inputs),
        out_specs=[vmem] * len(out_shape),
        out_shape=out_shape,
        scratch_shapes=[pltpu.VMEM((16 * 8 * steps, LANE), bf16)] if sending else [],
        compiler_params=params(),
        cost_estimate=SMALL,
        name="middle_backward",
    )(core, *inputs)


def pair_rows_kernel(tiles, back_k_ref, back_v_ref, key_ref, value_ref, even_ref, odd_ref, *rest):
    total = dot_nt(back_k_ref[...], key_ref[...]) + dot_nt(back_v_ref[...], value_ref[...])
    half = even_ref.shape[1]
    step = pl.program_id(0)

    @pl.when(step < tiles)
    def _():
        even_ref[0] = total[:half].astype(bf16)
        odd_ref[0] = total[half:].astype(bf16)

    if rest:

        @pl.when(step >= tiles)
        def _():
            rest[0][...] = total


def pair_rows(back_k, back_v, key, value, pieces, piece_rows):
    count, width = back_k.shape[0], key.shape[0]
    tile = 2 * piece_rows
    tiles = pieces // 2
    steps = count // tile
    resident = lambda array: pl.BlockSpec(array.shape, lambda t: (0, 0), pipeline_mode=pl.Buffered(1))
    rows = pl.BlockSpec((tile, back_k.shape[1]), lambda t: (t, 0))
    part = pl.BlockSpec((1, piece_rows, width), lambda t: (jnp.minimum(t, tiles - 1), 0, 0))
    out_specs, out_shape = [part, part], [shaped((tiles, piece_rows, width), bf16)] * 2
    if steps > tiles:
        out_specs.append(pl.BlockSpec((tile, width), lambda t: (jnp.maximum(t - tiles, 0), 0)))
        out_shape.append(shaped((count - tiles * tile, width), f32))
    return pl.pallas_call(
        functools.partial(pair_rows_kernel, tiles),
        grid=(steps,),
        in_specs=[rows, rows, resident(key), resident(value)],
        out_specs=out_specs,
        out_shape=out_shape,
        compiler_params=params(),
        cost_estimate=SMALL,
        name="pair_rows",
    )(back_k, back_v, key, value)


def last_kernel(
    steps, core_ref, x_ref, keyed_ref, back_ref, back_q_ref, back_e_ref, back_k_ref, back_v_ref,
    query_ref, relative_ref, key_ref, value_ref,
    key_send_ref, value_send_ref, query_send_ref, embed_send_ref, even_ref, odd_ref, out_ref,
):
    columns = core_columns(keyed_ref, 1 - core_ref[0], steps)
    key_send_ref[...] = dot_tn(columns, back_k_ref[...]).astype(bf16)
    value_send_ref[...] = dot_tn(columns, back_v_ref[...]).astype(bf16)
    columns = core_columns(x_ref, 1 - core_ref[0], steps)
    query_send_ref[...] = dot_tn(columns, back_q_ref[...]).astype(bf16)
    embed_send_ref[...] = dot_tn(columns, back_e_ref[...]).astype(bf16)
    pair_tiles(back_k_ref, back_v_ref, key_ref, value_ref, even_ref, odd_ref)
    main = even_ref.shape[0] * 2 * even_ref.shape[1]
    skip = out_ref.shape[0] - (back_k_ref.shape[0] - main)
    total = back_ref[...] + dot_nt(back_q_ref[...], query_ref[...]) + dot_nt(back_e_ref[...], relative_ref[...])
    out_ref[:skip, :] = total[:skip]
    lanes = dot_nt(back_k_ref[main:, :], key_ref[...]) + dot_nt(back_v_ref[main:, :], value_ref[...])
    out_ref[skip:, :] = total[skip:] + lanes


def last_backward(x, keyed, back, back_q, back_e, back_k, back_v, query, relative, key, value, core, steps, pieces):
    width = x.shape[1]
    half = shaped((width // 2, width), bf16)
    pair = shaped((pieces // 2, x.shape[0] // 3, width), bf16)
    out_shape = [half, half, half, shaped((width // 2, back_e.shape[1]), bf16), pair, pair, shaped(back.shape, f32)]
    vmem = pl.BlockSpec(memory_space=pltpu.VMEM)
    return pl.pallas_call(
        functools.partial(last_kernel, steps),
        in_specs=[SMEM_SPEC] + [vmem] * 11,
        out_specs=[vmem] * len(out_shape),
        out_shape=out_shape,
        compiler_params=params(),
        cost_estimate=SMALL,
        name="last_backward",
    )(core, x, keyed, back, back_q, back_e, back_k, back_v, query, relative, key, value)


def after(value, *others):
    return lax.optimization_barrier((value,) + others)[0]


def tie(*values):
    return lax.optimization_barrier(values)


def ctx_hop(array, bit):
    size = lax.axis_size("ctx")
    return lax.ppermute(array, "ctx", [(i, i ^ bit) for i in range(size)])


def z_hop(array, step):
    size = lax.axis_size("fsdp")
    return lax.ppermute(array, "fsdp", [(i, (i + step) % size) for i in range(size)])


def first_spread(array):
    return array, ctx_hop(array, XBIT), ctx_hop(array, YBIT)


def corner_spread(firsts, axis, cut, *held):
    array, from_x, from_y = firsts
    if held:
        from_x, from_y, *_ = lax.optimization_barrier((from_x, from_y, *held))
    size = array.shape[axis]
    corner_one = ctx_hop(lax.slice_in_dim(from_y, 0, cut, axis=axis), XBIT)
    corner_two = ctx_hop(lax.slice_in_dim(from_x, cut, size, axis=axis), YBIT)
    return [array, from_x, from_y, corner_one, corner_two]


SPREAD_PLAN = tuple(
    (offset + core, part) for core in (0, 1) for offset, part in ((0, 0), (XBIT, 0), (YBIT, 0), (XBIT + YBIT, 1), (XBIT + YBIT, 2))
)


def piece_number(index):
    return (index & 1) * 4 + (index >> 1)


def block_copies(layout):
    copies = []
    row = 0
    for number, (shard_rows, columns) in enumerate(layout):
        piece_rows = shard_rows // 8
        if columns >= 1024:
            for block in range(columns // 1024):
                copies.append((row, piece_rows, 0, 1024, number, 0, block * 1024))
                row += piece_rows
        else:
            parts = 1024 // columns
            rows = piece_rows // parts
            for part in range(parts):
                copies.append((row, rows, part * columns, columns, number, part * rows, 0))
            row += rows
    return tuple(copies), row


def place_copies(copies, cut):
    def chosen(part):
        if part == 0:
            return copies
        if part == 1:
            return tuple(item for item in copies if item[0] < cut)
        return tuple((item[0] - cut,) + item[1:] for item in copies if item[0] >= cut)

    return chosen


def group_loads(layout, copies, cut, steps, place_ref, sources, stages, sems, base=0):
    count = len(layout)
    chosen = place_copies(copies, cut)
    loads = []
    for number, (shard_rows, _) in enumerate(layout):
        target = stages[number]
        if steps > 1:
            start = pl.multiple_of(place_ref[base] * shard_rows, shard_rows)
            target = target.at[pl.ds(start, shard_rows), :]
        loads.append((number, pltpu.make_async_copy(sources[number], target, sems.at[number])))
    for arrival, (offset, part) in zip(sources[count:], SPREAD_PLAN):
        for step in range(1, steps):
            for row, rows, col, cols, number, prow, wcol in chosen(part):
                shard_rows = layout[number][0]
                start = place_ref[base + step] * shard_rows
                start = start + place_ref[base + steps + offset] * (shard_rows // 8) + prow
                source = arrival.at[step - 1, pl.ds(row, rows), pl.ds(col, cols)]
                target = stages[number].at[pl.ds(pl.multiple_of(start, 16), rows), pl.ds(wcol, cols)]
                loads.append((number, pltpu.make_async_copy(source, target, sems.at[number])))
    return loads


def place_of(z_index, c_index, steps):
    return jnp.stack(
        [(z_index - step) % steps for step in range(steps)] + [piece_number(c_index ^ j) for j in range(8)]
    ).astype(jnp.int32)


def project_kernel(layout, copies, cut, steps, products, pieces, tail, place_ref, *refs):
    count = len(layout)
    number_in = count + len(SPREAD_PLAN)
    own_ref, refs = (refs[0], refs[1:]) if tail else (None, refs)
    parts, sources, refs = refs[:pieces], refs[pieces : pieces + number_in], refs[pieces + number_in :]
    outs, refs = refs[: len(products)], refs[len(products) :]
    rows_out, weights_out, refs = refs[0], refs[1 : 1 + count], refs[1 + count :]
    rows_ref, stages, sems, row_sem, out_sem = refs[0], refs[1 : 1 + count], refs[-3], refs[-2], refs[-1]
    step = pl.program_id(0)
    piece_rows = parts[0].shape[0]

    def stores():
        moves = [pltpu.make_async_copy(rows_ref, rows_out, out_sem.at[count])]
        return moves + [pltpu.make_async_copy(stages[i], weights_out[i], out_sem.at[i]) for i in range(count)]

    @pl.when(step == 0)
    def _():
        loads = [
            pltpu.make_async_copy(part, rows_ref.at[pl.ds(j * piece_rows, piece_rows), :], row_sem)
            for j, part in enumerate(parts)
        ]
        loads += [load for _, load in group_loads(layout, copies, cut, steps, place_ref, sources, stages, sems)]
        for load in loads:
            load.start()
        if tail:
            rows_ref[pieces * piece_rows :, :] = own_ref[piece_rows:, :]
        for load in loads:
            load.wait()
        for move in stores():
            move.start()

    for out, (from_rows, number) in zip(outs, products):
        block = out.shape[1]
        cols = pl.ds(pl.multiple_of(step * block, LANE), block)
        left = rows_ref[...] if from_rows else own_ref[...]
        out[...] = dot_nn(left, stages[number][:, cols]).astype(bf16)

    @pl.when(step == pl.num_programs(0) - 1)
    def _():
        for move in stores():
            move.wait()


def project(own, parts, weights, arrivals, layout, cut, products, place, steps):
    copies, _ = block_copies(layout)
    count = len(layout)
    piece_rows, width = parts[0].shape
    rows = piece_rows * len(parts) + (own.shape[0] - piece_rows if own is not None else 0)
    blocks = 4
    hbm = pl.BlockSpec(memory_space=pl.ANY)
    first = [] if own is None else [own]
    shapes = [(shard_rows * steps, columns) for shard_rows, columns in layout]
    out_shape, out_specs = [], []
    for from_rows, number in products:
        left_rows = rows if from_rows else own.shape[0]
        out_shape.append(shaped((left_rows, shapes[number][1]), bf16))
        out_specs.append(pl.BlockSpec((left_rows, shapes[number][1] // blocks), lambda t: (0, t)))
    out_shape += [shaped((rows, width), bf16)] + [shaped(item, bf16) for item in shapes]
    outs = pl.pallas_call(
        functools.partial(project_kernel, layout, copies, cut, steps, products, len(parts), own is not None),
        grid=(blocks,),
        in_specs=[SMEM_SPEC]
        + [pl.BlockSpec(item.shape, lambda t: (0, 0), pipeline_mode=pl.Buffered(1)) for item in first]
        + [hbm] * (len(parts) + len(weights) + len(arrivals)),
        out_specs=out_specs + [hbm] * (1 + count),
        out_shape=out_shape,
        scratch_shapes=[pltpu.VMEM((rows, width), bf16)]
        + [pltpu.VMEM(item, bf16) for item in shapes]
        + [pltpu.SemaphoreType.DMA((count,)), pltpu.SemaphoreType.DMA, pltpu.SemaphoreType.DMA((count + 1,))],
        compiler_params=params(),
        cost_estimate=SMALL,
        name="project",
    )(place, *first, *parts, *weights, *arrivals)
    return outs[: len(products)], outs[len(products)], outs[len(products) + 1 :]


def query_kernel(norm_count, x_ref, mixed_ref, outer_ref, query_ref, vectors_ref, total_ref, unit_ref, scale_ref, low_ref, out_ref, norms_ref):
    pieces = vectors_ref.shape[0] // 16
    width = x_ref.shape[1]
    part = width // pieces
    copy_row = lax.broadcasted_iota(jnp.int32, (LANE, width), 0)
    copy_col = lax.broadcasted_iota(jnp.int32, (LANE, width), 1)
    copy = jnp.where(copy_row == lax.rem(copy_col, part), 1.0, 0.0).astype(bf16)
    wide = dot_nn(vectors_ref[...], copy)
    piece = lax.broadcasted_iota(jnp.int32, wide.shape, 0) // 16
    column = lax.broadcasted_iota(jnp.int32, wide.shape, 1) // part
    wide = jnp.where(piece == column, wide, 0.0).astype(bf16)
    pick_row = lax.broadcasted_iota(jnp.int32, (16, pieces * 16), 0)
    pick_col = lax.broadcasted_iota(jnp.int32, (16, pieces * 16), 1)
    pick = jnp.where(pick_row == lax.rem(pick_col, 16), 1.0, 0.0).astype(bf16)
    norms_ref[...] = dot_nn(pick, wide)
    unit, scale = norm_parts(x_ref[...].astype(f32) + dot_nn(mixed_ref[...], outer_ref[...]))
    total = unit * norms_ref[0:1, :] + norms_ref[1:2, :]
    unit_ref[...] = unit
    scale_ref[...] = scale
    total_ref[...] = total
    low_ref[...] = total.astype(bf16)
    out_ref[...] = dot_nn(low_ref[...], query_ref[...]).astype(bf16)


def query_rows(x, mixed, outer, query, vectors, norm_count):
    rows, width = x.shape
    full = lambda array: pl.BlockSpec(array.shape, lambda t: (0, 0))
    wide, low = shaped((rows, width), f32), shaped((rows, width), bf16)
    outs = [wide, wide, shaped((rows, 1), f32), low, low, shaped((16, width), f32)]
    return pl.pallas_call(
        functools.partial(query_kernel, norm_count),
        grid=(1,),
        in_specs=[full(x), full(mixed), full(outer), full(query), pl.BlockSpec((vectors.shape[0], LANE), lambda t: (0, 0))],
        out_specs=[full(item) for item in outs],
        out_shape=outs,
        compiler_params=params(),
        cost_estimate=SMALL,
        name="query_rows",
    )(x, mixed, outer, query, vectors)


def pieces_kernel(layouts, plans, place_ref, *refs):
    count = sum(len(layout) for layout in layouts)
    weights, outs, sem = refs[:count], refs[count:-1], refs[-1]
    moves = []
    first = 0
    for layout, copies, out in zip(layouts, plans, outs):
        for row, rows, col, cols, number, prow, wcol in copies:
            start = pl.multiple_of(place_ref[0] * (layout[number][0] // 8) + prow, 16)
            source = weights[first + number].at[pl.ds(start, rows), pl.ds(wcol, cols)]
            moves.append(pltpu.make_async_copy(source, out.at[pl.ds(row, rows), pl.ds(col, cols)], sem))
        first += len(layout)
    for move in moves:
        move.start()
    for move in moves:
        move.wait()


def own_pieces(groups, layouts, c_index):
    plans = [block_copies(layout) for layout in layouts]
    weights = [w for group in groups for w in group]
    return pl.pallas_call(
        functools.partial(pieces_kernel, layouts, [plan[0] for plan in plans]),
        in_specs=[SMEM_SPEC] + [pl.BlockSpec(memory_space=pl.ANY)] * len(weights),
        out_specs=[pl.BlockSpec(memory_space=pltpu.VMEM)] * len(groups),
        out_shape=[shaped((plan[1], 1024), bf16) for plan in plans],
        scratch_shapes=[pltpu.SemaphoreType.DMA],
        compiler_params=params(),
        cost_estimate=SMALL,
        name="own_pieces",
    )(piece_number(c_index).astype(jnp.int32).reshape(1), *weights)


def stack_kernel(count, *refs):
    out, sem = refs[count], refs[count + 1]
    moves = [pltpu.make_async_copy(refs[i], out.at[i], sem) for i in range(count)]
    for move in moves:
        move.start()
    for move in moves:
        move.wait()


def stack_rows(items):
    return pl.pallas_call(
        functools.partial(stack_kernel, len(items)),
        in_specs=[pl.BlockSpec(memory_space=pl.ANY)] * len(items),
        out_specs=pl.BlockSpec(memory_space=pltpu.VMEM),
        out_shape=shaped((len(items),) + items[0].shape, items[0].dtype),
        scratch_shapes=[pltpu.SemaphoreType.DMA],
        compiler_params=params(),
        cost_estimate=SMALL,
        name="stack_rows",
    )(*items)


def z_spread(mine):
    return [z_hop(mine, step) for step in range(1, lax.axis_size("fsdp"))]


def core_columns(ref, which, steps):
    block = ref.shape[1] // (2 * steps)
    parts = [ref[:, pl.ds(pl.multiple_of((2 * step + which) * block, block), block)] for step in range(steps)]
    return jnp.concatenate(parts, axis=1)


def fold_grads_kernel(groups, steps, extra_rows, plain_rows, place_ref, *refs):
    count = len(groups)
    half = steps // 2
    lefts, refs = refs[: max(groups) + 1], refs[max(groups) + 1 :]
    rights, arrivals, refs = refs[:count], refs[count : 2 * count], refs[2 * count :]
    if extra_rows:
        extra_keep, extra_got, refs = refs[0], refs[1], refs[2:]
    if plain_rows:
        plain_keep, plain_got, refs = refs[0], refs[1], refs[2:]
    outs, work = refs[:8], refs[8:]
    step = pl.program_id(0)

    for number, group in enumerate(groups):
        work[number][...] = dot_tn(lefts[group][...], rights[number][...])
    for first_x in (True, False):

        @pl.when((step < half) if first_x else (step >= half))
        def _(first_x=first_x):
            some = outs[:4] if first_x else outs[4:]
            for offset in range(4):
                y_bit, x_bit = offset >> 1, offset & 1
                on, other = (x_bit, y_bit) if first_x else (y_bit, x_bit)
                out = some[2 * (1 - on) + other]
                yx = place_ref[1] ^ offset
                row = extra_rows
                if extra_rows:
                    total = extra_keep[offset, 0].astype(f32) + extra_got[offset, 0].astype(f32)
                    out[0, :extra_rows, :] = total.astype(bf16)
                for number in range(count):
                    piece, columns = arrivals[number].shape[1:]
                    total = work[number][pl.ds(pl.multiple_of(yx * piece, piece), piece), :]
                    total = (total + arrivals[number][yx].astype(f32)).astype(bf16)
                    if columns >= 1024:
                        for block in range(columns // 1024):
                            out[0, row : row + piece, :] = total[:, block * 1024 : (block + 1) * 1024]
                            row += piece
                    else:
                        parts = 1024 // columns
                        low = piece // parts
                        for part in range(parts):
                            out[0, row : row + low, part * columns : (part + 1) * columns] = total[
                                part * low : (part + 1) * low
                            ]
                        row += low
                if plain_rows:
                    total = plain_keep[yx].astype(f32) + plain_got[yx].astype(f32)
                    out[0, row : row + plain_rows, :] = total.astype(bf16)


def fold_grads(pairs, arrivals, extra, plain, place, steps):
    half = steps // 2
    lefts = [left for left, _ in pairs]
    groups = [number for number, (_, rights) in enumerate(pairs) for _ in rights]
    rights = [right for _, some in pairs for right in some]

    def around(t, p):
        return lax.rem(p[0] + t, steps)

    def resident(array):
        return pl.BlockSpec(array.shape, lambda t, p: (0, 0), pipeline_mode=pl.Buffered(1))

    def by_z(array):
        return pl.BlockSpec((4,) + array.shape[1:], lambda t, p: (around(t, p), 0, 0))

    in_specs = [
        pl.BlockSpec((left.shape[0], left.shape[1] // (2 * steps)), lambda t, p: (0, 2 * around(t, p) + p[2]))
        for left in lefts
    ]
    in_specs += [resident(item) for item in rights] + [by_z(item) for item in arrivals]
    total_rows = sum(item.shape[1] * item.shape[2] // 1024 for item in arrivals)
    extra_rows = plain_rows = 0
    if extra is not None:
        extra_rows = extra[0].shape[2]
        in_specs += [pl.BlockSpec((4, 1, extra_rows, 1024), lambda t, p: (0, t, 0, 0))] * 2
    if plain is not None:
        plain_rows = plain[0].shape[1]
        in_specs += [by_z(item) for item in plain]
    total_rows += extra_rows + plain_rows
    a_spec = pl.BlockSpec((1, total_rows, 1024), lambda t, p: (jnp.minimum(t, half - 1), 0, 0))
    b_spec = pl.BlockSpec((1, total_rows, 1024), lambda t, p: (jnp.maximum(t - half, 0), 0, 0))
    return pl.pallas_call(
        functools.partial(fold_grads_kernel, groups, steps, extra_rows, plain_rows),
        grid_spec=pltpu.PrefetchScalarGridSpec(
            num_scalar_prefetch=1,
            grid=(steps,),
            in_specs=in_specs,
            out_specs=[a_spec] * 4 + [b_spec] * 4,
            scratch_shapes=[
                pltpu.VMEM((lefts[group].shape[1] // (2 * steps), right.shape[1]), f32)
                for group, right in zip(groups, rights)
            ],
        ),
        out_shape=[shaped((half, total_rows, 1024), bf16)] * 8,
        compiler_params=params(),
        cost_estimate=SMALL,
        name="fold_grads",
    )(place, *lefts, *rights, *arrivals, *(extra or ()), *(plain or ()))


def unpack_kernel(layout, copies, cut, vectors, place_ref, *refs):
    arrivals = refs[: len(SPREAD_PLAN)]
    outs = refs[len(SPREAD_PLAN) :]
    weights = len(layout) - (1 if vectors else 0)
    chosen = place_copies(copies, cut)
    for arrival, (offset, part) in zip(arrivals, SPREAD_PLAN):
        for row, rows, col, cols, number, prow, wcol in chosen(part):
            piece_rows = layout[number][0] // 8
            if number < weights:
                start = pl.multiple_of(place_ref[offset] * piece_rows + prow, 8)
                target = outs[number]
                target[pl.ds(start, rows), wcol : wcol + cols] = arrival[row : row + rows, col : col + cols].astype(f32)
            else:
                start = pl.multiple_of(place_ref[offset] * piece_rows, 16)
                outs[-1][pl.ds(start, rows), :] = arrival[row : row + rows, :LANE]
    if vectors:
        pieces, width = 8, outs[weights].shape[1]
        part = width // pieces
        copy_row = lax.broadcasted_iota(jnp.int32, (LANE, width), 0)
        copy_col = lax.broadcasted_iota(jnp.int32, (LANE, width), 1)
        copy = jnp.where(copy_row == lax.rem(copy_col, part), 1.0, 0.0).astype(bf16)
        wide = dot_nn(outs[-1][...], copy)
        piece = lax.broadcasted_iota(jnp.int32, wide.shape, 0) // 16
        column = lax.broadcasted_iota(jnp.int32, wide.shape, 1) // part
        wide = jnp.where(piece == column, wide, 0.0).astype(bf16)
        pick_row = lax.broadcasted_iota(jnp.int32, (16, pieces * 16), 0)
        pick_col = lax.broadcasted_iota(jnp.int32, (16, pieces * 16), 1)
        pick = jnp.where(pick_row == lax.rem(pick_col, 16), 1.0, 0.0).astype(bf16)
        whole = dot_nn(pick, wide)
        for index in range(vectors):
            outs[weights + index][...] = whole[index : index + 1, :]


def add_low(a, b):
    return (a.astype(f32) + b.astype(f32)).astype(bf16)


class Reduction:
    def __init__(self, pairs, layout, cut, z_index, c_index):
        self.pairs, self.layout, self.cut, self.c_index = pairs, layout, cut, c_index
        self.steps = lax.axis_size("fsdp")
        self.half = self.steps // 2
        self.copies, self.rows = block_copies(layout)
        self.place = jnp.stack([z_index, c_index >> 1, c_index & 1]).astype(jnp.int32)

    def fold(self, arrivals, extra, plain, *held):
        steps = self.steps
        arrivals = [a.reshape(steps * 4, rows // 8, columns) for a, (rows, columns) in zip(arrivals, self.layout)]
        self.lead = 0
        if extra is not None:
            self.lead = extra[0].shape[1] // steps
            extra = [item.reshape(4, steps, self.lead, 1024) for item in extra]
        place = after(self.place, *held)
        self.folded = list(fold_grads(self.pairs, arrivals, extra, plain, place, steps))

    def first_hops(self, part):
        return ctx_hop(self.folded[part], XBIT), ctx_hop(self.folded[4 + part], YBIT)

    def second_sums(self, got_x, got_y):
        self.sums = add_low(self.folded[3], got_x), add_low(self.folded[7], got_y)

    def second_hops(self):
        return ctx_hop(self.sums[0], YBIT), ctx_hop(self.sums[1], XBIT)

    def z_sums(self, got_x, got_y, late_x, late_y):
        done = []
        for keep, got, late in ((self.folded[2], got_x, late_x), (self.folded[6], got_y, late_y)):
            for kk in range(self.half):
                done.append(keep[kk].astype(f32) + got[kk].astype(f32) + late[kk].astype(f32))
        self.extra = [item[: self.lead] for item in done]
        self.terms = [item[self.lead :] for item in done]
        self.total = self.terms[-1].astype(bf16)

    def z_step(self, step, got=None):
        if got is not None:
            self.total = (self.terms[self.steps - step].astype(f32) + got.astype(f32)).astype(bf16)
        return z_hop(self.total, 1)

    def z_end(self, got):
        self.total = (self.terms[0] + got.astype(f32)).astype(bf16)

    def spread(self):
        self.near = list(first_spread(self.total))
        return self.near[1:]

    def corners(self, from_x, from_y):
        self.near = corner_spread([self.near[0], from_x, from_y], 0, self.cut)
        return self.near[3:]

    def grads(self, arrivals, vectors=0):
        place = jnp.stack([piece_number(self.c_index ^ j) for j in range(8)]).astype(jnp.int32)
        vmem = pl.BlockSpec(memory_space=pltpu.VMEM)
        out_shape = [shaped((rows, columns), f32) for rows, columns in self.layout]
        if vectors:
            out_shape[-1:] = [shaped((1, self.layout[0][0]), f32)] * vectors
        return pl.pallas_call(
            functools.partial(unpack_kernel, self.layout, self.copies, self.cut, vectors),
            in_specs=[SMEM_SPEC] + [vmem] * len(arrivals),
            out_specs=[vmem] * len(out_shape),
            out_shape=out_shape,
            scratch_shapes=[pltpu.VMEM((128, LANE), bf16)] if vectors else [],
            compiler_params=params(),
            cost_estimate=SMALL,
            name="unpack",
        )(place, *arrivals)

    def extra_sum(self):
        return jnp.concatenate(self.extra, axis=0)


def on_device(
    hidden, encoder_out, out_grad, slot_len, enc_len, rel_bucket,
    query_weight, key_weight, value_weight, relative_weight, output_weight, self_norm_gain, self_norm_shift,
    cross_query_weight, cross_key_weight, cross_value_weight, cross_output_weight, cross_norm_gain,
    cross_norm_shift, up_weight, down_weight, feed_norm_gain, feed_norm_shift,
):
    lanes, slots, halves, half_rows, width = hidden.shape
    rows = halves * half_rows
    enc_rows = encoder_out.shape[1]
    ctx_count = lax.axis_size("ctx")
    steps = lax.axis_size("fsdp")
    z_index = lax.axis_index("fsdp")
    c_index = lax.axis_index("ctx")
    seq_len = ctx_count * rows
    all_rows = lanes * slots * rows
    slab = (lanes, slots, rows, width)
    paired = ctx_count == 8 and steps == 4 and query_weight.shape[0] % 256 == 0 and width == 1024
    paired = paired and enc_rows == rows

    norms = jnp.stack(
        [self_norm_gain, self_norm_shift, cross_norm_gain, cross_norm_shift, feed_norm_gain, feed_norm_shift]
    )
    norm_count, norm_shard = norms.shape

    self_set = (query_weight, relative_weight, key_weight, value_weight)
    cross_set = (output_weight, cross_query_weight, cross_key_weight, cross_value_weight, cross_output_weight)
    feed_set = (up_weight, down_weight)
    layouts = [tuple(w.shape for w in group) for group in (self_set, cross_set, feed_set)]
    x_all = hidden.reshape(all_rows, width)
    x_rows = hidden.reshape(slab)
    if paired:
        cuts = (48, 96, 128)
        where = place_of(z_index, c_index, steps)
        main, enc = x_all[: slots * rows], encoder_out.reshape(slots * rows, width)
        (piece,) = own_pieces((self_set,), layouts[:1], c_index)
        ring = [z_hop(piece, 1)]
        main_x, enc_x = ctx_hop(main, XBIT), ctx_hop(enc, XBIT)
        main_y, enc_y = ctx_hop(main, YBIT), ctx_hop(enc, YBIT)
        vectors = norms.reshape(norm_count, 8, norm_shard // 8).transpose(1, 0, 2)
        vectors = jnp.pad(vectors, ((0, 0), (0, 16 - norm_count), (0, 1024 - norm_shard // 8))).reshape(128, 1024)
        second_set = (*cross_set, vectors)
        second_layout = layouts[1] + (vectors.shape,)
        second_piece, feed_piece = own_pieces((second_set, feed_set), (second_layout, layouts[2]), c_index)
        held, main_x, main_y, enc_x, enc_y = tie(ring[0], main_x, main_y, enc_x, enc_y)
        ring.append(z_hop(held, 1))
        main_corner, enc_corner = ctx_hop(main_y, XBIT), ctx_hop(enc_x, YBIT)
        main_far, enc_far = [ctx_hop(main, CORE)], [ctx_hop(enc, CORE)]
        held, main_corner, enc_corner, main_far[0], enc_far[0] = tie(
            ring[1], main_corner, enc_corner, main_far[0], enc_far[0]
        )
        ring.append(z_hop(held, 1))
        main_far += [ctx_hop(main_x, CORE), ctx_hop(main_y, CORE)]
        enc_far += [ctx_hop(enc_x, CORE), ctx_hop(enc_y, CORE)]
        last, main_far[1], main_far[2], enc_far[1], enc_far[2] = tie(
            ring[2], main_far[1], main_far[2], enc_far[1], enc_far[2]
        )
        first_stack = stack_rows([*ring[:2], last])
        main_far.append(ctx_hop(main_corner, CORE))
        enc_far.append(ctx_hop(enc_corner, CORE))
        main_parts = [item for pair in zip([main, main_x, main_y, main_corner], main_far) for item in pair]
        enc_parts = [item for pair in zip([enc, enc_x, enc_y, enc_corner], enc_far) for item in pair]

        ring = [z_hop(after(second_piece, first_stack), 1)]
        near = list(first_spread(first_stack))
        held, near[1], near[2], main_parts[7], enc_parts[7] = tie(ring[0], near[1], near[2], main_parts[7], enc_parts[7])
        ring.append(z_hop(held, 1))
        near = corner_spread(near, 1, cuts[0])
        far = [ctx_hop(near[0], CORE), ctx_hop(near[1], CORE)]
        held, *near[2:], far[0], far[1] = tie(ring[1], *near[2:], far[0], far[1])
        ring.append(z_hop(held, 1))
        far += [ctx_hop(item, CORE) for item in near[2:]]
        (q, e, k, v), keyed_flat, first = project(
            x_all, main_parts, self_set, near + far, layouts[0], cuts[0],
            ((False, 0), (False, 1), (True, 2), (True, 3)), where, steps,
        )
        second_stack = stack_rows(tie(*ring, q)[: steps - 1])
        second_near = list(first_spread(second_stack))
        feed_ring = [z_hop(after(feed_piece, second_stack), 1)]
        k = after(k, second_stack)
        peers = [c_index ^ j for j in range(8)]
    else:
        norms = lax.all_gather(norms, "fsdp", axis=1, tiled=True)
        gather = lambda w: lax.all_gather(w, "fsdp", axis=0, tiled=True)
        first, second, third = [[gather(w) for w in group] for group in (self_set, cross_set, feed_set)]
        peers = [jnp.int32(j) for j in range(ctx_count)]
        main = lax.all_gather(x_rows[0], "ctx", axis=0)
        keyed_flat = jnp.concatenate([main, x_rows[1:]], axis=0).reshape(-1, width)
        enc_flat = lax.all_gather(encoder_out, "ctx", axis=0).reshape(-1, width)
        q, e = matmul(x_all, first[0]).astype(bf16), matmul(x_all, first[1]).astype(bf16)
        k, v = matmul(keyed_flat, first[2]).astype(bf16), matmul(keyed_flat, first[3]).astype(bf16)
        ck, cv = matmul(enc_flat, second[2]).astype(bf16), matmul(enc_flat, second[3]).astype(bf16)
    query_full, relative_full, key_full, value_full = first

    place = jnp.stack(peers).astype(jnp.int32)
    local = jnp.arange(half_rows, dtype=jnp.int32)

    def both_halves(start):
        return jnp.concatenate([start + local, seq_len - 1 - start - local])

    positions = both_halves(c_index * half_rows)
    key_positions = jnp.concatenate([both_halves(place[j] * half_rows) for j in range(ctx_count)])
    enc_positions = (place[:, None] * enc_rows + jnp.arange(enc_rows, dtype=jnp.int32)[None, :]).reshape(1, -1)
    levels = jnp.arange(BUCKETS + 1, dtype=jnp.int32)
    bounds = jnp.sum((rel_bucket[None, :] < levels[:, None]).astype(jnp.int32), axis=1)

    q, e = q.reshape(slab), e.reshape(lanes, slots, rows, -1)
    k, v = k.reshape(-1, slots, rows, width), v.reshape(-1, slots, rows, width)
    self_inputs = (slot_len, bounds, positions[:, None], key_positions[None])
    made = self_forward(*self_inputs, q, e, k, v, 0, 2)
    q_late = q
    if paired:
        held, q_late, _ = tie(feed_ring[0], q, made[0])
        feed_ring.append(z_hop(held, 1))
    o, probs, own = self_forward(*self_inputs, q_late, e, k, v, 1, 2, made)
    o_flat = o.reshape(all_rows, width)
    if paired:
        second_near[1], second_near[2], held, _ = tie(second_near[1], second_near[2], feed_ring[1], o)
        feed_ring.append(z_hop(held, 1))
        second_near = corner_spread(second_near, 1, cuts[1])
        second_far = [ctx_hop(second_near[0], CORE)]
        feed_ring[2], *second_near[1:], second_far[0] = tie(feed_ring[2], *second_near[1:], second_far[0])
        second_far += [ctx_hop(item, CORE) for item in second_near[1:]]
        third_stack = stack_rows(tie(*feed_ring, *second_far[2:])[: steps - 1])
        third_near = list(first_spread(third_stack))
        (ck, cv), enc_flat, second = project(
            None, enc_parts, second_set, second_near + second_far, second_layout, cuts[1],
            ((True, 2), (True, 3)), after(where, third_stack), steps,
        )
        output_full, cquery_full, ckey_full, cvalue_full, coutput_full, vectors = second
        normed_one, unit_one, scale_one, normed_one_low, cq, norms = query_rows(
            x_all, o_flat, output_full, cquery_full, vectors, norm_count
        )
    else:
        output_full, cquery_full, ckey_full, cvalue_full, coutput_full = second
        norms = norms.astype(f32)
        resid_one = x_all.astype(f32) + matmul(o_flat, output_full)
        normed_one, unit_one, scale_one = norm_forward(resid_one, norms[0:1], norms[1:2])
        normed_one_low = normed_one.astype(bf16)
        cq = matmul(normed_one_low, cquery_full).astype(bf16)

    enc_shape = (ctx_count, slots, enc_rows, width)
    cq, ck, cv = cq.reshape(slab), ck.reshape(enc_shape), cv.reshape(enc_shape)
    oc, cprobs = cross_forward(enc_len, enc_positions, cq, ck, cv)
    oc_flat = oc.reshape(all_rows, width)

    core = (c_index & 1).astype(jnp.int32).reshape(1)

    def reduction(pairs, index, *more):
        return Reduction(pairs, layouts[index] + more, cuts[index], z_index, c_index)

    far = lambda *items: [ctx_hop(item, CORE) for item in items]

    row_valid = (positions[None, None, :] < slot_len[None, :, None]).astype(f32)
    row_valid = jnp.broadcast_to(row_valid, (lanes, slots, rows)).reshape(all_rows, 1)
    if paired:
        third_near[1], third_near[2], _ = tie(third_near[1], third_near[2], oc_flat)
        third_near = corner_spread(third_near, 1, cuts[2])
        third_far = [ctx_hop(item, CORE) for item in third_near[:3]]
        third_near[3], third_near[4], *third_far = tie(third_near[3], third_near[4], *third_far)
        third_far += [ctx_hop(item, CORE) for item in third_near[3:]]
        third = third_near + third_far
        feed_inputs = (feed_set, third, layouts[2], cuts[2], jnp.concatenate([core, where]))
    else:
        feed_inputs = (third, (), tuple(w.shape for w in third), 0, core)
    layer_out, normed_two_low, act_low, back_pre, back_feed, back_two, back_cross, back_oc, feed_norms, *sent = (
        feed_forward_backward(
            normed_one, oc_flat, coutput_full, norms, out_grad.reshape(all_rows, width), row_valid, *feed_inputs, steps, paired
        )
    )
    if paired:
        sent_up, sent_down, sent_coutput = sent
        third_sum = reduction([(normed_two_low, [back_pre]), (act_low, [back_feed])], 2)
        far_feed = far(sent_up, sent_down, sent_coutput)
    back_cq, back_ck, back_cv = cross_backward(cprobs, back_oc.reshape(slab), cq, ck, cv)
    back_cq = back_cq.reshape(all_rows, width)
    back_ck = back_ck.reshape(-1, width)
    back_cv = back_cv.reshape(-1, width)
    sending = ()
    if paired:
        *far_feed, back_cq = tie(*far_feed, back_cq)
        third_sum.fold(far_feed[:2], None, None, back_cq)
        third_first = third_sum.first_hops(1)
        back_cq = after(back_cq, third_sum.folded[0])
        sending = (normed_one_low, o_flat, feed_norms, enc_flat, back_ck, back_cv, ckey_full, cvalue_full)
    back_one, back_self, back_o, norm_grads, *sent = middle_backward(
        back_cq, cquery_full, back_two, unit_one, scale_one, norms, output_full, core, steps, sending
    )
    if paired:
        second_sum = reduction(
            [(o_flat, [back_self]), (normed_one_low, [back_cq]), (enc_flat, [back_ck, back_cv]), (oc_flat, [back_cross])],
            1,
            (128, 1024),
        )
        got_x, got_y, back_o, *sent = tie(*third_first, back_o, *sent)
        sent_cquery, sent_output, norm_keep, norm_send, sent_ckey, sent_cvalue, enc_keep, enc_send = sent
        third_sum.second_sums(got_x, got_y)
        third_late = third_sum.second_hops()
        far_some = far(sent_cquery, sent_output, sent_ckey)
        back_o = after(back_o, *third_sum.sums)
    else:
        enc_part = pair_rows(back_ck, back_cv, ckey_full, cvalue_full, ctx_count, slots * enc_rows)
    self_inputs = (bounds, positions[:, None], key_positions[None], probs, own)
    part_one = self_backward(*self_inputs, back_o.reshape(slab), q, k, v, 0, 2)
    if paired:
        late_x, late_y, *far_some, sent_cvalue, norm_send, enc_send, third_sum.folded[0], third_sum.folded[4], _ = tie(
            *third_late, *far_some, sent_cvalue, norm_send, enc_send, third_sum.folded[0], third_sum.folded[4], part_one[0]
        )
        third_got = third_sum.first_hops(0)
        norm_shape = (4 * steps, 16, width)
        far_rest = far(sent_cvalue, norm_send.reshape(norm_shape), enc_send)
        second_sum.fold(
            [far_some[1], far_some[0], far_some[2], far_rest[0], far_feed[2]],
            [enc_keep, far_rest[2]],
            [norm_keep.reshape(norm_shape), far_rest[1]],
        )
        *third_got, second_sum.folded[1], second_sum.folded[5] = tie(
            *third_got, second_sum.folded[1], second_sum.folded[5]
        )
        third_sum.z_sums(*third_got, late_x, late_y)
        hop = third_sum.z_step(1)
        second_first = second_sum.first_hops(1)
        back_o = after(back_o, second_sum.folded[1], third_sum.total)
    back_q, back_k, back_v, back_e = self_backward(*self_inputs, back_o.reshape(slab), q, k, v, 1, 2, part_one)
    back_q = back_q.reshape(all_rows, width)
    back_e = back_e.reshape(all_rows, -1)
    back_k = back_k.reshape(-1, width)
    back_v = back_v.reshape(-1, width)

    if paired:
        first_sum = reduction([(x_all, [back_q, back_e]), (keyed_flat, [back_k, back_v])], 0)
        hop, got_x, got_y, back_q, back_k = tie(hop, *second_first, back_q, back_k)
        hop = third_sum.z_step(2, hop)
        second_sum.second_sums(got_x, got_y)
        second_late = second_sum.second_hops()
        back_q = after(back_q, third_sum.total, *second_sum.sums)
        *sent_first, main_keep, main_send, back_x = last_backward(
            x_all, keyed_flat, back_one, back_q, back_e, back_k, back_v, query_full, relative_full, key_full, value_full,
            core, steps, ctx_count,
        )
        hop, late_x, late_y, main_send, second_sum.folded[0], second_sum.folded[4], *sent_first = tie(
            hop, *second_late, main_send, second_sum.folded[0], second_sum.folded[4], *sent_first
        )
        far_keys, far_values, far_query, far_main = far(*sent_first[:3], main_send)
        far_embed, hop, far_keys = tie(*far(sent_first[3]), hop, far_keys)
        hop = third_sum.z_step(3, hop)
        second_got = second_sum.first_hops(0)
        first_sum.fold([far_query, far_embed, far_keys, far_values], [main_keep, far_main], None, third_sum.total)
        got_x, got_y, hop, first_sum.folded[1], first_sum.folded[5] = tie(
            *second_got, hop, first_sum.folded[1], first_sum.folded[5]
        )
        first_first = first_sum.first_hops(1)
        third_sum.z_end(hop)
        second_sum.z_sums(got_x, got_y, late_x, late_y)
        hop = second_sum.z_step(1)
        hop, got_x, got_y = tie(hop, *first_first)
        first_sum.second_sums(got_x, got_y)
        first_late = first_sum.second_hops()
        first_sum.folded[0], first_sum.folded[4], hop, _ = tie(
            first_sum.folded[0], first_sum.folded[4], hop, first_sum.sums[0]
        )
        first_got = first_sum.first_hops(0)
        hop = second_sum.z_step(2, hop)
        hop, *rest, third_total = tie(hop, *first_got, *first_late, third_sum.total)
        third_sum.total = third_total
        first_sum.z_sums(*rest)
        first_hop = first_sum.z_step(1)
        hop = second_sum.z_step(3, hop)
        main_sum = jnp.concatenate(first_sum.extra, axis=0)
        hidden_grad = jnp.concatenate([back_x[: main_sum.shape[0]] + main_sum, back_x[main_sum.shape[0] :]], axis=0)
        encoder_grad = jnp.concatenate(second_sum.extra, axis=0)
        hop, first_hop, third_x, third_y = tie(hop, first_hop, *third_sum.spread())
        second_sum.z_end(hop)
        first_hop = first_sum.z_step(2, first_hop)
        corners = third_sum.corners(third_x, third_y)
        spread = second_sum.spread()
        first_hop, second_x, second_y, *third_sum.near[1:], hidden_grad = tie(
            first_hop, *spread, third_x, third_y, *corners, hidden_grad
        )
        first_hop = first_sum.z_step(3, first_hop)
        corners = second_sum.corners(second_x, second_y)
        third_far = far(*third_sum.near[1:3])
        first_hop, *second_sum.near[1:], third_far[0], third_far[1], encoder_grad = tie(
            first_hop, second_x, second_y, *corners, *third_far, encoder_grad
        )
        first_sum.z_end(first_hop)
        spread = first_sum.spread()
        more = far(third_sum.near[0], *third_sum.near[3:])
        *more, held = tie(*more, second_sum.near[0])
        third_far = [more[0], *third_far, *more[1:]]
        second_sum.near[0] = held
        second_far = far(*second_sum.near[:3])
        third_grads = third_sum.grads(third_sum.near + third_far)
        first_x, first_y, *second_far = tie(*spread, *second_far)
        corners = first_sum.corners(first_x, first_y)
        second_far += far(*second_sum.near[3:])
        *first_sum.near[1:], second_far[3], second_far[4], _ = tie(first_x, first_y, *corners, *second_far[3:], third_grads[0])
        first_far = far(*first_sum.near)
        outs = second_sum.grads(second_sum.near + second_far, norm_count)
        second_grads, norm_grads = outs[:-norm_count], [item.reshape(norm_shard) for item in outs[-norm_count:]]
        first_grads = first_sum.grads(first_sum.near + first_far)
    else:
        *main_part, other_part = pair_rows(back_k, back_v, key_full, value_full, ctx_count, slots * rows)
        back_x = back_one + matmul_back(back_q, query_full) + matmul_back(back_e, relative_full)
        back_x = jnp.concatenate([back_x[: slots * rows], back_x[slots * rows :] + other_part], axis=0)
        norm_grads = lax.psum(jnp.concatenate([norm_grads, feed_norms], axis=0), ("fsdp", "ctx"))
        norm_grads = lax.dynamic_slice_in_dim(norm_grads, z_index * norm_shard, norm_shard, 1)

        def reduce(left, right):
            shard = lax.psum_scatter(outer_rows(left, right).astype(bf16), "fsdp", scatter_dimension=0, tiled=True)
            return lax.psum(shard, "ctx").astype(f32)

        def scatter(parts):
            whole = jnp.stack(parts, axis=1).reshape(ctx_count, -1, width)
            return lax.psum_scatter(whole, "ctx", scatter_dimension=0, tiled=True).astype(f32).reshape(-1, width)

        first_grads = [
            reduce(x_all, back_q), reduce(x_all, back_e), reduce(keyed_flat, back_k), reduce(keyed_flat, back_v),
        ]
        second_grads = [
            reduce(o_flat, back_self), reduce(normed_one_low, back_cq), reduce(enc_flat, back_ck),
            reduce(enc_flat, back_cv), reduce(oc_flat, back_cross),
        ]
        third_grads = [reduce(normed_two_low, back_pre), reduce(act_low, back_feed)]
        encoder_grad = scatter(enc_part)
        main_sum = scatter(main_part)
        hidden_grad = jnp.concatenate([back_x[: main_sum.shape[0]] + main_sum, back_x[main_sum.shape[0] :]], axis=0)
    out_shape = hidden.shape
    return (
        layer_out.reshape(out_shape), hidden_grad.reshape(out_shape), encoder_grad.reshape(encoder_out.shape),
        first_grads[0], first_grads[2], first_grads[3], first_grads[1], second_grads[0], norm_grads[0], norm_grads[1],
        second_grads[1], second_grads[2], second_grads[3], second_grads[4], norm_grads[2], norm_grads[3],
        third_grads[0], third_grads[1], norm_grads[4], norm_grads[5],
    )


def solution(mesh):
    rows = P("fsdp", None)
    vector = P("fsdp")
    slab = P(None, "fsdp", None, "ctx", None)
    encoder = P("fsdp", "ctx", None)
    weights = (rows,) * 5 + (vector,) * 2 + (rows,) * 4 + (vector,) * 2 + (rows,) * 2 + (vector,) * 2
    return jax.shard_map(
        on_device,
        mesh=mesh,
        in_specs=(slab, encoder, slab, vector, vector, P()) + weights,
        out_specs=(slab, slab, encoder) + weights,
        check_vma=False,
    )
```

```python
import functools

import jax
import jax.numpy as jnp
from jax import lax
from jax.experimental import pallas as pl
from jax.experimental.pallas import tpu as pltpu
from jax.sharding import PartitionSpec as P

HEAD_DIM = 64
BUCKETS = 32
LANE = 128
GROUP = 4
SUB = 8
eps_norm = 1e-05
neg_fill = -1e30
bf16 = jnp.bfloat16
f32 = jnp.float32
CORE, XBIT, YBIT = 1, 2, 4
VMEM_LIMIT = 63 * 1024 * 1024


def matmul(left_side, right_side):
    return jnp.dot(left_side, right_side, preferred_element_type=f32)


def matmul_back(left_side, right_side):
    return lax.dot_general(left_side, right_side, (((1,), (1,)), ((), ())), preferred_element_type=f32)


def outer_rows(left_side, right_side):
    return lax.dot_general(left_side, right_side, (((0,), (0,)), ((), ())), preferred_element_type=f32)


def norm_forward(values, gain, shift):
    row_mean = jnp.mean(values, axis=-1, keepdims=True)
    centered = values - row_mean
    scale = lax.rsqrt(jnp.mean(centered * centered, axis=-1, keepdims=True) + eps_norm)
    unit = centered * scale
    return unit * gain + shift, unit, scale


def norm_backward(unit, scale, gain, cotangent):
    back_unit = cotangent * gain
    first = jnp.mean(back_unit, axis=-1, keepdims=True)
    second = jnp.mean(back_unit * unit, axis=-1, keepdims=True)
    back = scale * (back_unit - first - unit * second)
    return back, jnp.sum(cotangent * unit, axis=0), jnp.sum(cotangent, axis=0)


def dot_nt(left_side, right_side):
    return lax.dot_general(left_side, right_side, (((1,), (1,)), ((), ())), preferred_element_type=f32)


def dot_nn(left_side, right_side):
    return lax.dot_general(left_side, right_side, (((1,), (0,)), ((), ())), preferred_element_type=f32)


def dot_tn(left_side, right_side):
    return lax.dot_general(left_side, right_side, (((0,), (0,)), ((), ())), preferred_element_type=f32)


def stack_heads(pair, low_half):
    zero = jnp.zeros_like(pair)
    return jnp.concatenate([jnp.where(low_half, pair, zero), jnp.where(low_half, zero, pair)], axis=0)


def rows_of(ref, first, last, cols):
    block = ref[first:last, 0, :, cols]
    return block.reshape(block.shape[0] * block.shape[1], block.shape[2])


def fill_one_hot(bucket_ref, one_hot_ref):
    keys = bucket_ref.shape[1]
    levels = lax.broadcasted_iota(jnp.int32, (BUCKETS, keys), 0)

    def fill(row, carry):
        line = jnp.broadcast_to(bucket_ref[pl.ds(row, 1), :], (BUCKETS, keys))
        start = pl.multiple_of(lax.rem(row, SUB) * BUCKETS, BUCKETS)
        one_hot_ref[row // SUB, pl.ds(start, BUCKETS), :] = jnp.where(line == levels, 1.0, 0.0).astype(bf16)
        return carry

    lax.fori_loop(0, bucket_ref.shape[0], fill, 0)


def fill_buckets(distance, bounds_ref, bucket_ref):
    bucket_ref[...] = jnp.zeros(distance.shape, jnp.int32)

    def fill(level, carry):
        bucket_ref[...] += (distance >= bounds_ref[level]).astype(jnp.int32)
        return carry

    lax.fori_loop(1, BUCKETS, fill, 0)


def own_block_mask(rows):
    row = lax.broadcasted_iota(jnp.int32, (rows, SUB * BUCKETS), 0)
    col = lax.broadcasted_iota(jnp.int32, (rows, SUB * BUCKETS), 1)
    return (row & (SUB - 1)) == (col // BUCKETS)


def self_forward_kernel(
    held, base, length_ref, bounds_ref, posq_ref, posk_ref, q_ref, e_ref, k_ref, v_ref, *refs,
):
    o_ref, p_ref, own_ref, bucket_ref, one_hot_ref, spread_ref, bias_ref = refs[held:]
    slot = pl.program_id(0)
    group = pl.program_id(1)
    lanes, _, rows, _ = q_ref.shape
    pieces = k_ref.shape[0] - (lanes - 1)
    keys = pieces * k_ref.shape[2]
    heads = bias_ref.shape[0]
    span = SUB * BUCKETS

    @pl.when((slot == 0) & (group == 0))
    def _():
        fill_buckets(posq_ref[...] - posk_ref[...], bounds_ref, bucket_ref)
        fill_one_hot(bucket_ref, one_hot_ref)

    @pl.when(group == 0)
    def _():
        keep = own_block_mask(lanes * rows)
        source = lax.broadcasted_iota(jnp.int32, (LANE, span), 0)
        target = lax.broadcasted_iota(jnp.int32, (LANE, span), 1) & (BUCKETS - 1)
        for part in range(LANE // BUCKETS):
            copy = jnp.where(source == target + part * BUCKETS, 1.0, 0.0).astype(bf16)
            for block in range(heads * BUCKETS // LANE):
                column = base * GROUP * BUCKETS + block * LANE
                rows_e = rows_of(e_ref, 0, lanes, slice(column, column + LANE))
                head = block * (LANE // BUCKETS) + part
                spread_ref[head] = jnp.where(keep, dot_nn(rows_e, copy), 0.0)
        distance = posq_ref[...] - posk_ref[...]
        valid = posk_ref[...] < length_ref[slot]
        fills = [jnp.where(valid & (distance >= edge), 0.0, neg_fill) for edge in (0, 1)]
        for g in range(rows // SUB):
            starts = [lane * rows + g * SUB for lane in range(lanes)]
            left = [spread_ref[:, start : start + SUB, :].reshape(heads * SUB, span) for start in starts]
            bias = dot_nn(jnp.concatenate(left, axis=0).astype(bf16), one_hot_ref[g])
            bias = bias.reshape(lanes, heads, SUB, keys)
            for lane, start in enumerate(starts):
                fill = fills[min(lane, 1)][None, g * SUB : (g + 1) * SUB, :]
                bias_ref[:, start : start + SUB, :] = bias[lane] + fill

    low_half = lax.broadcasted_iota(jnp.int32, (1, LANE), 1) < HEAD_DIM
    lane_id = lax.broadcasted_iota(jnp.int32, (1, LANE), 1)
    own_all = [jnp.zeros((rows, LANE), f32) for _ in range(lanes)]
    e_cols = pl.ds(pl.multiple_of((base + group) * (GROUP * BUCKETS), LANE), GROUP * BUCKETS)
    tables = [None] + [e_ref[lane, 0, :, e_cols].astype(f32) for lane in range(1, lanes)]
    for pair in range(GROUP // 2):
        cols = slice(pair * LANE, (pair + 1) * LANE)
        q_pair = rows_of(q_ref, 0, lanes, cols) * jnp.asarray(HEAD_DIM**-0.5, bf16)
        k_main = rows_of(k_ref, 0, pieces, cols)
        v_main = rows_of(v_ref, 0, pieces, cols)
        scores = dot_nt(stack_heads(q_pair, low_half), k_main)
        own_pair = []
        for half in range(2):
            head = pair * 2 + half
            keep = low_half if half == 0 else jnp.logical_not(low_half)
            for lane in range(lanes):
                start = (half * lanes + lane) * rows
                part = scores[start : start + rows]
                part = part + bias_ref[group * GROUP + head, lane * rows : (lane + 1) * rows, :]
                top = jnp.max(part, axis=1, keepdims=True)
                if lane > 0:
                    q_row = q_pair[lane * rows : (lane + 1) * rows].astype(f32)
                    k_row = k_ref[pieces + lane - 1, 0, :, cols].astype(f32)
                    own = jnp.sum(jnp.where(keep, q_row * k_row, 0.0), axis=1, keepdims=True)
                    own = own + tables[lane][:, head * BUCKETS : head * BUCKETS + 1]
                    top = jnp.maximum(top, own)
                    own_exp = jnp.exp(own - top)
                terms = jnp.exp(part - top)
                total = jnp.sum(terms, axis=1, keepdims=True)
                if lane > 0:
                    total = total + own_exp
                inverse = 1.0 / total
                p_ref[0, head, lane * rows : (lane + 1) * rows, :] = (terms * inverse).astype(bf16)
                if lane > 0:
                    own_prob = own_exp * inverse
                    own_all[lane] = jnp.where(lane_id == head, own_prob, own_all[lane])
                else:
                    own_prob = jnp.zeros((rows, 1), f32)
                own_pair.append(own_prob)
        p_low = p_ref[0, pair * 2 : pair * 2 + 2].reshape(2 * lanes * rows, keys)
        mixed = dot_nn(p_low, v_main)
        for lane in range(lanes):
            first = lane * rows
            second = (lanes + lane) * rows
            out = jnp.where(low_half, mixed[first : first + rows], mixed[second : second + rows])
            if lane > 0:
                own_prob = jnp.where(low_half, own_pair[lane], own_pair[lanes + lane])
                v_row = v_ref[pieces + lane - 1, 0, :, cols].astype(f32)
                out = out + own_prob.astype(bf16).astype(f32) * v_row
            o_ref[lane, 0, :, cols] = out.astype(bf16)
    for lane in range(lanes):
        own_ref[0, 0, lane * rows : (lane + 1) * rows, :] = own_all[lane]


def self_backward_kernel(
    held, bounds_ref, posq_ref, posk_ref, p_ref, own_ref, do_ref, q_ref, k_ref, v_ref, *refs,
):
    dq_ref, dk_ref, dv_ref, de_ref = refs[held : held + 4]
    bucket_ref, one_hot_ref, turned_ref, scores_ref, down_ref, wide_ref = refs[held + 4 :]
    group = pl.program_id(1)
    lanes, _, rows, _ = q_ref.shape
    pieces = k_ref.shape[0] - (lanes - 1)
    piece_rows = k_ref.shape[2]
    keys = pieces * piece_rows
    scale = HEAD_DIM**-0.5

    heads = scores_ref.shape[0]
    span = SUB * BUCKETS

    @pl.when((pl.program_id(0) == 0) & (group == 0))
    def _():
        fill_buckets(posq_ref[...] - posk_ref[...], bounds_ref, bucket_ref)
        fill_one_hot(bucket_ref, one_hot_ref)
        for g in range(rows // SUB):
            turned_ref[g] = one_hot_ref[g].T

    lane_id = lax.broadcasted_iota(jnp.int32, (1, LANE), 1)
    low_half = lane_id < HEAD_DIM
    downs = [jnp.zeros((rows, LANE), f32) for _ in range(lanes)]
    for pair in range(GROUP // 2):
        cols = slice(pair * LANE, (pair + 1) * LANE)
        q_pair = rows_of(q_ref, 0, lanes, cols) * jnp.asarray(scale, bf16)
        do_pair = rows_of(do_ref, 0, lanes, cols)
        k_main = rows_of(k_ref, 0, pieces, cols)
        v_main = rows_of(v_ref, 0, pieces, cols)
        q_stack = stack_heads(q_pair, low_half)
        do_stack = stack_heads(do_pair, low_half)
        back_probs = dot_nt(do_stack, v_main)
        p_low = p_ref[0, pair * 2 : pair * 2 + 2].reshape(2 * lanes * rows, keys)
        probs = p_low.astype(f32)
        weighted = probs * back_probs
        delta = jnp.sum(weighted, axis=1, keepdims=True)
        down_pair = []
        delta_list = []
        for half in range(2):
            head = pair * 2 + half
            keep = low_half if half == 0 else jnp.logical_not(low_half)
            for lane in range(lanes):
                start = (half * lanes + lane) * rows
                part = delta[start : start + rows]
                if lane > 0:
                    do_row = do_pair[lane * rows : (lane + 1) * rows].astype(f32)
                    v_row = v_ref[pieces + lane - 1, 0, :, cols].astype(f32)
                    back_own = jnp.sum(jnp.where(keep, do_row * v_row, 0.0), axis=1, keepdims=True)
                    own_prob = own_ref[0, 0, lane * rows : (lane + 1) * rows, head : head + 1]
                    part = part + own_prob * back_own
                    down_pair.append((own_prob * (back_own - part)).astype(bf16).astype(f32))
                else:
                    down_pair.append(None)
                delta_list.append(part)
        delta = jnp.concatenate(delta_list, axis=0)
        back_scores = (weighted - probs * delta).astype(bf16)
        back_q = dot_nn(back_scores, k_main)
        back_k = dot_tn(q_stack, back_scores)
        back_v = dot_tn(do_stack, p_low)
        dk_ref[:pieces, 0, :, cols] = back_k.T.astype(bf16).reshape(pieces, piece_rows, LANE)
        dv_ref[:pieces, 0, :, cols] = back_v.T.astype(bf16).reshape(pieces, piece_rows, LANE)
        scores_ref[pl.ds(group * GROUP + pair * 2, 2)] = back_scores.astype(f32).reshape(2, lanes * rows, keys)
        for lane in range(lanes):
            first = lane * rows
            second = (lanes + lane) * rows
            back = jnp.where(low_half, back_q[first : first + rows], back_q[second : second + rows])
            if lane > 0:
                k_row = k_ref[pieces + lane - 1, 0, :, cols].astype(f32)
                down = jnp.where(low_half, down_pair[lane], down_pair[lanes + lane])
                back = back + down * k_row
                own_low = jnp.where(
                    low_half,
                    own_ref[0, 0, lane * rows : (lane + 1) * rows, pair * 2 : pair * 2 + 1],
                    own_ref[0, 0, lane * rows : (lane + 1) * rows, pair * 2 + 1 : pair * 2 + 2],
                )
                own_low = own_low.astype(bf16).astype(f32)
                dk_ref[pieces + lane - 1, 0, :, cols] = (
                    down * q_pair[first : first + rows].astype(f32)
                ).astype(bf16)
                dv_ref[pieces + lane - 1, 0, :, cols] = (
                    own_low * do_pair[first : first + rows].astype(f32)
                ).astype(bf16)
            dq_ref[lane, 0, :, cols] = (back * scale).astype(bf16)
            if lane > 0:
                for half in range(2):
                    spot = (pair * 2 + half) * BUCKETS
                    downs[lane] = jnp.where(lane_id == spot, down_pair[half * lanes + lane], downs[lane])
    for lane in range(1, lanes):
        down_ref[group, lane] = downs[lane]

    @pl.when(group == pl.num_programs(1) - 1)
    def _():
        keep = own_block_mask(lanes * heads * SUB)
        source = lax.broadcasted_iota(jnp.int32, (span, LANE), 0) & (BUCKETS - 1)
        target = lax.broadcasted_iota(jnp.int32, (span, LANE), 1) & (BUCKETS - 1)
        fold = jnp.where(source == target, 1.0, 0.0).astype(bf16)
        per_block = LANE // BUCKETS
        for g in range(rows // SUB):
            starts = [lane * rows + g * SUB for lane in range(lanes)]
            left = [scores_ref[:, start : start + SUB, :].reshape(heads * SUB, keys) for start in starts]
            sums = dot_nn(jnp.concatenate(left, axis=0).astype(bf16), turned_ref[g])
            embed = dot_nn(jnp.where(keep, sums, 0.0).astype(bf16), fold).reshape(lanes, heads, SUB, LANE)
            for lane in range(lanes):
                for block in range(heads // per_block):
                    out = embed[lane, block * per_block]
                    for part in range(1, per_block):
                        out = jnp.where(lane_id // BUCKETS == part, embed[lane, block * per_block + part], out)
                    if lane > 0:
                        out = out + down_ref[block, lane, g * SUB : (g + 1) * SUB, :]
                    wide_ref[lane, g * SUB : (g + 1) * SUB, block * LANE : (block + 1) * LANE] = out
        for lane in range(lanes):
            de_ref[lane, 0] = wide_ref[lane].astype(bf16)


def cross_forward_kernel(length_ref, posk_ref, q_ref, k_ref, v_ref, o_ref, p_ref):
    slot = pl.program_id(0)
    lanes, _, rows, _ = q_ref.shape
    pieces = k_ref.shape[0]
    keys = pieces * k_ref.shape[2]
    low_half = lax.broadcasted_iota(jnp.int32, (1, LANE), 1) < HEAD_DIM
    fill = jnp.where(posk_ref[...] < length_ref[slot], 0.0, neg_fill)
    count = lanes * rows
    for pair in range(GROUP // 2):
        cols = slice(pair * LANE, (pair + 1) * LANE)
        q_pair = rows_of(q_ref, 0, lanes, cols) * jnp.asarray(HEAD_DIM**-0.5, bf16)
        k_main = rows_of(k_ref, 0, pieces, cols)
        v_main = rows_of(v_ref, 0, pieces, cols)
        scores = dot_nt(stack_heads(q_pair, low_half), k_main) + fill
        top = jnp.max(scores, axis=1, keepdims=True)
        terms = jnp.exp(scores - top)
        inverse = 1.0 / jnp.sum(terms, axis=1, keepdims=True)
        p_low = (terms * inverse).astype(bf16)
        p_ref[0, pair * 2 : pair * 2 + 2] = p_low.reshape(2, count, keys)
        mixed = dot_nn(p_low, v_main)
        out = jnp.where(low_half, mixed[:count], mixed[count:]).astype(bf16)
        o_ref[:, 0, :, cols] = out.reshape(lanes, rows, LANE)


def cross_backward_kernel(p_ref, do_ref, q_ref, k_ref, v_ref, dq_ref, dk_ref, dv_ref):
    lanes, _, rows, _ = q_ref.shape
    pieces = k_ref.shape[0]
    piece_rows = k_ref.shape[2]
    keys = pieces * piece_rows
    count = lanes * rows
    scale = HEAD_DIM**-0.5
    low_half = lax.broadcasted_iota(jnp.int32, (1, LANE), 1) < HEAD_DIM
    for pair in range(GROUP // 2):
        cols = slice(pair * LANE, (pair + 1) * LANE)
        q_pair = rows_of(q_ref, 0, lanes, cols) * jnp.asarray(scale, bf16)
        do_pair = rows_of(do_ref, 0, lanes, cols)
        k_main = rows_of(k_ref, 0, pieces, cols)
        v_main = rows_of(v_ref, 0, pieces, cols)
        q_stack = stack_heads(q_pair, low_half)
        do_stack = stack_heads(do_pair, low_half)
        back_probs = dot_nt(do_stack, v_main)
        p_low = p_ref[0, pair * 2 : pair * 2 + 2].reshape(2 * count, keys)
        probs = p_low.astype(f32)
        weighted = probs * back_probs
        delta = jnp.sum(weighted, axis=1, keepdims=True)
        back_scores = (weighted - probs * delta).astype(bf16)
        back_q = dot_nn(back_scores, k_main)
        back_k = dot_tn(q_stack, back_scores)
        back_v = dot_tn(do_stack, p_low)
        dk_ref[:, 0, :, cols] = back_k.T.astype(bf16).reshape(pieces, piece_rows, LANE)
        dv_ref[:, 0, :, cols] = back_v.T.astype(bf16).reshape(pieces, piece_rows, LANE)
        back = jnp.where(low_half, back_q[:count], back_q[count:]) * scale
        dq_ref[:, 0, :, cols] = back.astype(bf16).reshape(lanes, rows, LANE)


def head_block(array, width=GROUP * HEAD_DIM):
    return pl.BlockSpec((array.shape[0], 1, array.shape[2], width), lambda s, g: (0, s, 0, g))


def slot_block(array):
    return pl.BlockSpec((array.shape[0], 1) + array.shape[2:], lambda s, g: (0, s, 0, 0))


def whole_block(array):
    return pl.BlockSpec(array.shape, lambda s, g: (0,) * array.ndim)


SMALL = pl.CostEstimate(flops=1000, bytes_accessed=1000, transcendentals=0)
SMEM_SPEC = pl.BlockSpec(memory_space=pltpu.SMEM)


def params():
    return pltpu.CompilerParams(vmem_limit_bytes=VMEM_LIMIT)


def shaped(shape, dtype):
    return jax.ShapeDtypeStruct(shape, dtype)


def self_forward(length, bounds, posq, posk, q, e, k, v, part, parts, made=()):
    lanes, slots, rows, width = q.shape
    all_heads = width // HEAD_DIM
    heads = all_heads // parts
    keys = posk.shape[1]
    count = lanes * rows
    groups = heads // GROUP
    base = part * groups

    def block(array):
        return pl.BlockSpec((array.shape[0], 1, array.shape[2], GROUP * HEAD_DIM), lambda s, g: (0, s, 0, base + g))

    inputs = [length, bounds, posq, posk, q, e, k, v]
    return pl.pallas_call(
        functools.partial(self_forward_kernel, len(made), base),
        grid=(slots, groups),
        in_specs=[
            SMEM_SPEC, SMEM_SPEC, whole_block(posq), whole_block(posk), block(q), slot_block(e), block(k), block(v),
        ] + [pl.BlockSpec(memory_space=pl.ANY)] * len(made),
        out_specs=[
            block(q),
            pl.BlockSpec((1, GROUP, count, keys), lambda s, g: (s, base + g, 0, 0)),
            pl.BlockSpec((1, 1, count, LANE), lambda s, g: (s, base + g, 0, 0)),
        ],
        out_shape=[
            shaped(q.shape, bf16),
            shaped((slots, all_heads, count, keys), bf16),
            shaped((slots, all_heads // GROUP, count, LANE), f32),
        ],
        scratch_shapes=[
            pltpu.VMEM((rows, keys), jnp.int32),
            pltpu.VMEM((rows // SUB, SUB * BUCKETS, keys), bf16),
            pltpu.VMEM((heads, count, SUB * BUCKETS), f32),
            pltpu.VMEM((heads, count, keys), f32),
        ],
        input_output_aliases={len(inputs) + i: i for i in range(len(made))},
        compiler_params=params(),
        cost_estimate=SMALL,
        name="self_forward",
    )(*inputs, *made)


def self_backward(bounds, posq, posk, p, own, do, q, k, v, part, parts, made=()):
    lanes, slots, rows, width = q.shape
    heads = width // HEAD_DIM // parts
    keys = p.shape[3]
    count = lanes * rows
    groups = heads // GROUP
    base = part * groups

    def block(array):
        return pl.BlockSpec((array.shape[0], 1, array.shape[2], GROUP * HEAD_DIM), lambda s, g: (0, s, 0, base + g))

    inputs = [bounds, posq, posk, p, own, do, q, k, v]
    return pl.pallas_call(
        functools.partial(self_backward_kernel, len(made)),
        grid=(slots, groups),
        in_specs=[
            SMEM_SPEC, whole_block(posq), whole_block(posk),
            pl.BlockSpec((1, GROUP, count, keys), lambda s, g: (s, base + g, 0, 0)),
            pl.BlockSpec((1, 1, count, LANE), lambda s, g: (s, base + g, 0, 0)),
            block(do), block(q), block(k), block(v),
        ] + [pl.BlockSpec(memory_space=pl.ANY)] * len(made),
        out_specs=[
            block(q), block(k), block(v),
            pl.BlockSpec((lanes, 1, rows, heads * BUCKETS), lambda s, g: (0, s, 0, part)),
        ],
        out_shape=[
            shaped(q.shape, bf16), shaped(k.shape, bf16), shaped(v.shape, bf16),
            shaped((lanes, slots, rows, heads * parts * BUCKETS), bf16),
        ],
        scratch_shapes=[
            pltpu.VMEM((rows, keys), jnp.int32),
            pltpu.VMEM((rows // SUB, SUB * BUCKETS, keys), bf16),
            pltpu.VMEM((rows // SUB, keys, SUB * BUCKETS), bf16),
            pltpu.VMEM((heads, count, keys), f32),
            pltpu.VMEM((groups, lanes, rows, LANE), f32),
            pltpu.VMEM((lanes, rows, heads * BUCKETS), f32),
        ],
        input_output_aliases={len(inputs) + i: i for i in range(len(made))},
        compiler_params=params(),
        cost_estimate=SMALL,
        name="self_backward",
    )(*inputs, *made)


def cross_forward(length, posk, q, k, v):
    lanes, slots, rows, width = q.shape
    heads = width // HEAD_DIM
    keys = posk.shape[1]
    count = lanes * rows
    return pl.pallas_call(
        cross_forward_kernel,
        grid=(slots, heads // GROUP),
        in_specs=[SMEM_SPEC, whole_block(posk), head_block(q), head_block(k), head_block(v)],
        out_specs=[head_block(q), pl.BlockSpec((1, GROUP, count, keys), lambda s, g: (s, g, 0, 0))],
        out_shape=[shaped(q.shape, bf16), shaped((slots, heads, count, keys), bf16)],
        compiler_params=params(),
        cost_estimate=SMALL,
        name="cross_forward",
    )(length, posk, q, k, v)


def cross_backward(p, do, q, k, v):
    lanes, slots, rows, width = q.shape
    heads = width // HEAD_DIM
    keys = p.shape[3]
    count = lanes * rows
    return pl.pallas_call(
        cross_backward_kernel,
        grid=(slots, heads // GROUP),
        in_specs=[
            pl.BlockSpec((1, GROUP, count, keys), lambda s, g: (s, g, 0, 0)),
            head_block(do), head_block(q), head_block(k), head_block(v),
        ],
        out_specs=[head_block(q), head_block(k), head_block(v)],
        out_shape=[shaped(q.shape, bf16), shaped(k.shape, bf16), shaped(v.shape, bf16)],
        compiler_params=params(),
        cost_estimate=SMALL,
        name="cross_backward",
    )(p, do, q, k, v)


FEED_BLOCK = 512


def norm_parts(values):
    row_mean = jnp.mean(values, axis=-1, keepdims=True)
    centered = values - row_mean
    scale = lax.rsqrt(jnp.mean(centered * centered, axis=-1, keepdims=True) + eps_norm)
    return centered * scale, scale


def feed_kernel(
    sending, loading, core_ref, base_ref, mixed_ref, outer_ref, norms_ref, cot_ref, valid_ref, *refs,
):
    layout, copies, cut, parts, number_in = loading
    sources, refs = refs[:number_in], refs[number_in:]
    feed_body(sending, (layout, copies, cut, parts, sources), core_ref, base_ref, mixed_ref, outer_ref, norms_ref, cot_ref, valid_ref, *refs)


def feed_body(
    sending, loading, core_ref, base_ref, mixed_ref, outer_ref, norms_ref, cot_ref, valid_ref,
    out_ref, low_ref, act_ref, back_pre_ref, feed_ref, back_ref, cross_ref, back_mixed_ref, grads_ref, *rest,
):
    if sending:
        up_send_ref, down_send_ref, outer_send_ref, *rest = rest
    unit_ref, total_ref, turned_ref, act_all_ref, slope_ref, row_scale_ref, up_all_ref, down_all_ref, sems = rest
    phase, block = pl.program_id(0), pl.program_id(1)
    last = pl.num_programs(1) - 1
    cols = pl.ds(pl.multiple_of(block * FEED_BLOCK, FEED_BLOCK), FEED_BLOCK)

    up_ref = lambda: up_all_ref[:, cols]
    down_ref = lambda: down_all_ref[cols, :]
    layout, copies, cut, parts, sources = loading

    def loads():
        return group_loads(layout, copies, cut, parts, core_ref, sources, (up_all_ref, down_all_ref), sems, 1)

    @pl.when((phase == 0) & (block == 0))
    def _():
        for _, load in loads():
            load.start()
        unit, scale = norm_parts(base_ref[...] + dot_nn(mixed_ref[...], outer_ref[...]))
        normed = unit * norms_ref[2:3, :] + norms_ref[3:4, :]
        unit_ref[...] = unit
        row_scale_ref[...] = scale
        total_ref[...] = normed
        low_ref[...] = normed.astype(bf16)
        if sending:
            turned_ref[...] = core_columns(low_ref, 1 - core_ref[0], sending).T
        for _, load in loads():
            load.wait()

    @pl.when(phase == 0)
    def _():
        pre = dot_nn(low_ref[...], up_ref())
        below = 0.5 * (1.0 + lax.erf(pre * 0.7071067811865476))
        act = (pre * below).astype(bf16)
        slope_ref[:, cols] = below + pre * (jnp.exp(-0.5 * pre * pre) * 0.3989422804014327)
        act_all_ref[:, cols] = act
        act_ref[...] = act
        total_ref[...] += dot_nn(act, down_ref())

    @pl.when((phase == 0) & (block == last))
    def _():
        unit, scale = norm_parts(total_ref[...])
        gain = norms_ref[4:5, :]
        out_ref[...] = (unit * gain + norms_ref[5:6, :]).astype(bf16)
        cotangent = cot_ref[...].astype(f32) * valid_ref[...]
        back, gain_grad, shift_grad = norm_backward(unit, scale, gain, cotangent)
        grads_ref[2:3, :] = gain_grad[None]
        grads_ref[3:4, :] = shift_grad[None]
        total_ref[...] = back
        feed_ref[...] = back.astype(bf16)

    @pl.when(phase == 1)
    def _():
        back_act = dot_nt(feed_ref[...], down_ref())
        back_pre = (back_act * slope_ref[:, cols]).astype(bf16)
        back_pre_ref[...] = back_pre
        total_ref[...] += dot_nt(back_pre, up_ref())
        if sending:
            up_send_ref[...] = dot_nn(turned_ref[...], back_pre).astype(bf16)

            @pl.when((block & 1) == 1 - core_ref[0])
            def _():
                down_send_ref[...] = dot_tn(act_all_ref[:, cols], feed_ref[...]).astype(bf16)

    @pl.when((phase == 1) & (block == last))
    def _():
        back, gain_grad, shift_grad = norm_backward(
            unit_ref[...], row_scale_ref[...], norms_ref[2:3, :], total_ref[...]
        )
        back_ref[...] = back
        cross_ref[...] = back.astype(bf16)
        back_mixed_ref[...] = dot_nt(cross_ref[...], outer_ref[...]).astype(bf16)
        if sending:
            outer_send_ref[...] = dot_tn(core_columns(mixed_ref, 1 - core_ref[0], sending), cross_ref[...]).astype(bf16)
        grads_ref[0:1, :] = gain_grad[None]
        grads_ref[1:2, :] = shift_grad[None]


def feed_forward_backward(base, mixed, outer, norms, cot, valid, weights, arrivals, layout, cut, place, steps, sending):
    rows, width = base.shape
    hidden = layout[0][1]
    blocks = hidden // FEED_BLOCK
    copies, _ = block_copies(layout)
    sources = [*weights, *arrivals]
    parts = steps if arrivals else 1
    single = pl.Buffered(1)
    whole = lambda array: pl.BlockSpec(array.shape, lambda p, b, c: (0, 0), pipeline_mode=single)
    full = pl.BlockSpec((rows, width), lambda p, b, c: (0, 0))
    first = lambda p, b: jnp.where(p == 0, b, blocks - 1)
    second = lambda p, b: jnp.where(p == 0, 0, b)
    out_specs = [
        full, full,
        pl.BlockSpec((rows, FEED_BLOCK), lambda p, b, c: (0, first(p, b))),
        pl.BlockSpec((rows, FEED_BLOCK), lambda p, b, c: (0, second(p, b))),
        full, full, full, full,
        pl.BlockSpec((4, width), lambda p, b, c: (0, 0)),
    ]
    low = shaped((rows, width), bf16)
    wide = shaped((rows, hidden), bf16)
    out_shape = [low, low, wide, wide, low, shaped((rows, width), f32), low, low, shaped((4, width), f32)]
    if sending:
        assert hidden // (2 * steps) == FEED_BLOCK
        out_specs += [
            pl.BlockSpec((width // 2, FEED_BLOCK), lambda p, b, c: (0, second(p, b))),
            pl.BlockSpec((FEED_BLOCK, width), lambda p, b, c: (second(p, b) // 2, 0)),
            pl.BlockSpec((width // 2, width), lambda p, b, c: (0, 0)),
        ]
        out_shape += [
            shaped((width // 2, hidden), bf16), shaped((hidden // 2, width), bf16), shaped((width // 2, width), bf16),
        ]
    return pl.pallas_call(
        functools.partial(feed_kernel, steps if sending else 0, (layout, copies, cut, parts, len(sources))),
        grid_spec=pltpu.PrefetchScalarGridSpec(
            num_scalar_prefetch=1,
            grid=(2, blocks),
            in_specs=[
                whole(base), whole(mixed), whole(outer), whole(norms), whole(cot), whole(valid),
            ] + [pl.BlockSpec(memory_space=pl.ANY)] * len(sources),
            out_specs=out_specs,
            scratch_shapes=[
                pltpu.VMEM((rows, width), f32), pltpu.VMEM((rows, width), f32),
                pltpu.VMEM((width // 2, rows), bf16), pltpu.VMEM((rows, hidden), bf16), pltpu.VMEM((rows, hidden), f32),
                pltpu.VMEM((rows, 1), f32),
                pltpu.VMEM((width, hidden), bf16), pltpu.VMEM((hidden, width), bf16), pltpu.SemaphoreType.DMA((2,)),
            ],
        ),
        out_shape=out_shape,
        compiler_params=params(),
        cost_estimate=SMALL,
        name="feed",
    )(place, base, mixed, outer, norms, cot, valid, *sources)


def middle_kernel(
    sending, core_ref, back_cq_ref, query_ref, back_two_ref, unit_ref, scale_ref, norms_ref, outer_ref, *refs
):
    if sending:
        normed_ref, mixed_ref, feed_norms_ref, enc_ref, back_k_ref, back_v_ref, key_ref, value_ref, *refs = refs
        back_ref, low_ref, back_mixed_ref, grads_ref, query_send_ref, outer_send_ref, *refs = refs
        norm_keep_ref, norm_send_ref, key_send_ref, value_send_ref, even_ref, odd_ref, pieces_ref = refs
    else:
        back_ref, low_ref, back_mixed_ref, grads_ref = refs
    total = back_two_ref[...] + dot_nt(back_cq_ref[...], query_ref[...])
    back, gain_grad, shift_grad = norm_backward(unit_ref[...], scale_ref[...], norms_ref[0:1, :], total)
    back_ref[...] = back
    low_ref[...] = back.astype(bf16)
    grads_ref[0:1, :] = gain_grad[None]
    grads_ref[1:2, :] = shift_grad[None]
    back_mixed_ref[...] = dot_nt(low_ref[...], outer_ref[...]).astype(bf16)
    if sending:
        for left, right, out in ((normed_ref, back_cq_ref, query_send_ref), (mixed_ref, low_ref, outer_send_ref)):
            out[...] = dot_tn(core_columns(left, 1 - core_ref[0], sending), right[...]).astype(bf16)
        width = back.shape[1]
        pieces = pieces_ref.shape[0] // 16
        part = width // pieces
        vectors = jnp.concatenate(
            [gain_grad[None], shift_grad[None], feed_norms_ref[...], jnp.zeros((16 - 6, width), f32)], axis=0
        )
        pick_row = lax.broadcasted_iota(jnp.int32, (pieces * 16, 16), 0)
        pick_col = lax.broadcasted_iota(jnp.int32, (pieces * 16, 16), 1)
        pick = jnp.where(lax.rem(pick_row, 16) == pick_col, 1.0, 0.0).astype(bf16)
        wide = dot_nn(pick, vectors.astype(bf16))
        piece = lax.broadcasted_iota(jnp.int32, wide.shape, 0) // 16
        column = lax.broadcasted_iota(jnp.int32, wide.shape, 1) // part
        wide = jnp.where(piece == column, wide, 0.0).astype(bf16)
        copy_row = lax.broadcasted_iota(jnp.int32, (width, LANE), 0)
        copy_col = lax.broadcasted_iota(jnp.int32, (width, LANE), 1)
        copy = jnp.where(lax.rem(copy_row, part) == copy_col, 1.0, 0.0).astype(bf16)
        pieces_ref[...] = dot_nn(wide, copy).astype(bf16)
        norm_keep_ref[...] = jnp.zeros(norm_keep_ref.shape, bf16)
        norm_send_ref[...] = jnp.zeros(norm_send_ref.shape, bf16)
        size = pieces * 16 // (2 * sending)
        for step in range(sending):
            for out, which in ((norm_keep_ref, core_ref[0]), (norm_send_ref, 1 - core_ref[0])):
                start = pl.multiple_of((2 * step + which) * size, size)
                out[step * size : (step + 1) * size, :LANE] = pieces_ref[pl.ds(start, size), :]
        columns = core_columns(enc_ref, 1 - core_ref[0], sending)
        key_send_ref[...] = dot_tn(columns, back_k_ref[...]).astype(bf16)
        value_send_ref[...] = dot_tn(columns, back_v_ref[...]).astype(bf16)
        pair_tiles(back_k_ref, back_v_ref, key_ref, value_ref, even_ref, odd_ref)


def pair_tiles(back_k_ref, back_v_ref, key_ref, value_ref, even_ref, odd_ref):
    half = even_ref.shape[1]

    def fill(tile, carry):
        rows = pl.ds(pl.multiple_of(tile * 2 * half, 2 * half), 2 * half)
        total = dot_nt(back_k_ref[rows, :], key_ref[...]) + dot_nt(back_v_ref[rows, :], value_ref[...])
        even_ref[tile] = total[:half].astype(bf16)
        odd_ref[tile] = total[half:].astype(bf16)
        return carry

    lax.fori_loop(0, even_ref.shape[0], fill, 0)


def middle_backward(
    back_cq, query, back_two, unit, scale, norms, outer, core, steps, sending=()
):
    rows, width = back_two.shape
    low = shaped((rows, width), bf16)
    out_shape = [shaped((rows, width), f32), low, low, shaped((2, width), f32)]
    inputs = [back_cq, query, back_two, unit, scale, norms, outer]
    if sending:
        half = shaped((width // 2, width), bf16)
        pair = shaped((4, sending[3].shape[0] // 8, width), bf16)
        out_shape += [half, half] + [shaped((16 * 4 * steps, width), bf16)] * 2 + [half, half, pair, pair]
        inputs += sending
    vmem = pl.BlockSpec(memory_space=pltpu.VMEM)
    return pl.pallas_call(
        functools.partial(middle_kernel, steps if sending else 0),
        in_specs=[SMEM_SPEC] + [vmem] * len(inputs),
        out_specs=[vmem] * len(out_shape),
        out_shape=out_shape,
        scratch_shapes=[pltpu.VMEM((16 * 8 * steps, LANE), bf16)] if sending else [],
        compiler_params=params(),
        cost_estimate=SMALL,
        name="middle_backward",
    )(core, *inputs)


def pair_rows_kernel(tiles, back_k_ref, back_v_ref, key_ref, value_ref, even_ref, odd_ref, *rest):
    total = dot_nt(back_k_ref[...], key_ref[...]) + dot_nt(back_v_ref[...], value_ref[...])
    half = even_ref.shape[1]
    step = pl.program_id(0)

    @pl.when(step < tiles)
    def _():
        even_ref[0] = total[:half].astype(bf16)
        odd_ref[0] = total[half:].astype(bf16)

    if rest:

        @pl.when(step >= tiles)
        def _():
            rest[0][...] = total


def pair_rows(back_k, back_v, key, value, pieces, piece_rows):
    count, width = back_k.shape[0], key.shape[0]
    tile = 2 * piece_rows
    tiles = pieces // 2
    steps = count // tile
    resident = lambda array: pl.BlockSpec(array.shape, lambda t: (0, 0), pipeline_mode=pl.Buffered(1))
    rows = pl.BlockSpec((tile, back_k.shape[1]), lambda t: (t, 0))
    part = pl.BlockSpec((1, piece_rows, width), lambda t: (jnp.minimum(t, tiles - 1), 0, 0))
    out_specs, out_shape = [part, part], [shaped((tiles, piece_rows, width), bf16)] * 2
    if steps > tiles:
        out_specs.append(pl.BlockSpec((tile, width), lambda t: (jnp.maximum(t - tiles, 0), 0)))
        out_shape.append(shaped((count - tiles * tile, width), f32))
    return pl.pallas_call(
        functools.partial(pair_rows_kernel, tiles),
        grid=(steps,),
        in_specs=[rows, rows, resident(key), resident(value)],
        out_specs=out_specs,
        out_shape=out_shape,
        compiler_params=params(),
        cost_estimate=SMALL,
        name="pair_rows",
    )(back_k, back_v, key, value)


def last_kernel(
    steps, core_ref, x_ref, keyed_ref, back_ref, back_q_ref, back_e_ref, back_k_ref, back_v_ref,
    query_ref, relative_ref, key_ref, value_ref,
    key_send_ref, value_send_ref, query_send_ref, embed_send_ref, even_ref, odd_ref, out_ref,
):
    columns = core_columns(keyed_ref, 1 - core_ref[0], steps)
    key_send_ref[...] = dot_tn(columns, back_k_ref[...]).astype(bf16)
    value_send_ref[...] = dot_tn(columns, back_v_ref[...]).astype(bf16)
    columns = core_columns(x_ref, 1 - core_ref[0], steps)
    query_send_ref[...] = dot_tn(columns, back_q_ref[...]).astype(bf16)
    embed_send_ref[...] = dot_tn(columns, back_e_ref[...]).astype(bf16)
    pair_tiles(back_k_ref, back_v_ref, key_ref, value_ref, even_ref, odd_ref)
    main = even_ref.shape[0] * 2 * even_ref.shape[1]
    skip = out_ref.shape[0] - (back_k_ref.shape[0] - main)
    total = back_ref[...] + dot_nt(back_q_ref[...], query_ref[...]) + dot_nt(back_e_ref[...], relative_ref[...])
    out_ref[:skip, :] = total[:skip]
    lanes = dot_nt(back_k_ref[main:, :], key_ref[...]) + dot_nt(back_v_ref[main:, :], value_ref[...])
    out_ref[skip:, :] = total[skip:] + lanes


def last_backward(x, keyed, back, back_q, back_e, back_k, back_v, query, relative, key, value, core, steps, pieces):
    width = x.shape[1]
    half = shaped((width // 2, width), bf16)
    pair = shaped((pieces // 2, x.shape[0] // 3, width), bf16)
    out_shape = [half, half, half, shaped((width // 2, back_e.shape[1]), bf16), pair, pair, shaped(back.shape, f32)]
    vmem = pl.BlockSpec(memory_space=pltpu.VMEM)
    return pl.pallas_call(
        functools.partial(last_kernel, steps),
        in_specs=[SMEM_SPEC] + [vmem] * 11,
        out_specs=[vmem] * len(out_shape),
        out_shape=out_shape,
        compiler_params=params(),
        cost_estimate=SMALL,
        name="last_backward",
    )(core, x, keyed, back, back_q, back_e, back_k, back_v, query, relative, key, value)


def after(value, *others):
    return lax.optimization_barrier((value,) + others)[0]


def tie(*values):
    return lax.optimization_barrier(values)


def ctx_hop(array, bit):
    size = lax.axis_size("ctx")
    return lax.ppermute(array, "ctx", [(i, i ^ bit) for i in range(size)])


def z_hop(array, step):
    size = lax.axis_size("fsdp")
    return lax.ppermute(array, "fsdp", [(i, (i + step) % size) for i in range(size)])


def first_spread(array):
    return array, ctx_hop(array, XBIT), ctx_hop(array, YBIT)


def corner_spread(firsts, axis, cut, *held):
    array, from_x, from_y = firsts
    if held:
        from_x, from_y, *_ = lax.optimization_barrier((from_x, from_y, *held))
    size = array.shape[axis]
    corner_one = ctx_hop(lax.slice_in_dim(from_y, 0, cut, axis=axis), XBIT)
    corner_two = ctx_hop(lax.slice_in_dim(from_x, cut, size, axis=axis), YBIT)
    return [array, from_x, from_y, corner_one, corner_two]


SPREAD_PLAN = tuple(
    (offset + core, part) for core in (0, 1) for offset, part in ((0, 0), (XBIT, 0), (YBIT, 0), (XBIT + YBIT, 1), (XBIT + YBIT, 2))
)


def piece_number(index):
    return (index & 1) * 4 + (index >> 1)


def block_copies(layout):
    copies = []
    row = 0
    for number, (shard_rows, columns) in enumerate(layout):
        piece_rows = shard_rows // 8
        if columns >= 1024:
            for block in range(columns // 1024):
                copies.append((row, piece_rows, 0, 1024, number, 0, block * 1024))
                row += piece_rows
        else:
            parts = 1024 // columns
            rows = piece_rows // parts
            for part in range(parts):
                copies.append((row, rows, part * columns, columns, number, part * rows, 0))
            row += rows
    return tuple(copies), row


def place_copies(copies, cut):
    def chosen(part):
        if part == 0:
            return copies
        if part == 1:
            return tuple(item for item in copies if item[0] < cut)
        return tuple((item[0] - cut,) + item[1:] for item in copies if item[0] >= cut)

    return chosen


def group_loads(layout, copies, cut, steps, place_ref, sources, stages, sems, base=0):
    count = len(layout)
    chosen = place_copies(copies, cut)
    loads = []
    for number, (shard_rows, _) in enumerate(layout):
        target = stages[number]
        if steps > 1:
            start = pl.multiple_of(place_ref[base] * shard_rows, shard_rows)
            target = target.at[pl.ds(start, shard_rows), :]
        loads.append((number, pltpu.make_async_copy(sources[number], target, sems.at[number])))
    for arrival, (offset, part) in zip(sources[count:], SPREAD_PLAN):
        for step in range(1, steps):
            for row, rows, col, cols, number, prow, wcol in chosen(part):
                shard_rows = layout[number][0]
                start = place_ref[base + step] * shard_rows
                start = start + place_ref[base + steps + offset] * (shard_rows // 8) + prow
                source = arrival.at[step - 1, pl.ds(row, rows), pl.ds(col, cols)]
                target = stages[number].at[pl.ds(pl.multiple_of(start, 16), rows), pl.ds(wcol, cols)]
                loads.append((number, pltpu.make_async_copy(source, target, sems.at[number])))
    return loads


def place_of(z_index, c_index, steps):
    return jnp.stack(
        [(z_index - step) % steps for step in range(steps)] + [piece_number(c_index ^ j) for j in range(8)]
    ).astype(jnp.int32)


def project_kernel(layout, copies, cut, steps, products, pieces, tail, place_ref, *refs):
    count = len(layout)
    number_in = count + len(SPREAD_PLAN)
    own_ref, refs = (refs[0], refs[1:]) if tail else (None, refs)
    parts, sources, refs = refs[:pieces], refs[pieces : pieces + number_in], refs[pieces + number_in :]
    outs, refs = refs[: len(products)], refs[len(products) :]
    rows_out, weights_out, refs = refs[0], refs[1 : 1 + count], refs[1 + count :]
    rows_ref, stages, sems, row_sem, out_sem = refs[0], refs[1 : 1 + count], refs[-3], refs[-2], refs[-1]
    step = pl.program_id(0)
    piece_rows = parts[0].shape[0]

    def stores():
        moves = [pltpu.make_async_copy(rows_ref, rows_out, out_sem.at[count])]
        return moves + [pltpu.make_async_copy(stages[i], weights_out[i], out_sem.at[i]) for i in range(count)]

    @pl.when(step == 0)
    def _():
        loads = [
            pltpu.make_async_copy(part, rows_ref.at[pl.ds(j * piece_rows, piece_rows), :], row_sem)
            for j, part in enumerate(parts)
        ]
        loads += [load for _, load in group_loads(layout, copies, cut, steps, place_ref, sources, stages, sems)]
        for load in loads:
            load.start()
        if tail:
            rows_ref[pieces * piece_rows :, :] = own_ref[piece_rows:, :]
        for load in loads:
            load.wait()
        for move in stores():
            move.start()

    for out, (from_rows, number) in zip(outs, products):
        block = out.shape[1]
        cols = pl.ds(pl.multiple_of(step * block, LANE), block)
        left = rows_ref[...] if from_rows else own_ref[...]
        out[...] = dot_nn(left, stages[number][:, cols]).astype(bf16)

    @pl.when(step == pl.num_programs(0) - 1)
    def _():
        for move in stores():
            move.wait()


def project(own, parts, weights, arrivals, layout, cut, products, place, steps):
    copies, _ = block_copies(layout)
    count = len(layout)
    piece_rows, width = parts[0].shape
    rows = piece_rows * len(parts) + (own.shape[0] - piece_rows if own is not None else 0)
    blocks = 4
    hbm = pl.BlockSpec(memory_space=pl.ANY)
    first = [] if own is None else [own]
    shapes = [(shard_rows * steps, columns) for shard_rows, columns in layout]
    out_shape, out_specs = [], []
    for from_rows, number in products:
        left_rows = rows if from_rows else own.shape[0]
        out_shape.append(shaped((left_rows, shapes[number][1]), bf16))
        out_specs.append(pl.BlockSpec((left_rows, shapes[number][1] // blocks), lambda t: (0, t)))
    out_shape += [shaped((rows, width), bf16)] + [shaped(item, bf16) for item in shapes]
    outs = pl.pallas_call(
        functools.partial(project_kernel, layout, copies, cut, steps, products, len(parts), own is not None),
        grid=(blocks,),
        in_specs=[SMEM_SPEC]
        + [pl.BlockSpec(item.shape, lambda t: (0, 0), pipeline_mode=pl.Buffered(1)) for item in first]
        + [hbm] * (len(parts) + len(weights) + len(arrivals)),
        out_specs=out_specs + [hbm] * (1 + count),
        out_shape=out_shape,
        scratch_shapes=[pltpu.VMEM((rows, width), bf16)]
        + [pltpu.VMEM(item, bf16) for item in shapes]
        + [pltpu.SemaphoreType.DMA((count,)), pltpu.SemaphoreType.DMA, pltpu.SemaphoreType.DMA((count + 1,))],
        compiler_params=params(),
        cost_estimate=SMALL,
        name="project",
    )(place, *first, *parts, *weights, *arrivals)
    return outs[: len(products)], outs[len(products)], outs[len(products) + 1 :]


def query_kernel(norm_count, x_ref, mixed_ref, outer_ref, query_ref, vectors_ref, total_ref, unit_ref, scale_ref, low_ref, out_ref, norms_ref):
    pieces = vectors_ref.shape[0] // 16
    width = x_ref.shape[1]
    part = width // pieces
    copy_row = lax.broadcasted_iota(jnp.int32, (LANE, width), 0)
    copy_col = lax.broadcasted_iota(jnp.int32, (LANE, width), 1)
    copy = jnp.where(copy_row == lax.rem(copy_col, part), 1.0, 0.0).astype(bf16)
    wide = dot_nn(vectors_ref[...], copy)
    piece = lax.broadcasted_iota(jnp.int32, wide.shape, 0) // 16
    column = lax.broadcasted_iota(jnp.int32, wide.shape, 1) // part
    wide = jnp.where(piece == column, wide, 0.0).astype(bf16)
    pick_row = lax.broadcasted_iota(jnp.int32, (16, pieces * 16), 0)
    pick_col = lax.broadcasted_iota(jnp.int32, (16, pieces * 16), 1)
    pick = jnp.where(pick_row == lax.rem(pick_col, 16), 1.0, 0.0).astype(bf16)
    norms_ref[...] = dot_nn(pick, wide)
    unit, scale = norm_parts(x_ref[...].astype(f32) + dot_nn(mixed_ref[...], outer_ref[...]))
    total = unit * norms_ref[0:1, :] + norms_ref[1:2, :]
    unit_ref[...] = unit
    scale_ref[...] = scale
    total_ref[...] = total
    low_ref[...] = total.astype(bf16)
    out_ref[...] = dot_nn(low_ref[...], query_ref[...]).astype(bf16)


def query_rows(x, mixed, outer, query, vectors, norm_count):
    rows, width = x.shape
    full = lambda array: pl.BlockSpec(array.shape, lambda t: (0, 0))
    wide, low = shaped((rows, width), f32), shaped((rows, width), bf16)
    outs = [wide, wide, shaped((rows, 1), f32), low, low, shaped((16, width), f32)]
    return pl.pallas_call(
        functools.partial(query_kernel, norm_count),
        grid=(1,),
        in_specs=[full(x), full(mixed), full(outer), full(query), pl.BlockSpec((vectors.shape[0], LANE), lambda t: (0, 0))],
        out_specs=[full(item) for item in outs],
        out_shape=outs,
        compiler_params=params(),
        cost_estimate=SMALL,
        name="query_rows",
    )(x, mixed, outer, query, vectors)


def pieces_kernel(layouts, plans, place_ref, *refs):
    count = sum(len(layout) for layout in layouts)
    weights, outs, sem = refs[:count], refs[count:-1], refs[-1]
    moves = []
    first = 0
    for layout, copies, out in zip(layouts, plans, outs):
        for row, rows, col, cols, number, prow, wcol in copies:
            start = pl.multiple_of(place_ref[0] * (layout[number][0] // 8) + prow, 16)
            source = weights[first + number].at[pl.ds(start, rows), pl.ds(wcol, cols)]
            moves.append(pltpu.make_async_copy(source, out.at[pl.ds(row, rows), pl.ds(col, cols)], sem))
        first += len(layout)
    for move in moves:
        move.start()
    for move in moves:
        move.wait()


def own_pieces(groups, layouts, c_index):
    plans = [block_copies(layout) for layout in layouts]
    weights = [w for group in groups for w in group]
    return pl.pallas_call(
        functools.partial(pieces_kernel, layouts, [plan[0] for plan in plans]),
        in_specs=[SMEM_SPEC] + [pl.BlockSpec(memory_space=pl.ANY)] * len(weights),
        out_specs=[pl.BlockSpec(memory_space=pltpu.VMEM)] * len(groups),
        out_shape=[shaped((plan[1], 1024), bf16) for plan in plans],
        scratch_shapes=[pltpu.SemaphoreType.DMA],
        compiler_params=params(),
        cost_estimate=SMALL,
        name="own_pieces",
    )(piece_number(c_index).astype(jnp.int32).reshape(1), *weights)


def stack_kernel(count, *refs):
    out, sem = refs[count], refs[count + 1]
    moves = [pltpu.make_async_copy(refs[i], out.at[i], sem) for i in range(count)]
    for move in moves:
        move.start()
    for move in moves:
        move.wait()


def stack_rows(items):
    return pl.pallas_call(
        functools.partial(stack_kernel, len(items)),
        in_specs=[pl.BlockSpec(memory_space=pl.ANY)] * len(items),
        out_specs=pl.BlockSpec(memory_space=pltpu.VMEM),
        out_shape=shaped((len(items),) + items[0].shape, items[0].dtype),
        scratch_shapes=[pltpu.SemaphoreType.DMA],
        compiler_params=params(),
        cost_estimate=SMALL,
        name="stack_rows",
    )(*items)


def z_spread(mine):
    return [z_hop(mine, step) for step in range(1, lax.axis_size("fsdp"))]


def core_columns(ref, which, steps):
    block = ref.shape[1] // (2 * steps)
    parts = [ref[:, pl.ds(pl.multiple_of((2 * step + which) * block, block), block)] for step in range(steps)]
    return jnp.concatenate(parts, axis=1)


def fold_grads_kernel(groups, steps, extra_rows, plain_rows, place_ref, *refs):
    count = len(groups)
    half = steps // 2
    lefts, refs = refs[: max(groups) + 1], refs[max(groups) + 1 :]
    rights, arrivals, refs = refs[:count], refs[count : 2 * count], refs[2 * count :]
    if extra_rows:
        extra_keep, extra_got, refs = refs[0], refs[1], refs[2:]
    if plain_rows:
        plain_keep, plain_got, refs = refs[0], refs[1], refs[2:]
    outs, work = refs[:8], refs[8:]
    step = pl.program_id(0)

    for number, group in enumerate(groups):
        work[number][...] = dot_tn(lefts[group][...], rights[number][...])
    for first_x in (True, False):

        @pl.when((step < half) if first_x else (step >= half))
        def _(first_x=first_x):
            some = outs[:4] if first_x else outs[4:]
            for offset in range(4):
                y_bit, x_bit = offset >> 1, offset & 1
                on, other = (x_bit, y_bit) if first_x else (y_bit, x_bit)
                out = some[2 * (1 - on) + other]
                yx = place_ref[1] ^ offset
                row = extra_rows
                if extra_rows:
                    total = extra_keep[offset, 0].astype(f32) + extra_got[offset, 0].astype(f32)
                    out[0, :extra_rows, :] = total.astype(bf16)
                for number in range(count):
                    piece, columns = arrivals[number].shape[1:]
                    total = work[number][pl.ds(pl.multiple_of(yx * piece, piece), piece), :]
                    total = (total + arrivals[number][yx].astype(f32)).astype(bf16)
                    if columns >= 1024:
                        for block in range(columns // 1024):
                            out[0, row : row + piece, :] = total[:, block * 1024 : (block + 1) * 1024]
                            row += piece
                    else:
                        parts = 1024 // columns
                        low = piece // parts
                        for part in range(parts):
                            out[0, row : row + low, part * columns : (part + 1) * columns] = total[
                                part * low : (part + 1) * low
                            ]
                        row += low
                if plain_rows:
                    total = plain_keep[yx].astype(f32) + plain_got[yx].astype(f32)
                    out[0, row : row + plain_rows, :] = total.astype(bf16)


def fold_grads(pairs, arrivals, extra, plain, place, steps):
    half = steps // 2
    lefts = [left for left, _ in pairs]
    groups = [number for number, (_, rights) in enumerate(pairs) for _ in rights]
    rights = [right for _, some in pairs for right in some]

    def around(t, p):
        return lax.rem(p[0] + t, steps)

    def resident(array):
        return pl.BlockSpec(array.shape, lambda t, p: (0, 0), pipeline_mode=pl.Buffered(1))

    def by_z(array):
        return pl.BlockSpec((4,) + array.shape[1:], lambda t, p: (around(t, p), 0, 0))

    in_specs = [
        pl.BlockSpec((left.shape[0], left.shape[1] // (2 * steps)), lambda t, p: (0, 2 * around(t, p) + p[2]))
        for left in lefts
    ]
    in_specs += [resident(item) for item in rights] + [by_z(item) for item in arrivals]
    total_rows = sum(item.shape[1] * item.shape[2] // 1024 for item in arrivals)
    extra_rows = plain_rows = 0
    if extra is not None:
        extra_rows = extra[0].shape[2]
        in_specs += [pl.BlockSpec((4, 1, extra_rows, 1024), lambda t, p: (0, t, 0, 0))] * 2
    if plain is not None:
        plain_rows = plain[0].shape[1]
        in_specs += [by_z(item) for item in plain]
    total_rows += extra_rows + plain_rows
    a_spec = pl.BlockSpec((1, total_rows, 1024), lambda t, p: (jnp.minimum(t, half - 1), 0, 0))
    b_spec = pl.BlockSpec((1, total_rows, 1024), lambda t, p: (jnp.maximum(t - half, 0), 0, 0))
    return pl.pallas_call(
        functools.partial(fold_grads_kernel, groups, steps, extra_rows, plain_rows),
        grid_spec=pltpu.PrefetchScalarGridSpec(
            num_scalar_prefetch=1,
            grid=(steps,),
            in_specs=in_specs,
            out_specs=[a_spec] * 4 + [b_spec] * 4,
            scratch_shapes=[
                pltpu.VMEM((lefts[group].shape[1] // (2 * steps), right.shape[1]), f32)
                for group, right in zip(groups, rights)
            ],
        ),
        out_shape=[shaped((half, total_rows, 1024), bf16)] * 8,
        compiler_params=params(),
        cost_estimate=SMALL,
        name="fold_grads",
    )(place, *lefts, *rights, *arrivals, *(extra or ()), *(plain or ()))


def unpack_kernel(layout, copies, cut, vectors, place_ref, *refs):
    arrivals = refs[: len(SPREAD_PLAN)]
    outs = refs[len(SPREAD_PLAN) :]
    weights = len(layout) - (1 if vectors else 0)
    chosen = place_copies(copies, cut)
    for arrival, (offset, part) in zip(arrivals, SPREAD_PLAN):
        for row, rows, col, cols, number, prow, wcol in chosen(part):
            piece_rows = layout[number][0] // 8
            if number < weights:
                start = pl.multiple_of(place_ref[offset] * piece_rows + prow, 8)
                target = outs[number]
                target[pl.ds(start, rows), wcol : wcol + cols] = arrival[row : row + rows, col : col + cols].astype(f32)
            else:
                start = pl.multiple_of(place_ref[offset] * piece_rows, 16)
                outs[-1][pl.ds(start, rows), :] = arrival[row : row + rows, :LANE]
    if vectors:
        pieces, width = 8, outs[weights].shape[1]
        part = width // pieces
        copy_row = lax.broadcasted_iota(jnp.int32, (LANE, width), 0)
        copy_col = lax.broadcasted_iota(jnp.int32, (LANE, width), 1)
        copy = jnp.where(copy_row == lax.rem(copy_col, part), 1.0, 0.0).astype(bf16)
        wide = dot_nn(outs[-1][...], copy)
        piece = lax.broadcasted_iota(jnp.int32, wide.shape, 0) // 16
        column = lax.broadcasted_iota(jnp.int32, wide.shape, 1) // part
        wide = jnp.where(piece == column, wide, 0.0).astype(bf16)
        pick_row = lax.broadcasted_iota(jnp.int32, (16, pieces * 16), 0)
        pick_col = lax.broadcasted_iota(jnp.int32, (16, pieces * 16), 1)
        pick = jnp.where(pick_row == lax.rem(pick_col, 16), 1.0, 0.0).astype(bf16)
        whole = dot_nn(pick, wide)
        for index in range(vectors):
            outs[weights + index][...] = whole[index : index + 1, :]


def add_low(a, b):
    return (a.astype(f32) + b.astype(f32)).astype(bf16)


class Reduction:
    def __init__(self, pairs, layout, cut, z_index, c_index):
        self.pairs, self.layout, self.cut, self.c_index = pairs, layout, cut, c_index
        self.steps = lax.axis_size("fsdp")
        self.half = self.steps // 2
        self.copies, self.rows = block_copies(layout)
        self.place = jnp.stack([z_index, c_index >> 1, c_index & 1]).astype(jnp.int32)

    def fold(self, arrivals, extra, plain, *held):
        steps = self.steps
        arrivals = [a.reshape(steps * 4, rows // 8, columns) for a, (rows, columns) in zip(arrivals, self.layout)]
        self.lead = 0
        if extra is not None:
            self.lead = extra[0].shape[1] // steps
            extra = [item.reshape(4, steps, self.lead, 1024) for item in extra]
        place = after(self.place, *held)
        self.folded = list(fold_grads(self.pairs, arrivals, extra, plain, place, steps))

    def first_hops(self, part):
        return ctx_hop(self.folded[part], XBIT), ctx_hop(self.folded[4 + part], YBIT)

    def second_sums(self, got_x, got_y):
        self.sums = add_low(self.folded[3], got_x), add_low(self.folded[7], got_y)

    def second_hops(self):
        return ctx_hop(self.sums[0], YBIT), ctx_hop(self.sums[1], XBIT)

    def z_sums(self, got_x, got_y, late_x, late_y):
        done = []
        for keep, got, late in ((self.folded[2], got_x, late_x), (self.folded[6], got_y, late_y)):
            for kk in range(self.half):
                done.append(keep[kk].astype(f32) + got[kk].astype(f32) + late[kk].astype(f32))
        self.extra = [item[: self.lead] for item in done]
        self.terms = [item[self.lead :] for item in done]
        self.total = self.terms[-1].astype(bf16)

    def z_step(self, step, got=None):
        if got is not None:
            self.total = (self.terms[self.steps - step].astype(f32) + got.astype(f32)).astype(bf16)
        return z_hop(self.total, 1)

    def z_end(self, got):
        self.total = (self.terms[0] + got.astype(f32)).astype(bf16)

    def spread(self):
        self.near = list(first_spread(self.total))
        return self.near[1:]

    def corners(self, from_x, from_y):
        self.near = corner_spread([self.near[0], from_x, from_y], 0, self.cut)
        return self.near[3:]

    def grads(self, arrivals, vectors=0):
        place = jnp.stack([piece_number(self.c_index ^ j) for j in range(8)]).astype(jnp.int32)
        vmem = pl.BlockSpec(memory_space=pltpu.VMEM)
        out_shape = [shaped((rows, columns), f32) for rows, columns in self.layout]
        if vectors:
            out_shape[-1:] = [shaped((1, self.layout[0][0]), f32)] * vectors
        return pl.pallas_call(
            functools.partial(unpack_kernel, self.layout, self.copies, self.cut, vectors),
            in_specs=[SMEM_SPEC] + [vmem] * len(arrivals),
            out_specs=[vmem] * len(out_shape),
            out_shape=out_shape,
            scratch_shapes=[pltpu.VMEM((128, LANE), bf16)] if vectors else [],
            compiler_params=params(),
            cost_estimate=SMALL,
            name="unpack",
        )(place, *arrivals)

    def extra_sum(self):
        return jnp.concatenate(self.extra, axis=0)


def on_device(
    hidden, encoder_out, out_grad, slot_len, enc_len, rel_bucket,
    query_weight, key_weight, value_weight, relative_weight, output_weight, self_norm_gain, self_norm_shift,
    cross_query_weight, cross_key_weight, cross_value_weight, cross_output_weight, cross_norm_gain,
    cross_norm_shift, up_weight, down_weight, feed_norm_gain, feed_norm_shift,
):
    lanes, slots, halves, half_rows, width = hidden.shape
    rows = halves * half_rows
    enc_rows = encoder_out.shape[1]
    ctx_count = lax.axis_size("ctx")
    steps = lax.axis_size("fsdp")
    z_index = lax.axis_index("fsdp")
    c_index = lax.axis_index("ctx")
    seq_len = ctx_count * rows
    all_rows = lanes * slots * rows
    slab = (lanes, slots, rows, width)
    paired = ctx_count == 8 and steps == 4 and query_weight.shape[0] % 256 == 0 and width == 1024
    paired = paired and enc_rows == rows

    norms = jnp.stack(
        [self_norm_gain, self_norm_shift, cross_norm_gain, cross_norm_shift, feed_norm_gain, feed_norm_shift]
    )
    norm_count, norm_shard = norms.shape

    self_set = (query_weight, relative_weight, key_weight, value_weight)
    cross_set = (output_weight, cross_query_weight, cross_key_weight, cross_value_weight, cross_output_weight)
    feed_set = (up_weight, down_weight)
    layouts = [tuple(w.shape for w in group) for group in (self_set, cross_set, feed_set)]
    x_all = hidden.reshape(all_rows, width)
    x_rows = hidden.reshape(slab)
    if paired:
        cuts = (48, 96, 128)
        where = place_of(z_index, c_index, steps)
        main, enc = x_all[: slots * rows], encoder_out.reshape(slots * rows, width)
        (piece,) = own_pieces((self_set,), layouts[:1], c_index)
        ring = [z_hop(piece, 1)]
        main_x, enc_x = ctx_hop(main, XBIT), ctx_hop(enc, XBIT)
        main_y, enc_y = ctx_hop(main, YBIT), ctx_hop(enc, YBIT)
        vectors = norms.reshape(norm_count, 8, norm_shard // 8).transpose(1, 0, 2)
        vectors = jnp.pad(vectors, ((0, 0), (0, 16 - norm_count), (0, 1024 - norm_shard // 8))).reshape(128, 1024)
        second_set = (*cross_set, vectors)
        second_layout = layouts[1] + (vectors.shape,)
        second_piece, feed_piece = own_pieces((second_set, feed_set), (second_layout, layouts[2]), c_index)
        held, main_x, main_y, enc_x, enc_y = tie(ring[0], main_x, main_y, enc_x, enc_y)
        ring.append(z_hop(held, 1))
        main_corner, enc_corner = ctx_hop(main_y, XBIT), ctx_hop(enc_x, YBIT)
        main_far, enc_far = [ctx_hop(main, CORE)], [ctx_hop(enc, CORE)]
        held, main_corner, enc_corner, main_far[0], enc_far[0] = tie(
            ring[1], main_corner, enc_corner, main_far[0], enc_far[0]
        )
        ring.append(z_hop(held, 1))
        main_far += [ctx_hop(main_x, CORE), ctx_hop(main_y, CORE)]
        enc_far += [ctx_hop(enc_x, CORE), ctx_hop(enc_y, CORE)]
        last, main_far[1], main_far[2], enc_far[1], enc_far[2] = tie(
            ring[2], main_far[1], main_far[2], enc_far[1], enc_far[2]
        )
        first_stack = stack_rows([*ring[:2], last])
        main_far.append(ctx_hop(main_corner, CORE))
        enc_far.append(ctx_hop(enc_corner, CORE))
        main_parts = [item for pair in zip([main, main_x, main_y, main_corner], main_far) for item in pair]
        enc_parts = [item for pair in zip([enc, enc_x, enc_y, enc_corner], enc_far) for item in pair]

        ring = [z_hop(after(second_piece, first_stack), 1)]
        near = list(first_spread(first_stack))
        held, near[1], near[2], main_parts[7], enc_parts[7] = tie(ring[0], near[1], near[2], main_parts[7], enc_parts[7])
        ring.append(z_hop(held, 1))
        near = corner_spread(near, 1, cuts[0])
        far = [ctx_hop(near[0], CORE), ctx_hop(near[1], CORE)]
        held, *near[2:], far[0], far[1] = tie(ring[1], *near[2:], far[0], far[1])
        ring.append(z_hop(held, 1))
        far += [ctx_hop(item, CORE) for item in near[2:]]
        (q, e, k, v), keyed_flat, first = project(
            x_all, main_parts, self_set, near + far, layouts[0], cuts[0],
            ((False, 0), (False, 1), (True, 2), (True, 3)), where, steps,
        )
        second_stack = stack_rows(tie(*ring, q)[: steps - 1])
        second_near = list(first_spread(second_stack))
        feed_ring = [z_hop(after(feed_piece, second_stack), 1)]
        k = after(k, second_stack)
        peers = [c_index ^ j for j in range(8)]
    else:
        norms = lax.all_gather(norms, "fsdp", axis=1, tiled=True)
        gather = lambda w: lax.all_gather(w, "fsdp", axis=0, tiled=True)
        first, second, third = [[gather(w) for w in group] for group in (self_set, cross_set, feed_set)]
        peers = [jnp.int32(j) for j in range(ctx_count)]
        main = lax.all_gather(x_rows[0], "ctx", axis=0)
        keyed_flat = jnp.concatenate([main, x_rows[1:]], axis=0).reshape(-1, width)
        enc_flat = lax.all_gather(encoder_out, "ctx", axis=0).reshape(-1, width)
        q, e = matmul(x_all, first[0]).astype(bf16), matmul(x_all, first[1]).astype(bf16)
        k, v = matmul(keyed_flat, first[2]).astype(bf16), matmul(keyed_flat, first[3]).astype(bf16)
        ck, cv = matmul(enc_flat, second[2]).astype(bf16), matmul(enc_flat, second[3]).astype(bf16)
    query_full, relative_full, key_full, value_full = first

    place = jnp.stack(peers).astype(jnp.int32)
    local = jnp.arange(half_rows, dtype=jnp.int32)

    def both_halves(start):
        return jnp.concatenate([start + local, seq_len - 1 - start - local])

    positions = both_halves(c_index * half_rows)
    key_positions = jnp.concatenate([both_halves(place[j] * half_rows) for j in range(ctx_count)])
    enc_positions = (place[:, None] * enc_rows + jnp.arange(enc_rows, dtype=jnp.int32)[None, :]).reshape(1, -1)
    levels = jnp.arange(BUCKETS + 1, dtype=jnp.int32)
    bounds = jnp.sum((rel_bucket[None, :] < levels[:, None]).astype(jnp.int32), axis=1)

    q, e = q.reshape(slab), e.reshape(lanes, slots, rows, -1)
    k, v = k.reshape(-1, slots, rows, width), v.reshape(-1, slots, rows, width)
    self_inputs = (slot_len, bounds, positions[:, None], key_positions[None])
    made = self_forward(*self_inputs, q, e, k, v, 0, 2)
    q_late = q
    if paired:
        held, q_late, _ = tie(feed_ring[0], q, made[0])
        feed_ring.append(z_hop(held, 1))
    o, probs, own = self_forward(*self_inputs, q_late, e, k, v, 1, 2, made)
    o_flat = o.reshape(all_rows, width)
    if paired:
        second_near[1], second_near[2], held, _ = tie(second_near[1], second_near[2], feed_ring[1], o)
        feed_ring.append(z_hop(held, 1))
        second_near = corner_spread(second_near, 1, cuts[1])
        second_far = [ctx_hop(second_near[0], CORE)]
        feed_ring[2], *second_near[1:], second_far[0] = tie(feed_ring[2], *second_near[1:], second_far[0])
        second_far += [ctx_hop(item, CORE) for item in second_near[1:]]
        third_stack = stack_rows(tie(*feed_ring, *second_far[2:])[: steps - 1])
        third_near = list(first_spread(third_stack))
        (ck, cv), enc_flat, second = project(
            None, enc_parts, second_set, second_near + second_far, second_layout, cuts[1],
            ((True, 2), (True, 3)), after(where, third_stack), steps,
        )
        output_full, cquery_full, ckey_full, cvalue_full, coutput_full, vectors = second
        normed_one, unit_one, scale_one, normed_one_low, cq, norms = query_rows(
            x_all, o_flat, output_full, cquery_full, vectors, norm_count
        )
    else:
        output_full, cquery_full, ckey_full, cvalue_full, coutput_full = second
        norms = norms.astype(f32)
        resid_one = x_all.astype(f32) + matmul(o_flat, output_full)
        normed_one, unit_one, scale_one = norm_forward(resid_one, norms[0:1], norms[1:2])
        normed_one_low = normed_one.astype(bf16)
        cq = matmul(normed_one_low, cquery_full).astype(bf16)

    enc_shape = (ctx_count, slots, enc_rows, width)
    cq, ck, cv = cq.reshape(slab), ck.reshape(enc_shape), cv.reshape(enc_shape)
    oc, cprobs = cross_forward(enc_len, enc_positions, cq, ck, cv)
    oc_flat = oc.reshape(all_rows, width)

    core = (c_index & 1).astype(jnp.int32).reshape(1)

    def reduction(pairs, index, *more):
        return Reduction(pairs, layouts[index] + more, cuts[index], z_index, c_index)

    far = lambda *items: [ctx_hop(item, CORE) for item in items]

    row_valid = (positions[None, None, :] < slot_len[None, :, None]).astype(f32)
    row_valid = jnp.broadcast_to(row_valid, (lanes, slots, rows)).reshape(all_rows, 1)
    if paired:
        third_near[1], third_near[2], _ = tie(third_near[1], third_near[2], oc_flat)
        third_near = corner_spread(third_near, 1, cuts[2])
        third_far = [ctx_hop(item, CORE) for item in third_near[:3]]
        third_near[3], third_near[4], *third_far = tie(third_near[3], third_near[4], *third_far)
        third_far += [ctx_hop(item, CORE) for item in third_near[3:]]
        third = third_near + third_far
        feed_inputs = (feed_set, third, layouts[2], cuts[2], jnp.concatenate([core, where]))
    else:
        feed_inputs = (third, (), tuple(w.shape for w in third), 0, core)
    layer_out, normed_two_low, act_low, back_pre, back_feed, back_two, back_cross, back_oc, feed_norms, *sent = (
        feed_forward_backward(
            normed_one, oc_flat, coutput_full, norms, out_grad.reshape(all_rows, width), row_valid, *feed_inputs, steps, paired
        )
    )
    if paired:
        sent_up, sent_down, sent_coutput = sent
        third_sum = reduction([(normed_two_low, [back_pre]), (act_low, [back_feed])], 2)
        far_feed = far(sent_up, sent_down, sent_coutput)
    back_cq, back_ck, back_cv = cross_backward(cprobs, back_oc.reshape(slab), cq, ck, cv)
    back_cq = back_cq.reshape(all_rows, width)
    back_ck = back_ck.reshape(-1, width)
    back_cv = back_cv.reshape(-1, width)
    sending = ()
    if paired:
        *far_feed, back_cq = tie(*far_feed, back_cq)
        third_sum.fold(far_feed[:2], None, None, back_cq)
        third_first = third_sum.first_hops(1)
        back_cq = after(back_cq, third_sum.folded[0])
        sending = (normed_one_low, o_flat, feed_norms, enc_flat, back_ck, back_cv, ckey_full, cvalue_full)
    back_one, back_self, back_o, norm_grads, *sent = middle_backward(
        back_cq, cquery_full, back_two, unit_one, scale_one, norms, output_full, core, steps, sending
    )
    if paired:
        second_sum = reduction(
            [(o_flat, [back_self]), (normed_one_low, [back_cq]), (enc_flat, [back_ck, back_cv]), (oc_flat, [back_cross])],
            1,
            (128, 1024),
        )
        got_x, got_y, back_o, *sent = tie(*third_first, back_o, *sent)
        sent_cquery, sent_output, norm_keep, norm_send, sent_ckey, sent_cvalue, enc_keep, enc_send = sent
        third_sum.second_sums(got_x, got_y)
        third_late = third_sum.second_hops()
        far_some = far(sent_cquery, sent_output, sent_ckey)
        back_o = after(back_o, *third_sum.sums)
    else:
        enc_part = pair_rows(back_ck, back_cv, ckey_full, cvalue_full, ctx_count, slots * enc_rows)
    self_inputs = (bounds, positions[:, None], key_positions[None], probs, own)
    if paired:
        *far_some, sent_cvalue, norm_send, enc_send = tie(*far_some, sent_cvalue, norm_send, enc_send)
        norm_shape = (4 * steps, 16, width)
        far_rest = far(sent_cvalue, norm_send.reshape(norm_shape), enc_send)
        second_sum.fold(
            [far_some[1], far_some[0], far_some[2], far_rest[0], far_feed[2]],
            [enc_keep, far_rest[2]],
            [norm_keep.reshape(norm_shape), far_rest[1]],
        )
        late_x, late_y, third_sum.folded[0], third_sum.folded[4], _ = tie(
            *third_late, third_sum.folded[0], third_sum.folded[4], second_sum.folded[0]
        )
        third_got = third_sum.first_hops(0)
        back_o = after(back_o, third_sum.folded[0])
    back_q, back_k, back_v, back_e = self_backward(*self_inputs, back_o.reshape(slab), q, k, v, 0, 1)
    back_q = back_q.reshape(all_rows, width)
    back_e = back_e.reshape(all_rows, -1)
    back_k = back_k.reshape(-1, width)
    back_v = back_v.reshape(-1, width)

    if paired:
        first_sum = reduction([(x_all, [back_q, back_e]), (keyed_flat, [back_k, back_v])], 0)
        got_x, got_y, second_sum.folded[1], second_sum.folded[5], back_q, back_k = tie(
            *third_got, second_sum.folded[1], second_sum.folded[5], back_q, back_k
        )
        third_sum.z_sums(got_x, got_y, late_x, late_y)
        hop = third_sum.z_step(1)
        second_first = second_sum.first_hops(1)
        back_q = after(back_q, third_sum.total, second_sum.folded[1])
        *sent_first, main_keep, main_send, back_x = last_backward(
            x_all, keyed_flat, back_one, back_q, back_e, back_k, back_v, query_full, relative_full, key_full, value_full,
            core, steps, ctx_count,
        )
        hop, got_x, got_y, main_send, *sent_first = tie(hop, *second_first, main_send, *sent_first)
        far_keys, far_values, far_query, far_main = far(*sent_first[:3], main_send)
        far_embed, hop, far_keys = tie(*far(sent_first[3]), hop, far_keys)
        hop = third_sum.z_step(2, hop)
        second_sum.second_sums(got_x, got_y)
        second_late = second_sum.second_hops()
        first_sum.fold(
            [far_query, far_embed, far_keys, far_values], [main_keep, far_main], None, third_sum.total, *second_sum.sums
        )
        hop, late_x, late_y, first_sum.folded[1], first_sum.folded[5], second_sum.folded[0], second_sum.folded[4] = tie(
            hop, *second_late, first_sum.folded[1], first_sum.folded[5], second_sum.folded[0], second_sum.folded[4]
        )
        first_first = first_sum.first_hops(1)
        second_got = second_sum.first_hops(0)
        hop = third_sum.z_step(3, hop)
        hop, got_x, got_y = tie(hop, *first_first)
        third_sum.z_end(hop)
        first_sum.second_sums(got_x, got_y)
        first_late = first_sum.second_hops()
        got_x, got_y, third_sum.total, _ = tie(*second_got, third_sum.total, first_sum.sums[0])
        second_sum.z_sums(got_x, got_y, late_x, late_y)
        hop = second_sum.z_step(1)
        first_sum.folded[0], first_sum.folded[4], _ = tie(first_sum.folded[0], first_sum.folded[4], second_sum.total)
        first_got = first_sum.first_hops(0)
        hop, *first_late = tie(hop, *first_late)
        hop = second_sum.z_step(2, hop)
        hop, *rest, third_sum.total = tie(hop, *first_got, *first_late, third_sum.total)
        first_sum.z_sums(*rest)
        first_hop = first_sum.z_step(1)
        hop = second_sum.z_step(3, hop)
        main_sum = jnp.concatenate(first_sum.extra, axis=0)
        hidden_grad = jnp.concatenate([back_x[: main_sum.shape[0]] + main_sum, back_x[main_sum.shape[0] :]], axis=0)
        encoder_grad = jnp.concatenate(second_sum.extra, axis=0)
        hop, first_hop, third_x, third_y = tie(hop, first_hop, *third_sum.spread())
        second_sum.z_end(hop)
        first_hop = first_sum.z_step(2, first_hop)
        corners = third_sum.corners(third_x, third_y)
        spread = second_sum.spread()
        first_hop, second_x, second_y, *third_sum.near[1:], hidden_grad = tie(
            first_hop, *spread, third_x, third_y, *corners, hidden_grad
        )
        first_hop = first_sum.z_step(3, first_hop)
        corners = second_sum.corners(second_x, second_y)
        third_far = far(*third_sum.near[1:3])
        first_hop, *second_sum.near[1:], third_far[0], third_far[1], encoder_grad = tie(
            first_hop, second_x, second_y, *corners, *third_far, encoder_grad
        )
        first_sum.z_end(first_hop)
        spread = first_sum.spread()
        more = far(third_sum.near[0], *third_sum.near[3:])
        *more, held = tie(*more, second_sum.near[0])
        third_far = [more[0], *third_far, *more[1:]]
        second_sum.near[0] = held
        second_far = far(*second_sum.near[:3])
        third_grads = third_sum.grads(third_sum.near + third_far)
        first_x, first_y, *second_far = tie(*spread, *second_far)
        corners = first_sum.corners(first_x, first_y)
        second_far += far(*second_sum.near[3:])
        *first_sum.near[1:], second_far[3], second_far[4], _ = tie(first_x, first_y, *corners, *second_far[3:], third_grads[0])
        first_far = far(*first_sum.near)
        outs = second_sum.grads(second_sum.near + second_far, norm_count)
        second_grads, norm_grads = outs[:-norm_count], [item.reshape(norm_shard) for item in outs[-norm_count:]]
        first_grads = first_sum.grads(first_sum.near + first_far)
    else:
        *main_part, other_part = pair_rows(back_k, back_v, key_full, value_full, ctx_count, slots * rows)
        back_x = back_one + matmul_back(back_q, query_full) + matmul_back(back_e, relative_full)
        back_x = jnp.concatenate([back_x[: slots * rows], back_x[slots * rows :] + other_part], axis=0)
        norm_grads = lax.psum(jnp.concatenate([norm_grads, feed_norms], axis=0), ("fsdp", "ctx"))
        norm_grads = lax.dynamic_slice_in_dim(norm_grads, z_index * norm_shard, norm_shard, 1)

        def reduce(left, right):
            shard = lax.psum_scatter(outer_rows(left, right).astype(bf16), "fsdp", scatter_dimension=0, tiled=True)
            return lax.psum(shard, "ctx").astype(f32)

        def scatter(parts):
            whole = jnp.stack(parts, axis=1).reshape(ctx_count, -1, width)
            return lax.psum_scatter(whole, "ctx", scatter_dimension=0, tiled=True).astype(f32).reshape(-1, width)

        first_grads = [
            reduce(x_all, back_q), reduce(x_all, back_e), reduce(keyed_flat, back_k), reduce(keyed_flat, back_v),
        ]
        second_grads = [
            reduce(o_flat, back_self), reduce(normed_one_low, back_cq), reduce(enc_flat, back_ck),
            reduce(enc_flat, back_cv), reduce(oc_flat, back_cross),
        ]
        third_grads = [reduce(normed_two_low, back_pre), reduce(act_low, back_feed)]
        encoder_grad = scatter(enc_part)
        main_sum = scatter(main_part)
        hidden_grad = jnp.concatenate([back_x[: main_sum.shape[0]] + main_sum, back_x[main_sum.shape[0] :]], axis=0)
    out_shape = hidden.shape
    return (
        layer_out.reshape(out_shape), hidden_grad.reshape(out_shape), encoder_grad.reshape(encoder_out.shape),
        first_grads[0], first_grads[2], first_grads[3], first_grads[1], second_grads[0], norm_grads[0], norm_grads[1],
        second_grads[1], second_grads[2], second_grads[3], second_grads[4], norm_grads[2], norm_grads[3],
        third_grads[0], third_grads[1], norm_grads[4], norm_grads[5],
    )


def solution(mesh):
    rows = P("fsdp", None)
    vector = P("fsdp")
    slab = P(None, "fsdp", None, "ctx", None)
    encoder = P("fsdp", "ctx", None)
    weights = (rows,) * 5 + (vector,) * 2 + (rows,) * 4 + (vector,) * 2 + (rows,) * 2 + (vector,) * 2
    return jax.shard_map(
        on_device,
        mesh=mesh,
        in_specs=(slab, encoder, slab, vector, vector, P()) + weights,
        out_specs=(slab, slab, encoder) + weights,
        check_vma=False,
    )
```
